32 devices in a mesh: inst: 4 (over x, core), space: 8 (over z, y).
Axes of the slice: x: 2, y: 2, z: 4, core: 2. Of those that a mesh axis runs over, the one named last changes fastest.
Arguments:
- adjoint_old: float32 [8, 6, 512, 512], P('inst', None, 'space'), may hold values from -6 to 6
- source_term: float32 [8, 6, 512, 512], P('inst', None, 'space'), may hold values from -6 to 6
- face_stream: float32 [8, 512, 512], P('inst', 'space'), may hold values from 0.2 to 1
- face_pitch: float32 [8, 512, 512], P('inst', 'space'), may hold values from 0.2 to 1
- diag_scale: float32 [8, 512, 512], P('inst', 'space'), may hold values from 0.1 to 0.4
- volume: float32 [512, 512], P('space'), may hold values from 0.5 to 2
- face_blocks: float32 [4, 6, 6], replicated, may hold values from -2.5 to 2.5
- diag_inverse: float32 [8, 6, 6], P('inst')
- periodic_block: float32 [6, 6], replicated, may hold values from -2.5 to 2.5
- frequency: float32 [1], replicated, may hold values from 0.5 to 2
- phase_shift: int32 [1], replicated, may hold values from 1 to 7
- periodic_cells: int32 [8, 8, 128], P('space'), may hold values from 0 to 32767
- periodic_targets: int32 [8, 8, 128], P(None, 'space'), may hold values from 0 to 32767
- periodic_weights: float32 [8, 8, 128], P('space'), may hold values from 0.5 to 1.5
- periodic_counts: int32 [8, 8], P('space'), may hold values from 0 to 128, as said below
Outputs:
- adjoint_new: float32 [8, 6, 512, 512], P('inst', None, 'space')
- residual: float32 [8, 6, 512, 512], P('inst', None, 'space')
The draws below stay inside these ranges and needn't reach their ends.
Inputs may be any that keep to these rules, and one draw needn't show every extreme that they name: `periodic_counts`: each partition's row has one peer with 128 live faces, and one partition receives 128 live faces from every partition. `periodic_cells`: local cell indices in the sending partition. `periodic_targets`: local cell indices in the receiving partition.
All inputs are finite; a program needn't handle non-finite values.
Results may differ from the reference program's by a relative error of at most 0.0001.
Values sent between devices are 32-bit elements; how exact they have to be, the bound alone decides.
A program may use at most 128 MiB of HBM per device.

```python
import math
import jax
import jax.numpy as jnp
from jax import lax

VARS = 6
CI = 64
NJ = 512
PSLOT = 128
SWEEPS = 2
INSTANCES = 8
NI = 512
N_SPACE = 8


def draw_diag_inverse(key, part):
    noise = jax.random.normal(key, (INSTANCES, VARS, VARS), jnp.float32) * 0.5
    return jnp.eye(VARS, dtype=jnp.float32)[None] + noise / math.sqrt(VARS)


def draw_periodic_counts(key, part):
    first = jax.random.fold_in(key, 11)
    second = jax.random.fold_in(key, 12)
    third = jax.random.fold_in(key, 13)
    counts = jax.random.randint(first, (N_SPACE, N_SPACE), 0, PSLOT + 1)
    peers = jax.random.permutation(second, N_SPACE)
    counts = counts.at[jnp.arange(N_SPACE), peers].set(PSLOT)
    column = jax.random.randint(third, (), 0, N_SPACE)
    counts = counts.at[:, column].set(PSLOT)
    return counts.astype(jnp.int32)


def with_ends(drawn, stream_key, low, largest):
    longest = drawn.shape.index(max(drawn.shape))
    spots = []
    for shift in (0, 1):
        where = [jax.random.randint(jax.random.fold_in(stream_key, axis), (), 0, length) for axis, length in enumerate(drawn.shape)]
        where[longest] = (where[longest] + shift) % drawn.shape[longest]
        spots.append(tuple(where))
    return drawn.at[spots[0]].set(low).at[spots[1]].set(largest)


def level_of(key, shape, cuts, least, top_value):
    loudness, own = 1.0, jax.random.fold_in(key, 6)
    for position, blocks in cuts:
        draws = jnp.exp(jax.random.uniform(jax.random.fold_in(own, position), (blocks,), jnp.float32, least / len(cuts), top_value / len(cuts)))
        loudness = loudness * jnp.repeat(draws, shape[position] // blocks).reshape([-1 if axis == position else 1 for axis in range(len(shape))])
    return loudness


def gaussian(rng, extent, width, bound, cuts=(), kind=jnp.bfloat16):
    loudness = level_of(rng, extent, cuts, -0.22, 0.18) if cuts else 1.0
    array = jax.random.normal(rng, extent, jnp.float32) * width * loudness
    return jnp.minimum(jnp.maximum(array, -bound), bound).astype(kind)


def setup_inputs(seed: int = 0) -> dict:
    streams_of = jax.random.split(jax.random.key(seed), 16)
    adjoint_old = gaussian(streams_of[0], (INSTANCES, VARS, NI, NJ), 1.0, 6.0, ((0, 4), (2, 8)), jnp.float32)
    source_term = gaussian(streams_of[1], (INSTANCES, VARS, NI, NJ), 1.0, 6.0, ((0, 4), (2, 8)), jnp.float32)
    face_stream = jnp.clip(0.2 + 0.8 * jax.random.uniform(streams_of[2], (INSTANCES, NI, NJ), jnp.float32) ** level_of(streams_of[2], (INSTANCES, NI, NJ), ((0, 4), (1, 8)), -0.2, 0.2), 0.2, 1.0)
    face_pitch = jnp.clip(0.2 + 0.8 * jax.random.uniform(streams_of[3], (INSTANCES, NI, NJ), jnp.float32) ** level_of(streams_of[3], (INSTANCES, NI, NJ), ((0, 4), (1, 8)), -0.2, 0.2), 0.2, 1.0)
    diag_scale = jnp.clip(jnp.exp(math.log(0.4) - 1.3862944 * jax.random.uniform(streams_of[4], (INSTANCES, NI, NJ), jnp.float32) ** level_of(streams_of[4], (INSTANCES, NI, NJ), ((0, 4), (1, 8)), -0.2, 0.2)), 0.1, 0.4)
    volume = jnp.clip(jnp.exp(math.log(2.0) - 1.3862944 * jax.random.uniform(streams_of[5], (NI, NJ), jnp.float32) ** level_of(streams_of[5], (NI, NJ), ((0, 8),), -0.2, 0.2)), 0.5, 2.0)
    face_blocks = gaussian(streams_of[6], (4, VARS, VARS), VARS ** -0.5, 2.5, (), jnp.float32)
    diag_inverse = draw_diag_inverse(jax.random.fold_in(streams_of[15], 71), 0)
    periodic_block = gaussian(streams_of[8], (VARS, VARS), VARS ** -0.5, 2.5, (), jnp.float32)
    frequency = jnp.clip(jnp.exp(jax.random.uniform(streams_of[9], (1,), jnp.float32, math.log(0.5), math.log(2.0))), 0.5, 2.0)
    phase_shift = jax.random.randint(streams_of[10], (1,), 1, INSTANCES).astype(jnp.int32)
    periodic_cells = with_ends(jax.random.randint(streams_of[11], (N_SPACE, N_SPACE, PSLOT), 0, CI * NJ), jax.random.fold_in(streams_of[11], 1), 0, (CI * NJ) - 1).astype(jnp.int32)
    periodic_targets = with_ends(jax.random.randint(streams_of[12], (N_SPACE, N_SPACE, PSLOT), 0, CI * NJ), jax.random.fold_in(streams_of[12], 1), 0, (CI * NJ) - 1).astype(jnp.int32)
    periodic_weights = jnp.clip(0.5 + 1.0 * jax.random.uniform(streams_of[13], (N_SPACE, N_SPACE, PSLOT), jnp.float32) ** level_of(streams_of[13], (N_SPACE, N_SPACE, PSLOT), ((0, 8),), -0.2, 0.2), 0.5, 1.5)
    periodic_counts = draw_periodic_counts(jax.random.fold_in(streams_of[15], 71), 0)
    return dict(adjoint_old=adjoint_old, source_term=source_term, face_stream=face_stream, face_pitch=face_pitch, diag_scale=diag_scale, volume=volume, face_blocks=face_blocks, diag_inverse=diag_inverse, periodic_block=periodic_block, frequency=frequency, phase_shift=phase_shift, periodic_cells=periodic_cells, periodic_targets=periodic_targets, periodic_weights=periodic_weights, periodic_counts=periodic_counts)


def spectral_matrix():
    order = jnp.arange(INSTANCES, dtype=jnp.int32)
    offset = order[:, None] - order[None, :]
    parity = jnp.where(offset % 2 == 0, 1.0, -1.0)
    nonzero = offset != 0
    angle = math.pi * offset / INSTANCES
    safe = jnp.where(nonzero, angle, 1.0)
    return jnp.where(nonzero, 0.5 * parity * jnp.cos(safe) / jnp.sin(safe), 0.0).astype(jnp.float32)


def transposed(block, field):
    return jnp.einsum("vu,kvij->kuij", block, field, precision=lax.Precision.HIGHEST)


def neighbours(adjoint, face_stream, face_pitch, face_blocks):
    zero_row = jnp.zeros_like(adjoint[:, :, :1])
    weighted = face_stream[:, None] * adjoint
    from_lower = jnp.concatenate([zero_row, weighted[:, :, :-1]], axis=2)
    from_upper = face_stream[:, None] * jnp.concatenate([adjoint[:, :, 1:], zero_row], axis=2)
    zero_col = jnp.zeros_like(adjoint[..., :1])
    side = face_pitch[:, None] * adjoint
    from_left = jnp.concatenate([zero_col, side[..., :-1]], axis=3)
    from_right = face_pitch[:, None] * jnp.concatenate([adjoint[..., 1:], zero_col], axis=3)
    return (transposed(face_blocks[0], from_lower) + transposed(face_blocks[1], from_upper)
            + transposed(face_blocks[2], from_left) + transposed(face_blocks[3], from_right))


def reference(adjoint_old, source_term, face_stream, face_pitch, diag_scale, volume, face_blocks, diag_inverse,
              periodic_block, frequency, phase_shift, periodic_cells, periodic_targets, periodic_weights,
              periodic_counts):
    cells = CI * NJ
    flat = adjoint_old.reshape(INSTANCES, VARS, N_SPACE, cells)
    index = periodic_cells.reshape(N_SPACE, N_SPACE * PSLOT)
    picked = jnp.take_along_axis(flat, index[None, None], axis=3)
    slots = jnp.arange(PSLOT, dtype=jnp.int32)
    live = slots[None, None, :] < periodic_counts[:, :, None]
    weights = jnp.where(live, periodic_weights, 0.0).reshape(N_SPACE, N_SPACE * PSLOT)
    picked = jnp.einsum("vu,gvpr->gupr", periodic_block, picked, precision=lax.Precision.HIGHEST) * weights
    picked = jnp.roll(picked, phase_shift[0], axis=0)
    owner = jnp.arange(N_SPACE, dtype=jnp.int32)[None, :, None] * cells
    target = (owner + periodic_targets).reshape(-1)
    periodic = jnp.zeros((INSTANCES, VARS, N_SPACE * cells), adjoint_old.dtype)
    periodic = periodic.at[:, :, target].add(picked.reshape(INSTANCES, VARS, -1))
    periodic = periodic.reshape(INSTANCES, VARS, NI, NJ)
    dmat = spectral_matrix()
    adjoint = adjoint_old
    residual = adjoint_old
    for sweep_index in range(SWEEPS):
        coupling = frequency[0] * volume * jnp.einsum("mg,mvij->gvij", dmat, adjoint,
                                                      precision=lax.Precision.HIGHEST)
        residual = source_term - neighbours(adjoint, face_stream, face_pitch, face_blocks) - coupling - periodic
        adjoint = diag_scale[:, None] * jnp.einsum("guv,gvij->guij", diag_inverse, residual,
                                                   precision=lax.Precision.HIGHEST)
    return adjoint, residual
```

```python
import functools
import math

import jax
import jax.numpy as jnp
from jax import lax
from jax.experimental import pallas as pl
from jax.experimental.pallas import tpu as pltpu
from jax.sharding import PartitionSpec as P

SWEEPS = 2
TILE = 8
LANES = 128
PARTS = 2
CHUNK = 16
EARLY = 2
AHEAD = 2
LAG = 3
GROUP = 4
MESH = pl.DeviceIdType.MESH


def spectral_entry(offset, count):
    offset = offset % count
    if offset == 0 or 2 * offset == count:
        return 0.0
    return 0.5 * (-1.0) ** offset / math.tan(math.pi * offset / count)


def split_parts(value):
    parts = []
    for _ in range(PARTS):
        part = value.astype(jnp.bfloat16)
        parts.append(part)
        value = value - part.astype(jnp.float32)
    return parts


def kernel(
    n_space,
    n_inst,
    a_hbm,
    s_hbm,
    fs_hbm,
    fp_hbm,
    ds_hbm,
    vol_hbm,
    blocks,
    dinv,
    pblock,
    freq,
    shift,
    cells,
    targets,
    weights,
    counts,
    out_r,
    A,
    SP,
    AT,
    ST,
    RT,
    FS,
    FP,
    DS,
    VOL,
    CL,
    CR,
    PW,
    PF,
    DV,
    DT,
    COL,
    PICK,
    ALLP,
    ROUTED,
    ARR,
    LHS,
    load_sem,
    own_s,
    own_r,
    a_s,
    a_r,
    c_s,
    c_r,
    s_s,
    s_r,
    r_s,
    r_r,
    d_s,
    d_r,
    cols_s,
    cols_r,
    hs,
    hr,
    ps,
    pr,
    q_s,
    q_r,
):
    per_dev, variables, rows, width = a_hbm.shape
    instances = n_inst * per_dev
    cols = width // n_inst
    slots = cells.shape[2]
    nb = rows // TILE
    na = rows // CHUNK
    inst = lax.axis_index("inst")
    me = lax.axis_index("space")
    odd = inst % 2
    sibling = inst + 1 - 2 * odd
    across = (inst + 2) % n_inst
    shift_bits = width.bit_length() - 1
    peers = (2, 1, 3)

    def remote(src, dst, send, recv, **device):
        return pltpu.make_async_remote_copy(
            src_ref=src, dst_ref=dst, send_sem=send, recv_sem=recv, device_id=device,
            device_id_type=MESH,
        )

    def columns(i):
        return pl.ds(pl.multiple_of(i * cols, cols), cols)

    def members(i):
        return pl.ds(i * per_dev, per_dev)

    def local(src, dst, n):
        return pltpu.make_async_copy(src, dst, load_sem.at[n])

    inner = pl.ds(TILE, rows)
    mine = columns(inst)
    own = members(inst)
    loads = [
        local(a_hbm, A, 0),
        local(s_hbm, SP, 1),
        local(a_hbm.at[:, :, :, mine], AT.at[0, own, :, inner, :], 2),
        local(fp_hbm.at[:, :, mine], FP.at[own], 3),
        local(fs_hbm.at[:, :, mine], FS.at[own, inner, :], 4),
        local(ds_hbm.at[:, :, mine], DS.at[own], 5),
        local(vol_hbm.at[:, mine], VOL, 6),
    ]
    for copy in loads:
        copy.start()

    barrier = pltpu.get_barrier_semaphore()
    for d in peers:
        pl.semaphore_signal(
            barrier, inc=1, device_id={"inst": (inst + d) % n_inst}, device_id_type=MESH
        )

    @pl.loop(1, n_space)
    def _(j):
        pl.semaphore_signal(
            barrier, inc=1, device_id={"space": (me + j) % n_space}, device_id_type=MESH
        )

    def to(d):
        return (inst + d) % n_inst

    def source(d):
        return (inst + n_inst - d) % n_inst

    def a_copy(d, c, sender, receiver):
        span = pl.multiple_of(c * CHUNK, CHUNK)
        return remote(
            a_hbm.at[:, :, pl.ds(span, CHUNK), columns(receiver)],
            AT.at[0, members(sender), :, pl.ds(span + TILE, CHUNK), :],
            a_s.at[d - 1, c], a_r.at[d - 1, c], inst=receiver,
        )

    def fp_copy(d, sender, receiver):
        return remote(
            fp_hbm.at[:, :, columns(receiver)], FP.at[members(sender)],
            c_s.at[d - 1, 0], c_r.at[d - 1, 0], inst=receiver,
        )

    def fs_copy(d, sender, receiver):
        return remote(
            fs_hbm.at[:, :, columns(receiver)], FS.at[members(sender), inner, :],
            c_s.at[d - 1, 1], c_r.at[d - 1, 1], inst=receiver,
        )

    def ds_copy(d, sender, receiver):
        return remote(
            ds_hbm.at[:, :, columns(receiver)], DS.at[members(sender)],
            c_s.at[d - 1, 2], c_r.at[d - 1, 2], inst=receiver,
        )

    def dv_copy(d, sender, receiver):
        return remote(
            DV.at[sender], DV.at[sender], d_s.at[d - 1], d_r.at[d - 1], inst=receiver
        )

    def order(n):
        return (n + nb - 1) % nb

    def s_copy(d, n, sender, receiver):
        row = pl.multiple_of(order(n) * TILE, TILE)
        return remote(
            SP.at[:, :, pl.ds(row, TILE), columns(receiver)],
            ST.at[members(sender), :, pl.ds(row, TILE), :],
            s_s.at[d - 1, n], s_r.at[d - 1, n], inst=receiver,
        )

    def r_copy(d, b, sender, receiver):
        row = pl.multiple_of(b * TILE, TILE)
        return remote(
            RT.at[members(receiver), :, pl.ds(row, TILE), :],
            out_r.at[:, :, pl.ds(row, TILE), columns(sender)],
            r_s.at[d - 1, b], r_r.at[d - 1, b], inst=receiver,
        )

    def s_own(n):
        row = pl.multiple_of(order(n) * TILE, TILE)
        return pltpu.make_async_copy(
            SP.at[:, :, pl.ds(row, TILE), mine], ST.at[own, :, pl.ds(row, TILE), :], own_s.at[n]
        )

    def r_own(b):
        row = pl.multiple_of(b * TILE, TILE)
        return pltpu.make_async_copy(
            RT.at[own, :, pl.ds(row, TILE), :], out_r.at[:, :, pl.ds(row, TILE), mine],
            own_r.at[b],
        )

    def start(copy, *args):
        for d in peers:
            copy(d, *args, inst, to(d)).start()

    def arrived(copy, *args):
        for d in peers:
            copy(d, *args, source(d), inst).wait_recv()

    def sent(copy, *args):
        for d in peers:
            copy(d, *args, inst, to(d)).wait_send()

    has_above = me < n_space - 1
    has_below = me > 0
    above = (me + 1) % n_space
    below = (me + n_space - 1) % n_space
    has_left = inst > 0
    has_right = inst < n_inst - 1
    left_dev = (inst + n_inst - 1) % n_inst
    right_dev = (inst + 1) % n_inst

    def halo_up(sweep):
        return remote(
            AT.at[sweep, :, :, pl.ds(rows, TILE), :],
            AT.at[sweep, :, :, pl.ds(0, TILE), :],
            hs.at[2 * sweep], hr.at[2 * sweep], space=above,
        )

    def halo_down(sweep):
        return remote(
            AT.at[sweep, :, :, pl.ds(TILE, TILE), :],
            AT.at[sweep, :, :, pl.ds(rows + TILE, TILE), :],
            hs.at[2 * sweep + 1], hr.at[2 * sweep + 1], space=below,
        )

    def halo_face():
        last = 2 * SWEEPS
        return remote(
            FS.at[:, pl.ds(rows, TILE), :], FS.at[:, pl.ds(0, TILE), :],
            hs.at[last], hr.at[last], space=above,
        )

    def col_right(sweep, span, n):
        return remote(
            PW.at[sweep, span], CL.at[sweep, span], cols_s.at[0, n], cols_r.at[0, n],
            inst=right_dev,
        )

    def col_left(sweep, span, n):
        return remote(
            PF.at[sweep, span], CR.at[sweep, span], cols_s.at[1, n], cols_r.at[1, n],
            inst=left_dev,
        )

    def zeros(*shape):
        return jnp.zeros(shape, jnp.float32)

    @pl.when(me == 0)
    def _():
        FS[:, 0:TILE, :] = zeros(instances, TILE, cols)
        for sweep in range(SWEEPS):
            AT[sweep, :, :, 0:TILE, :] = zeros(instances, variables, TILE, cols)

    @pl.when(me == n_space - 1)
    def _():
        for sweep in range(SWEEPS):
            AT[sweep, :, :, rows + TILE : rows + 2 * TILE, :] = zeros(
                instances, variables, TILE, cols
            )

    @pl.when(inst == 0)
    def _():
        CL[...] = zeros(SWEEPS, rows, cols)

    @pl.when(inst == n_inst - 1)
    def _():
        CR[...] = zeros(SWEEPS, rows, cols)

    sub8 = lax.broadcasted_iota(jnp.int32, (TILE, cols), 0)
    lane8 = lax.broadcasted_iota(jnp.int32, (TILE, cols), 1)

    packed = zeros(TILE, cols)
    for k in range(per_dev):
        for u in range(variables):
            for v in range(variables):
                n = (k * variables + u) * variables + v
                packed = jnp.where(lane8 == n, dinv[u, k, v], packed)
    DV[inst] = packed

    pl.semaphore_wait(barrier, n_space + n_inst - 2)

    for c in range(min(EARLY, na)):
        start(a_copy, c)
    start(dv_copy)

    sub_w = lax.broadcasted_iota(jnp.int32, (width, slots), 0)
    sub_r = lax.broadcasted_iota(jnp.int32, (rows, slots), 0)

    def column_table(index, chunk):
        for q in range(TILE):
            line = index(chunk * TILE + q)
            column = jnp.bitwise_and(line, width - 1)
            hot = jnp.where(sub_w == column, 1.0, 0.0).astype(jnp.bfloat16)
            COL[:, q * slots : (q + 1) * slots] = hot

    def cell_line(q):
        return cells[0, pl.ds(q, 1), :]

    def target_line(p):
        return targets[p, 0:1, :]

    chunks = n_space // TILE

    loads[0].wait()

    @pl.loop(0, chunks)
    def _(chunk):
        column_table(cell_line, chunk)

        @pl.loop(0, per_dev)
        def _(k):
            field = A[k].reshape(variables * rows, width)
            stacked = jnp.concatenate(split_parts(field), axis=0)
            terms = jnp.dot(stacked, COL[...], preferred_element_type=jnp.float32)
            height = variables * rows
            found = terms[:height]
            for part in range(1, PARTS):
                found = found + terms[part * height : (part + 1) * height]
            for q in range(TILE):
                hit = sub_r == lax.shift_right_logical(cell_line(chunk * TILE + q), shift_bits)
                for v in range(variables):
                    piece = found[v * rows : (v + 1) * rows, q * slots : (q + 1) * slots]
                    PICK[k, v, chunk, q : q + 1, :] = jnp.sum(
                        jnp.where(hit, piece, 0.0), axis=0, keepdims=True
                    )

        lane = lax.broadcasted_iota(jnp.int32, (TILE, slots), 1)
        sub = lax.broadcasted_iota(jnp.int32, (TILE, slots), 0)
        limit = jnp.zeros((TILE, slots), jnp.int32)
        for q in range(TILE):
            limit = jnp.where(sub == q, counts[0, chunk * TILE + q], limit)
        first = pl.multiple_of(chunk * TILE, TILE)
        weight = jnp.where(lane < limit, weights[0, pl.ds(first, TILE), :], 0.0)

        for k in range(per_dev):
            picked = [PICK[k, v, chunk] for v in range(variables)]
            for u in range(variables):
                mixed = pblock[0, u] * picked[0]
                for v in range(1, variables):
                    mixed = mixed + pblock[v, u] * picked[v]
                ALLP[0, k, u, chunk] = mixed * weight

    p_x = remote(ALLP.at[0], ALLP.at[2], ps.at[0], pr.at[0], inst=across)
    p_sib = remote(ALLP.at[0], ALLP.at[3 - 2 * odd], ps.at[1], pr.at[1 + odd], inst=sibling)
    p_rel = remote(ALLP.at[2], ALLP.at[1 + 2 * odd], ps.at[2], pr.at[2 - odd], inst=sibling)
    p_sib_in = remote(ALLP.at[0], ALLP.at[1 + 2 * odd], ps.at[1], pr.at[2 - odd], inst=sibling)
    p_rel_in = remote(ALLP.at[2], ALLP.at[3 - 2 * odd], ps.at[2], pr.at[1 + odd], inst=sibling)
    p_x.start()
    p_sib.start()
    start(fp_copy)
    for c in range(min(EARLY, na), na):
        start(a_copy, c)
    start(fs_copy)
    start(ds_copy)
    p_x.wait_recv()
    p_rel.start()
    p_sib_in.wait_recv()
    p_rel_in.wait_recv()
    for k in range(per_dev):
        wanted = lax.rem(k - shift[0] + 2 * instances, instances)
        group = lax.div(wanted, per_dev)
        member = lax.rem(wanted, per_dev)

        @pl.loop(0, chunks)
        def _(chunk):
            for u in range(variables):
                value = ALLP[group, member, u, chunk]
                for q in range(TILE):
                    ROUTED[chunk * TILE + q, k, u : u + 1, :] = value[q : q + 1, :]

    def a2a(j):
        return remote(
            ROUTED.at[(me + j) % n_space], ARR.at[me], q_s.at[j], q_r.at[j],
            space=(me + j) % n_space,
        )

    @pl.loop(1, n_space)
    def _(j):
        a2a(j).start()

    ARR[me] = ROUTED[me]
    loads[1].wait()
    column_table(target_line, 0)

    @pl.loop(1, n_space)
    def _(j):
        remote(
            ROUTED.at[0], ARR.at[(me + n_space - j) % n_space], q_s.at[j], q_r.at[j],
            space=(me + j) % n_space,
        ).wait_recv()

    @pl.loop(0, chunks)
    def _(chunk):
        if chunks > 1:
            column_table(target_line, chunk)

        for k in range(per_dev):
            for p in range(TILE):
                hit = sub_r == lax.shift_right_logical(target_line(chunk * TILE + p), shift_bits)
                parts = split_parts(ARR[chunk * TILE + p, k])
                for n, part in enumerate(parts):
                    for u in range(variables):
                        begin = (n * variables + u) * rows
                        LHS[begin : begin + rows, p * slots : (p + 1) * slots] = jnp.where(
                            hit, part[u : u + 1, :].astype(jnp.float32), 0.0
                        ).astype(jnp.bfloat16)
            terms = lax.dot_general(
                LHS[...], COL[...], (((1,), (1,)), ((), ())), preferred_element_type=jnp.float32
            )
            height = variables * rows
            summed = terms[:height]
            for part in range(1, PARTS):
                summed = summed + terms[part * height : (part + 1) * height]
            SP[k] = SP[k] - summed.reshape(variables, rows, width)

    for copy in loads[2:]:
        copy.wait()
    arrived(fp_copy)

    @pl.loop(0, na)
    def _(c):
        arrived(a_copy, c)

    @pl.when(has_above)
    def _():
        halo_up(0).start()

    @pl.when(has_below)
    def _():
        halo_down(0).start()

    def pack(sweep, row):
        here = pl.ds(row, TILE)
        mid = pl.ds(row + TILE, TILE)
        last = zeros(TILE, cols)
        first = zeros(TILE, cols)
        for g in range(instances):
            fp = FP[g, here, :]
            for v in range(variables):
                n = g * variables + v
                a = AT[sweep, g, v, mid, :]
                first = jnp.where(lane8 == n, pltpu.roll(a, n, 1) if n else a, first)
                last = jnp.where(lane8 == n, pltpu.roll(fp * a, n + 1, 1), last)
        PW[sweep, here, :] = last
        PF[sweep, here, :] = first

    @pl.loop(0, nb)
    def _(b):
        pack(0, pl.multiple_of(b * TILE, TILE))

    whole = pl.ds(0, rows)

    @pl.when(has_right)
    def _():
        col_right(0, whole, nb).start()

    @pl.when(has_left)
    def _():
        col_left(0, whole, nb).start()

    for n in range(AHEAD):
        start(s_copy, n)

    @pl.loop(0, nb)
    def _(n):
        s_own(n).start()

    arrived(dv_copy)
    for g in range(instances):
        vector = DV[g // per_dev]
        for n in range(variables * variables):
            lane = (g % per_dev) * variables * variables + n
            DT[g * variables * variables + n] = jnp.broadcast_to(
                vector[:, lane : lane + 1], (TILE, cols)
            )

    arrived(fs_copy)

    @pl.when(has_above)
    def _():
        halo_face().start()

    arrived(ds_copy)

    @pl.when(has_below)
    def _():
        halo_up(0).wait_recv()
        halo_face().wait_recv()

    @pl.when(has_above)
    def _():
        halo_down(0).wait_recv()

    @pl.when(has_left)
    def _():
        col_right(0, whole, nb).wait_recv()

    @pl.when(has_right)
    def _():
        col_left(0, whole, nb).wait_recv()

    f1, f2, f3 = (spectral_entry(d, instances) for d in (1, 2, 3))

    def update(sweep, row):
        here = pl.ds(row, TILE)
        mid = pl.ds(row + TILE, TILE)
        low = pl.ds(row, TILE)
        high = pl.ds(row + 2 * TILE, TILE)
        scaled = freq[0] * VOL[here, :]
        v1 = (0.5 * (f1 - f3)) * scaled
        v2 = f2 * scaled
        v3 = (0.5 * (f1 + f3)) * scaled
        for u in range(variables):
            a = [AT[sweep, g, u, mid, :] for g in range(instances)]
            b = [a[g] - a[g + 4] for g in range(4)]
            c = [a[g] + a[g + 4] for g in range(4)]
            even = v1 * (c[1] - c[3])
            odds = v1 * (c[2] - c[0])
            q = [even, odds, -even, -odds]
            p = [
                v2 * b[2] + v3 * (b[1] + b[3]),
                v2 * b[3] + v3 * (b[2] - b[0]),
                v3 * (b[3] - b[1]) - v2 * b[0],
                -(v2 * b[1] + v3 * (b[0] + b[2])),
            ]
            for g in range(4):
                RT[g, u, here, :] = ST[g, u, here, :] - (q[g] + p[g])
                RT[g + 4, u, here, :] = ST[g + 4, u, here, :] - (q[g] - p[g])
        top = sub8 == TILE - 1
        bottom = sub8 == 0
        for base in range(0, instances, GROUP):
            span = range(base, base + GROUP)
            acc = {(g, u): RT[g, u, here, :] for g in span for u in range(variables)}
            fm = {g: FS[g, mid, :] for g in span}
            fl = {g: jnp.where(top, FS[g, low, :], fm[g]) for g in span}
            fp = {g: FP[g, here, :] for g in span}
            cl = CL[sweep, here, :]
            cr = CR[sweep, here, :]
            for v in range(variables):
                terms = {}
                for g in span:
                    n = g * variables + v
                    a = AT[sweep, g, v, mid, :]
                    x = pltpu.roll(fl[g] * jnp.where(top, AT[sweep, g, v, low, :], a), 1, 0)
                    y = fm[g] * pltpu.roll(
                        jnp.where(bottom, AT[sweep, g, v, high, :], a), TILE - 1, 0
                    )
                    edge = pltpu.roll(cl, cols - n, 1) if n else cl
                    left = jnp.where(lane8 == 0, edge, pltpu.roll(fp[g] * a, 1, 1))
                    edge = pltpu.roll(cr, cols - 1 - n, 1)
                    right = fp[g] * jnp.where(
                        lane8 == cols - 1, edge, pltpu.roll(a, cols - 1, 1)
                    )
                    terms[g] = (x, y, left, right)
                for u in range(variables):
                    k0, k1, k2, k3 = (blocks[v, n, u] for n in range(4))
                    for g in span:
                        x, y, left, right = terms[g]
                        acc[g, u] = acc[g, u] - (
                            (k0 * x + k1 * y) + (k2 * left + k3 * right)
                        )
            if sweep == SWEEPS - 1:
                for g in span:
                    for u in range(variables):
                        RT[g, u, here, :] = acc[g, u]
            else:
                for g in span:
                    scale = DS[g, here, :]
                    for u in range(variables):
                        n = (g * variables + u) * variables
                        new = DT[n] * acc[g, 0]
                        for v in range(1, variables):
                            new = new + DT[n + v] * acc[g, v]
                        AT[sweep + 1, g, u, mid, :] = scale * new

    @pl.loop(0, nb + LAG)
    def _(n):
        @pl.when(n < nb)
        def _():
            row = pl.multiple_of(order(n) * TILE, TILE)
            s_own(n).wait()
            arrived(s_copy, n)

            @pl.when(n + AHEAD < nb)
            def _():
                start(s_copy, n + AHEAD)

            update(0, row)
            pack(1, row)
            span = pl.ds(row, TILE)

            @pl.when(has_right)
            def _():
                col_right(1, span, order(n)).start()

            @pl.when(has_left)
            def _():
                col_left(1, span, order(n)).start()

        @pl.when(n == 1)
        def _():
            @pl.when(has_above)
            def _():
                halo_up(1).start()

            @pl.when(has_below)
            def _():
                halo_down(1).start()

        @pl.when(n == LAG)
        def _():
            @pl.when(has_below)
            def _():
                halo_up(1).wait_recv()

            @pl.when(has_above)
            def _():
                halo_down(1).wait_recv()

        @pl.when(n >= LAG)
        def _():
            b = n - LAG
            row = pl.multiple_of(b * TILE, TILE)
            span = pl.ds(row, TILE)

            @pl.when(has_left)
            def _():
                col_right(1, span, b).wait_recv()

            @pl.when(has_right)
            def _():
                col_left(1, span, b).wait_recv()

            update(1, row)
            start(r_copy, b)
            r_own(b).start()

    start_list = (fp_copy, fs_copy, ds_copy, dv_copy)
    for copy in start_list:
        sent(copy)

    @pl.loop(0, na)
    def _(c):
        sent(a_copy, c)

    p_x.wait_send()
    p_sib.wait_send()
    p_rel.wait_send()

    @pl.loop(1, n_space)
    def _(j):
        a2a(j).wait_send()

    @pl.when(has_above)
    def _():
        for sweep in range(SWEEPS):
            halo_up(sweep).wait_send()
        halo_face().wait_send()

    @pl.when(has_below)
    def _():
        for sweep in range(SWEEPS):
            halo_down(sweep).wait_send()

    @pl.when(has_right)
    def _():
        col_right(0, whole, nb).wait_send()

    @pl.when(has_left)
    def _():
        col_left(0, whole, nb).wait_send()

    @pl.loop(0, nb)
    def _(b):
        span = pl.ds(pl.multiple_of(b * TILE, TILE), TILE)

        @pl.when(has_right)
        def _():
            col_right(1, span, b).wait_send()

        @pl.when(has_left)
        def _():
            col_left(1, span, b).wait_send()

        sent(s_copy, b)
        sent(r_copy, b)
        r_own(b).wait()
        arrived(r_copy, b)


def finish(dinv, r, ds, out_a, out_r):
    per_dev, variables = r.shape[:2]
    for k in range(per_dev):
        scale = ds[k]
        rest = [r[k, v] for v in range(variables)]
        for u in range(variables):
            out_r[k, u] = rest[u]
            new = dinv[u, k, 0] * rest[0]
            for v in range(1, variables):
                new = new + dinv[u, k, v] * rest[v]
            out_a[k, u] = scale * new


def body(n_space, n_inst, a, s, fs, fp, ds, vol, blocks, dinv, *rest):
    per_dev, variables, rows, width = a.shape
    slots = rest[3].shape[2]
    nb = rows // TILE
    na = rows // CHUNK
    chunks = n_space // TILE
    instances = n_inst * per_dev
    cols = width // n_inst
    f32 = jnp.float32
    hbm = pl.BlockSpec(memory_space=pl.ANY)
    smem = pl.BlockSpec(memory_space=pltpu.SMEM)
    vmem = pl.BlockSpec(memory_space=pltpu.VMEM)
    dma = pltpu.SemaphoreType.DMA
    field = (per_dev, variables, rows, width)
    out = jax.ShapeDtypeStruct(field, f32)
    moved = (instances, variables, rows, cols)
    blocks = jnp.transpose(blocks, (1, 0, 2))
    dinv = jnp.transpose(dinv, (1, 0, 2))
    r = pl.pallas_call(
        functools.partial(kernel, n_space, n_inst),
        out_shape=out,
        in_specs=[hbm] * 6 + [smem] * 5 + [vmem] * 3 + [smem],
        out_specs=hbm,
        scratch_shapes=[
            pltpu.VMEM(field, f32),
            pltpu.VMEM(field, f32),
            pltpu.VMEM((SWEEPS, instances, variables, rows + 2 * TILE, cols), f32),
            pltpu.VMEM(moved, f32),
            pltpu.VMEM(moved, f32),
            pltpu.VMEM((instances, rows + TILE, cols), f32),
            pltpu.VMEM((instances, rows, cols), f32),
            pltpu.VMEM((instances, rows, cols), f32),
            pltpu.VMEM((rows, cols), f32),
            pltpu.VMEM((SWEEPS, rows, cols), f32),
            pltpu.VMEM((SWEEPS, rows, cols), f32),
            pltpu.VMEM((SWEEPS, rows, cols), f32),
            pltpu.VMEM((SWEEPS, rows, cols), f32),
            pltpu.VMEM((n_inst, TILE, cols), f32),
            pltpu.VMEM((instances * variables * variables, TILE, cols), f32),
            pltpu.VMEM((width, TILE * slots), jnp.bfloat16),
            pltpu.VMEM((per_dev, variables, chunks, TILE, slots), f32),
            pltpu.VMEM((4, per_dev, variables, chunks, TILE, slots), f32),
            pltpu.VMEM((n_space, per_dev, variables, slots), f32),
            pltpu.VMEM((n_space, per_dev, variables, slots), f32),
            pltpu.VMEM((PARTS * variables * rows, TILE * slots), jnp.bfloat16),
            dma((7,)),
            dma((nb,)),
            dma((nb,)),
            dma((3, na)),
            dma((3, na)),
            dma((3, 3)),
            dma((3, 3)),
            dma((3, nb)),
            dma((3, nb)),
            dma((3, nb)),
            dma((3, nb)),
            dma((3,)),
            dma((3,)),
            dma((2, nb + 1)),
            dma((2, nb + 1)),
            dma((2 * SWEEPS + 1,)),
            dma((2 * SWEEPS + 1,)),
            dma((3,)),
            dma((3,)),
            dma((n_space,)),
            dma((n_space,)),
        ],
        compiler_params=pltpu.CompilerParams(
            collective_id=0, has_side_effects=True, vmem_limit_bytes=56 * 1024 * 1024
        ),
    )(a, s, fs, fp, ds, vol, blocks, dinv, *rest)
    block = pl.BlockSpec((per_dev, variables, CHUNK, width), lambda b: (0, 0, b, 0))
    return pl.pallas_call(
        finish,
        grid=(rows // CHUNK,),
        out_shape=(out, out),
        in_specs=[smem, block, pl.BlockSpec((per_dev, CHUNK, width), lambda b: (0, b, 0))],
        out_specs=(block, block),
    )(dinv, r, ds)


def solution(mesh):
    in_specs = (
        P("inst", None, "space", None),
        P("inst", None, "space", None),
        P("inst", "space", None),
        P("inst", "space", None),
        P("inst", "space", None),
        P("space", None),
        P(),
        P("inst", None, None),
        P(),
        P(),
        P(),
        P("space", None, None),
        P(None, "space", None),
        P("space", None, None),
        P("space", None),
    )
    out_specs = (P("inst", None, "space", None), P("inst", None, "space", None))
    return jax.shard_map(
        functools.partial(body, mesh.shape["space"], mesh.shape["inst"]),
        mesh=mesh,
        in_specs=in_specs,
        out_specs=out_specs,
        check_vma=False,
    )
```

```python
import functools
import math

import jax
import jax.numpy as jnp
from jax import lax
from jax.experimental import pallas as pl
from jax.experimental.pallas import tpu as pltpu
from jax.sharding import PartitionSpec as P

SWEEPS = 2
TILE = 8
LANES = 128
PARTS = 2
CHUNK = 16
EARLY = 2
AHEAD = 2
LAG = 3
GROUP = 4
MESH = pl.DeviceIdType.MESH


def spectral_entry(offset, count):
    offset = offset % count
    if offset == 0 or 2 * offset == count:
        return 0.0
    return 0.5 * (-1.0) ** offset / math.tan(math.pi * offset / count)


def split_parts(value):
    parts = []
    for _ in range(PARTS):
        part = value.astype(jnp.bfloat16)
        parts.append(part)
        value = value - part.astype(jnp.float32)
    return parts


def kernel(
    n_space,
    n_inst,
    a_hbm,
    s_hbm,
    fs_hbm,
    fp_hbm,
    ds_hbm,
    vol_hbm,
    blocks,
    dinv,
    pblock,
    freq,
    shift,
    cells,
    targets,
    weights,
    counts,
    out_a,
    out_r,
    A,
    SP,
    AT,
    ST,
    RT,
    FS,
    FP,
    DS,
    VOL,
    DH,
    CL,
    CR,
    PW,
    PF,
    DV,
    DT,
    COL,
    PICK,
    ALLP,
    ROUTED,
    ARR,
    LHS,
    load_sem,
    own_s,
    own_r,
    a_s,
    a_r,
    c_s,
    c_r,
    s_s,
    s_r,
    r_s,
    r_r,
    d_s,
    d_r,
    cols_s,
    cols_r,
    hs,
    hr,
    ps,
    pr,
    q_s,
    q_r,
):
    per_dev, variables, rows, width = a_hbm.shape
    instances = n_inst * per_dev
    cols = width // n_inst
    slots = cells.shape[2]
    nb = rows // TILE
    na = rows // CHUNK
    inst = lax.axis_index("inst")
    me = lax.axis_index("space")
    odd = inst % 2
    sibling = inst + 1 - 2 * odd
    across = (inst + 2) % n_inst
    shift_bits = width.bit_length() - 1
    peers = (2, 1, 3)

    def remote(src, dst, send, recv, **device):
        return pltpu.make_async_remote_copy(
            src_ref=src, dst_ref=dst, send_sem=send, recv_sem=recv, device_id=device,
            device_id_type=MESH,
        )

    def columns(i):
        return pl.ds(pl.multiple_of(i * cols, cols), cols)

    def members(i):
        return pl.ds(i * per_dev, per_dev)

    def local(src, dst, n):
        return pltpu.make_async_copy(src, dst, load_sem.at[n])

    inner = pl.ds(TILE, rows)
    mine = columns(inst)
    own = members(inst)
    loads = [
        local(a_hbm, A, 0),
        local(s_hbm, SP, 1),
        local(a_hbm.at[:, :, :, mine], AT.at[0, own, :, inner, :], 2),
        local(fp_hbm.at[:, :, mine], FP.at[own], 3),
        local(fs_hbm.at[:, :, mine], FS.at[own, inner, :], 4),
        local(ds_hbm.at[:, :, mine], DS.at[own], 5),
        local(vol_hbm.at[:, mine], VOL, 6),
        local(ds_hbm, DH, 7),
    ]
    for copy in loads:
        copy.start()

    barrier = pltpu.get_barrier_semaphore()
    for d in peers:
        pl.semaphore_signal(
            barrier, inc=1, device_id={"inst": (inst + d) % n_inst}, device_id_type=MESH
        )

    @pl.loop(1, n_space)
    def _(j):
        pl.semaphore_signal(
            barrier, inc=1, device_id={"space": (me + j) % n_space}, device_id_type=MESH
        )

    def to(d):
        return (inst + d) % n_inst

    def source(d):
        return (inst + n_inst - d) % n_inst

    def a_copy(d, c, sender, receiver):
        span = pl.multiple_of(c * CHUNK, CHUNK)
        return remote(
            a_hbm.at[:, :, pl.ds(span, CHUNK), columns(receiver)],
            AT.at[0, members(sender), :, pl.ds(span + TILE, CHUNK), :],
            a_s.at[d - 1, c], a_r.at[d - 1, c], inst=receiver,
        )

    def fp_copy(d, sender, receiver):
        return remote(
            fp_hbm.at[:, :, columns(receiver)], FP.at[members(sender)],
            c_s.at[d - 1, 0], c_r.at[d - 1, 0], inst=receiver,
        )

    def fs_copy(d, sender, receiver):
        return remote(
            fs_hbm.at[:, :, columns(receiver)], FS.at[members(sender), inner, :],
            c_s.at[d - 1, 1], c_r.at[d - 1, 1], inst=receiver,
        )

    def ds_copy(d, sender, receiver):
        return remote(
            ds_hbm.at[:, :, columns(receiver)], DS.at[members(sender)],
            c_s.at[d - 1, 2], c_r.at[d - 1, 2], inst=receiver,
        )

    def dv_copy(d, sender, receiver):
        return remote(
            DV.at[sender], DV.at[sender], d_s.at[d - 1], d_r.at[d - 1], inst=receiver
        )

    def order(n):
        return (n + nb - 1) % nb

    def s_copy(d, n, sender, receiver):
        row = pl.multiple_of(order(n) * TILE, TILE)
        return remote(
            SP.at[:, :, pl.ds(row, TILE), columns(receiver)],
            ST.at[members(sender), :, pl.ds(row, TILE), :],
            s_s.at[d - 1, n], s_r.at[d - 1, n], inst=receiver,
        )

    def r_copy(d, b, sender, receiver):
        row = pl.multiple_of(b * TILE, TILE)
        return remote(
            RT.at[members(receiver), :, pl.ds(row, TILE), :],
            out_r.at[:, :, pl.ds(row, TILE), columns(sender)],
            r_s.at[d - 1, b], r_r.at[d - 1, b], inst=receiver,
        )

    def s_own(n):
        row = pl.multiple_of(order(n) * TILE, TILE)
        return pltpu.make_async_copy(
            SP.at[:, :, pl.ds(row, TILE), mine], ST.at[own, :, pl.ds(row, TILE), :], own_s.at[n]
        )

    def r_own(b):
        row = pl.multiple_of(b * TILE, TILE)
        return pltpu.make_async_copy(
            RT.at[own, :, pl.ds(row, TILE), :], out_r.at[:, :, pl.ds(row, TILE), mine],
            own_r.at[b],
        )

    def start(copy, *args):
        for d in peers:
            copy(d, *args, inst, to(d)).start()

    def arrived(copy, *args):
        for d in peers:
            copy(d, *args, source(d), inst).wait_recv()

    def sent(copy, *args):
        for d in peers:
            copy(d, *args, inst, to(d)).wait_send()

    has_above = me < n_space - 1
    has_below = me > 0
    above = (me + 1) % n_space
    below = (me + n_space - 1) % n_space
    has_left = inst > 0
    has_right = inst < n_inst - 1
    left_dev = (inst + n_inst - 1) % n_inst
    right_dev = (inst + 1) % n_inst

    def halo_up(sweep):
        return remote(
            AT.at[sweep, :, :, pl.ds(rows + TILE - 1, 1), :],
            AT.at[sweep, :, :, pl.ds(TILE - 1, 1), :],
            hs.at[2 * sweep], hr.at[2 * sweep], space=above,
        )

    def halo_down(sweep):
        return remote(
            AT.at[sweep, :, :, pl.ds(TILE, 1), :],
            AT.at[sweep, :, :, pl.ds(rows + TILE, 1), :],
            hs.at[2 * sweep + 1], hr.at[2 * sweep + 1], space=below,
        )

    def halo_face():
        last = 2 * SWEEPS
        return remote(
            FS.at[:, pl.ds(rows + TILE - 1, 1), :], FS.at[:, pl.ds(TILE - 1, 1), :],
            hs.at[last], hr.at[last], space=above,
        )

    def col_right(sweep, span, n):
        return remote(
            PW.at[sweep, span], CL.at[sweep, span], cols_s.at[0, n], cols_r.at[0, n],
            inst=right_dev,
        )

    def col_left(sweep, span, n):
        return remote(
            PF.at[sweep, span], CR.at[sweep, span], cols_s.at[1, n], cols_r.at[1, n],
            inst=left_dev,
        )

    def zeros(*shape):
        return jnp.zeros(shape, jnp.float32)

    @pl.when(me == 0)
    def _():
        FS[:, 0:TILE, :] = zeros(instances, TILE, cols)
        for sweep in range(SWEEPS):
            AT[sweep, :, :, 0:TILE, :] = zeros(instances, variables, TILE, cols)

    @pl.when(me == n_space - 1)
    def _():
        for sweep in range(SWEEPS):
            AT[sweep, :, :, rows + TILE : rows + 2 * TILE, :] = zeros(
                instances, variables, TILE, cols
            )

    @pl.when(inst == 0)
    def _():
        CL[...] = zeros(SWEEPS, rows, cols)

    @pl.when(inst == n_inst - 1)
    def _():
        CR[...] = zeros(SWEEPS, rows, cols)

    sub8 = lax.broadcasted_iota(jnp.int32, (TILE, cols), 0)
    lane8 = lax.broadcasted_iota(jnp.int32, (TILE, cols), 1)

    packed = zeros(TILE, cols)
    for k in range(per_dev):
        for u in range(variables):
            for v in range(variables):
                n = (k * variables + u) * variables + v
                packed = jnp.where(lane8 == n, dinv[u, k, v], packed)
    DV[inst] = packed

    pl.semaphore_wait(barrier, n_space + n_inst - 2)

    for c in range(min(EARLY, na)):
        start(a_copy, c)
    start(dv_copy)

    sub_w = lax.broadcasted_iota(jnp.int32, (width, slots), 0)
    sub_r = lax.broadcasted_iota(jnp.int32, (rows, slots), 0)

    def column_table(index, chunk):
        for q in range(TILE):
            line = index(chunk * TILE + q)
            column = jnp.bitwise_and(line, width - 1)
            hot = jnp.where(sub_w == column, 1.0, 0.0).astype(jnp.bfloat16)
            COL[:, q * slots : (q + 1) * slots] = hot

    def cell_line(q):
        return cells[0, pl.ds(q, 1), :]

    def target_line(p):
        return targets[p, 0:1, :]

    chunks = n_space // TILE

    loads[0].wait()

    @pl.loop(0, chunks)
    def _(chunk):
        column_table(cell_line, chunk)

        @pl.loop(0, per_dev)
        def _(k):
            field = A[k].reshape(variables * rows, width)
            stacked = jnp.concatenate(split_parts(field), axis=0)
            terms = jnp.dot(stacked, COL[...], preferred_element_type=jnp.float32)
            height = variables * rows
            found = terms[:height]
            for part in range(1, PARTS):
                found = found + terms[part * height : (part + 1) * height]
            for q in range(TILE):
                hit = sub_r == lax.shift_right_logical(cell_line(chunk * TILE + q), shift_bits)
                for v in range(variables):
                    piece = found[v * rows : (v + 1) * rows, q * slots : (q + 1) * slots]
                    PICK[k, v, chunk, q : q + 1, :] = jnp.sum(
                        jnp.where(hit, piece, 0.0), axis=0, keepdims=True
                    )

        lane = lax.broadcasted_iota(jnp.int32, (TILE, slots), 1)
        sub = lax.broadcasted_iota(jnp.int32, (TILE, slots), 0)
        limit = jnp.zeros((TILE, slots), jnp.int32)
        for q in range(TILE):
            limit = jnp.where(sub == q, counts[0, chunk * TILE + q], limit)
        first = pl.multiple_of(chunk * TILE, TILE)
        weight = jnp.where(lane < limit, weights[0, pl.ds(first, TILE), :], 0.0)

        for k in range(per_dev):
            picked = [PICK[k, v, chunk] for v in range(variables)]
            for u in range(variables):
                mixed = pblock[0, u] * picked[0]
                for v in range(1, variables):
                    mixed = mixed + pblock[v, u] * picked[v]
                ALLP[0, k, u, chunk] = mixed * weight

    p_x = remote(ALLP.at[0], ALLP.at[2], ps.at[0], pr.at[0], inst=across)
    p_sib = remote(ALLP.at[0], ALLP.at[3 - 2 * odd], ps.at[1], pr.at[1 + odd], inst=sibling)
    p_rel = remote(ALLP.at[2], ALLP.at[1 + 2 * odd], ps.at[2], pr.at[2 - odd], inst=sibling)
    p_sib_in = remote(ALLP.at[0], ALLP.at[1 + 2 * odd], ps.at[1], pr.at[2 - odd], inst=sibling)
    p_rel_in = remote(ALLP.at[2], ALLP.at[3 - 2 * odd], ps.at[2], pr.at[1 + odd], inst=sibling)
    p_x.start()
    p_sib.start()
    start(fp_copy)
    for c in range(min(EARLY, na), na):
        start(a_copy, c)
    start(fs_copy)
    start(ds_copy)
    p_x.wait_recv()
    p_rel.start()
    p_sib_in.wait_recv()
    p_rel_in.wait_recv()
    for k in range(per_dev):
        wanted = lax.rem(k - shift[0] + 2 * instances, instances)
        group = lax.div(wanted, per_dev)
        member = lax.rem(wanted, per_dev)

        @pl.loop(0, chunks)
        def _(chunk):
            for u in range(variables):
                value = ALLP[group, member, u, chunk]
                for q in range(TILE):
                    ROUTED[chunk * TILE + q, k, u : u + 1, :] = value[q : q + 1, :]

    def a2a(j):
        return remote(
            ROUTED.at[(me + j) % n_space], ARR.at[me], q_s.at[j], q_r.at[j],
            space=(me + j) % n_space,
        )

    @pl.loop(1, n_space)
    def _(j):
        a2a(j).start()

    ARR[me] = ROUTED[me]
    loads[1].wait()
    column_table(target_line, 0)

    @pl.loop(1, n_space)
    def _(j):
        remote(
            ROUTED.at[0], ARR.at[(me + n_space - j) % n_space], q_s.at[j], q_r.at[j],
            space=(me + j) % n_space,
        ).wait_recv()

    @pl.loop(0, chunks)
    def _(chunk):
        if chunks > 1:
            column_table(target_line, chunk)

        for k in range(per_dev):
            for p in range(TILE):
                hit = sub_r == lax.shift_right_logical(target_line(chunk * TILE + p), shift_bits)
                parts = split_parts(ARR[chunk * TILE + p, k])
                for n, part in enumerate(parts):
                    for u in range(variables):
                        begin = (n * variables + u) * rows
                        LHS[begin : begin + rows, p * slots : (p + 1) * slots] = jnp.where(
                            hit, part[u : u + 1, :].astype(jnp.float32), 0.0
                        ).astype(jnp.bfloat16)
            terms = lax.dot_general(
                LHS[...], COL[...], (((1,), (1,)), ((), ())), preferred_element_type=jnp.float32
            )
            height = variables * rows
            summed = terms[:height]
            for part in range(1, PARTS):
                summed = summed + terms[part * height : (part + 1) * height]
            SP[k] = SP[k] - summed.reshape(variables, rows, width)

    for copy in loads[2:]:
        copy.wait()
    arrived(fp_copy)

    @pl.loop(0, na)
    def _(c):
        arrived(a_copy, c)

    @pl.when(has_above)
    def _():
        halo_up(0).start()

    @pl.when(has_below)
    def _():
        halo_down(0).start()

    def pack(sweep, row):
        here = pl.ds(row, TILE)
        mid = pl.ds(row + TILE, TILE)
        last = zeros(TILE, cols)
        first = zeros(TILE, cols)
        for g in range(instances):
            fp = FP[g, here, :]
            for v in range(variables):
                n = g * variables + v
                a = AT[sweep, g, v, mid, :]
                first = jnp.where(lane8 == n, pltpu.roll(a, n, 1) if n else a, first)
                last = jnp.where(lane8 == n, pltpu.roll(fp * a, n + 1, 1), last)
        PW[sweep, here, :] = last
        PF[sweep, here, :] = first

    @pl.loop(0, nb)
    def _(b):
        pack(0, pl.multiple_of(b * TILE, TILE))

    whole = pl.ds(0, rows)

    @pl.when(has_right)
    def _():
        col_right(0, whole, nb).start()

    @pl.when(has_left)
    def _():
        col_left(0, whole, nb).start()

    for n in range(AHEAD):
        start(s_copy, n)

    @pl.loop(0, nb)
    def _(n):
        s_own(n).start()

    arrived(dv_copy)
    for g in range(instances):
        vector = DV[g // per_dev]
        for n in range(variables * variables):
            lane = (g % per_dev) * variables * variables + n
            DT[g * variables * variables + n] = jnp.broadcast_to(
                vector[:, lane : lane + 1], (TILE, cols)
            )

    arrived(fs_copy)

    @pl.when(has_above)
    def _():
        halo_face().start()

    arrived(ds_copy)

    @pl.when(has_below)
    def _():
        halo_up(0).wait_recv()
        halo_face().wait_recv()

    @pl.when(has_above)
    def _():
        halo_down(0).wait_recv()

    @pl.when(has_left)
    def _():
        col_right(0, whole, nb).wait_recv()

    @pl.when(has_right)
    def _():
        col_left(0, whole, nb).wait_recv()

    f1, f2, f3 = (spectral_entry(d, instances) for d in (1, 2, 3))

    def update(sweep, row):
        here = pl.ds(row, TILE)
        mid = pl.ds(row + TILE, TILE)
        low = pl.ds(row, TILE)
        high = pl.ds(row + 2 * TILE, TILE)
        scaled = freq[0] * VOL[here, :]
        v1 = (0.5 * (f1 - f3)) * scaled
        v2 = f2 * scaled
        v3 = (0.5 * (f1 + f3)) * scaled
        for u in range(variables):
            a = [AT[sweep, g, u, mid, :] for g in range(instances)]
            b = [a[g] - a[g + 4] for g in range(4)]
            c = [a[g] + a[g + 4] for g in range(4)]
            even = v1 * (c[1] - c[3])
            odds = v1 * (c[2] - c[0])
            q = [even, odds, -even, -odds]
            p = [
                v2 * b[2] + v3 * (b[1] + b[3]),
                v2 * b[3] + v3 * (b[2] - b[0]),
                v3 * (b[3] - b[1]) - v2 * b[0],
                -(v2 * b[1] + v3 * (b[0] + b[2])),
            ]
            for g in range(4):
                RT[g, u, here, :] = ST[g, u, here, :] - (q[g] + p[g])
                RT[g + 4, u, here, :] = ST[g + 4, u, here, :] - (q[g] - p[g])
        top = sub8 == TILE - 1
        bottom = sub8 == 0
        for base in range(0, instances, GROUP):
            span = range(base, base + GROUP)
            acc = {(g, u): RT[g, u, here, :] for g in span for u in range(variables)}
            fm = {g: FS[g, mid, :] for g in span}
            fl = {g: jnp.where(top, FS[g, low, :], fm[g]) for g in span}
            fp = {g: FP[g, here, :] for g in span}
            cl = CL[sweep, here, :]
            cr = CR[sweep, here, :]
            for v in range(variables):
                terms = {}
                for g in span:
                    n = g * variables + v
                    a = AT[sweep, g, v, mid, :]
                    x = pltpu.roll(fl[g] * jnp.where(top, AT[sweep, g, v, low, :], a), 1, 0)
                    y = fm[g] * pltpu.roll(
                        jnp.where(bottom, AT[sweep, g, v, high, :], a), TILE - 1, 0
                    )
                    edge = pltpu.roll(cl, cols - n, 1) if n else cl
                    left = jnp.where(lane8 == 0, edge, pltpu.roll(fp[g] * a, 1, 1))
                    edge = pltpu.roll(cr, cols - 1 - n, 1)
                    right = fp[g] * jnp.where(
                        lane8 == cols - 1, edge, pltpu.roll(a, cols - 1, 1)
                    )
                    terms[g] = (x, y, left, right)
                for u in range(variables):
                    k0, k1, k2, k3 = (blocks[v, n, u] for n in range(4))
                    for g in span:
                        x, y, left, right = terms[g]
                        acc[g, u] = acc[g, u] - (
                            (k0 * x + k1 * y) + (k2 * left + k3 * right)
                        )
            if sweep == SWEEPS - 1:
                for g in span:
                    for u in range(variables):
                        RT[g, u, here, :] = acc[g, u]
            else:
                for g in span:
                    scale = DS[g, here, :]
                    for u in range(variables):
                        n = (g * variables + u) * variables
                        new = DT[n] * acc[g, 0]
                        for v in range(1, variables):
                            new = new + DT[n + v] * acc[g, v]
                        AT[sweep + 1, g, u, mid, :] = scale * new

    @pl.loop(0, nb + LAG)
    def _(n):
        @pl.when(n < nb)
        def _():
            row = pl.multiple_of(order(n) * TILE, TILE)
            s_own(n).wait()
            arrived(s_copy, n)

            @pl.when(n + AHEAD < nb)
            def _():
                start(s_copy, n + AHEAD)

            update(0, row)
            pack(1, row)
            span = pl.ds(row, TILE)

            @pl.when(has_right)
            def _():
                col_right(1, span, order(n)).start()

            @pl.when(has_left)
            def _():
                col_left(1, span, order(n)).start()

        @pl.when(n == 1)
        def _():
            @pl.when(has_above)
            def _():
                halo_up(1).start()

            @pl.when(has_below)
            def _():
                halo_down(1).start()

        @pl.when(n == LAG)
        def _():
            @pl.when(has_below)
            def _():
                halo_up(1).wait_recv()

            @pl.when(has_above)
            def _():
                halo_down(1).wait_recv()

        @pl.when(n >= LAG)
        def _():
            b = n - LAG
            row = pl.multiple_of(b * TILE, TILE)
            span = pl.ds(row, TILE)

            @pl.when(has_left)
            def _():
                col_right(1, span, b).wait_recv()

            @pl.when(has_right)
            def _():
                col_left(1, span, b).wait_recv()

            update(1, row)
            start(r_copy, b)
            r_own(b).start()

    @pl.loop(0, nb)
    def _(b):
        here = pl.ds(pl.multiple_of(b * TILE, TILE), TILE)
        r_own(b).wait()
        arrived(r_copy, b)
        for k in range(per_dev):
            scale = DH[k, here, :]
            rest = [out_r[k, v, here, :] for v in range(variables)]
            for u in range(variables):
                new = dinv[u, k, 0] * rest[0]
                for v in range(1, variables):
                    new = new + dinv[u, k, v] * rest[v]
                out_a[k, u, here, :] = scale * new

    for copy in (fp_copy, fs_copy, ds_copy, dv_copy):
        sent(copy)

    @pl.loop(0, na)
    def _(c):
        sent(a_copy, c)

    p_x.wait_send()
    p_sib.wait_send()
    p_rel.wait_send()

    @pl.loop(1, n_space)
    def _(j):
        a2a(j).wait_send()

    @pl.when(has_above)
    def _():
        for sweep in range(SWEEPS):
            halo_up(sweep).wait_send()
        halo_face().wait_send()

    @pl.when(has_below)
    def _():
        for sweep in range(SWEEPS):
            halo_down(sweep).wait_send()

    @pl.when(has_right)
    def _():
        col_right(0, whole, nb).wait_send()

    @pl.when(has_left)
    def _():
        col_left(0, whole, nb).wait_send()

    @pl.loop(0, nb)
    def _(b):
        span = pl.ds(pl.multiple_of(b * TILE, TILE), TILE)

        @pl.when(has_right)
        def _():
            col_right(1, span, b).wait_send()

        @pl.when(has_left)
        def _():
            col_left(1, span, b).wait_send()

        sent(s_copy, b)
        sent(r_copy, b)


def finish(a, r, out_a, out_r, sems):
    copies = [
        pltpu.make_async_copy(a, out_a, sems.at[0]),
        pltpu.make_async_copy(r, out_r, sems.at[1]),
    ]
    for copy in copies:
        copy.start()
    for copy in copies:
        copy.wait()


def body(n_space, n_inst, a, s, fs, fp, ds, vol, blocks, dinv, *rest):
    per_dev, variables, rows, width = a.shape
    slots = rest[3].shape[2]
    nb = rows // TILE
    na = rows // CHUNK
    chunks = n_space // TILE
    instances = n_inst * per_dev
    cols = width // n_inst
    f32 = jnp.float32
    hbm = pl.BlockSpec(memory_space=pl.ANY)
    smem = pl.BlockSpec(memory_space=pltpu.SMEM)
    vmem = pl.BlockSpec(memory_space=pltpu.VMEM)
    dma = pltpu.SemaphoreType.DMA
    field = (per_dev, variables, rows, width)
    out = jax.ShapeDtypeStruct(field, f32)
    moved = (instances, variables, rows, cols)
    blocks = jnp.transpose(blocks, (1, 0, 2))
    dinv = jnp.transpose(dinv, (1, 0, 2))
    placed = pltpu.VMEM(field, f32)
    new, r = pl.pallas_call(
        functools.partial(kernel, n_space, n_inst),
        out_shape=(placed, placed),
        in_specs=[hbm] * 6 + [smem] * 5 + [vmem] * 3 + [smem],
        out_specs=(vmem, vmem),
        scratch_shapes=[
            pltpu.VMEM(field, f32),
            pltpu.VMEM(field, f32),
            pltpu.VMEM((SWEEPS, instances, variables, rows + 2 * TILE, cols), f32),
            pltpu.VMEM(moved, f32),
            pltpu.VMEM(moved, f32),
            pltpu.VMEM((instances, rows + TILE, cols), f32),
            pltpu.VMEM((instances, rows, cols), f32),
            pltpu.VMEM((instances, rows, cols), f32),
            pltpu.VMEM((rows, cols), f32),
            pltpu.VMEM((per_dev, rows, width), f32),
            pltpu.VMEM((SWEEPS, rows, cols), f32),
            pltpu.VMEM((SWEEPS, rows, cols), f32),
            pltpu.VMEM((SWEEPS, rows, cols), f32),
            pltpu.VMEM((SWEEPS, rows, cols), f32),
            pltpu.VMEM((n_inst, TILE, cols), f32),
            pltpu.VMEM((instances * variables * variables, TILE, cols), f32),
            pltpu.VMEM((width, TILE * slots), jnp.bfloat16),
            pltpu.VMEM((per_dev, variables, chunks, TILE, slots), f32),
            pltpu.VMEM((4, per_dev, variables, chunks, TILE, slots), f32),
            pltpu.VMEM((n_space, per_dev, variables, slots), f32),
            pltpu.VMEM((n_space, per_dev, variables, slots), f32),
            pltpu.VMEM((PARTS * variables * rows, TILE * slots), jnp.bfloat16),
            dma((8,)),
            dma((nb,)),
            dma((nb,)),
            dma((3, na)),
            dma((3, na)),
            dma((3, 3)),
            dma((3, 3)),
            dma((3, nb)),
            dma((3, nb)),
            dma((3, nb)),
            dma((3, nb)),
            dma((3,)),
            dma((3,)),
            dma((2, nb + 1)),
            dma((2, nb + 1)),
            dma((2 * SWEEPS + 1,)),
            dma((2 * SWEEPS + 1,)),
            dma((3,)),
            dma((3,)),
            dma((n_space,)),
            dma((n_space,)),
        ],
        compiler_params=pltpu.CompilerParams(
            collective_id=0, has_side_effects=True, vmem_limit_bytes=56 * 1024 * 1024
        ),
    )(a, s, fs, fp, ds, vol, blocks, dinv, *rest)
    return pl.pallas_call(
        finish,
        out_shape=(out, out),
        in_specs=[vmem, vmem],
        out_specs=(hbm, hbm),
        scratch_shapes=[dma((2,))],
    )(*(pltpu.with_memory_space_constraint(x, pltpu.VMEM) for x in (new, r)))


def solution(mesh):
    in_specs = (
        P("inst", None, "space", None),
        P("inst", None, "space", None),
        P("inst", "space", None),
        P("inst", "space", None),
        P("inst", "space", None),
        P("space", None),
        P(),
        P("inst", None, None),
        P(),
        P(),
        P(),
        P("space", None, None),
        P(None, "space", None),
        P("space", None, None),
        P("space", None),
    )
    out_specs = (P("inst", None, "space", None), P("inst", None, "space", None))
    return jax.shard_map(
        functools.partial(body, mesh.shape["space"], mesh.shape["inst"]),
        mesh=mesh,
        in_specs=in_specs,
        out_specs=out_specs,
        check_vma=False,
    )
```

```python
import functools
import math

import jax
import jax.numpy as jnp
from jax import lax
from jax.experimental import pallas as pl
from jax.experimental.pallas import tpu as pltpu
from jax.sharding import PartitionSpec as P

SWEEPS = 2
TILE = 8
LANES = 128
PARTS = 2
CHUNK = 16
EARLY = 2
AHEAD = 2
LAG = 3
GROUP = 4
MESH = pl.DeviceIdType.MESH


def spectral_entry(offset, count):
    offset = offset % count
    if offset == 0 or 2 * offset == count:
        return 0.0
    return 0.5 * (-1.0) ** offset / math.tan(math.pi * offset / count)


def split_parts(value):
    parts = []
    for _ in range(PARTS):
        part = value.astype(jnp.bfloat16)
        parts.append(part)
        value = value - part.astype(jnp.float32)
    return parts


def kernel(
    n_space,
    n_inst,
    a_hbm,
    s_hbm,
    fs_hbm,
    fp_hbm,
    ds_hbm,
    vol_hbm,
    blocks,
    dinv,
    pblock,
    freq,
    shift,
    cells,
    targets,
    weights,
    counts,
    out_a,
    out_r,
    A,
    SP,
    AT,
    ST,
    RT,
    FS,
    FP,
    DS,
    VOL,
    DH,
    CL,
    CR,
    PW,
    PF,
    DV,
    DT,
    COL,
    PICK,
    ALLP,
    ROUTED,
    ARR,
    LHS,
    load_sem,
    own_s,
    own_r,
    a_s,
    a_r,
    c_s,
    c_r,
    s_s,
    s_r,
    r_s,
    r_r,
    d_s,
    d_r,
    cols_s,
    cols_r,
    hs,
    hr,
    ps,
    pr,
    q_s,
    q_r,
    token,
):
    per_dev, variables, rows, width = a_hbm.shape
    instances = n_inst * per_dev
    cols = width // n_inst
    slots = cells.shape[2]
    nb = rows // TILE
    na = rows // CHUNK
    inst = lax.axis_index("inst")
    me = lax.axis_index("space")
    odd = inst % 2
    sibling = inst + 1 - 2 * odd
    across = (inst + 2) % n_inst
    shift_bits = width.bit_length() - 1
    peers = (2, 1, 3)

    def remote(src, dst, send, recv, **device):
        return pltpu.make_async_remote_copy(
            src_ref=src, dst_ref=dst, send_sem=send, recv_sem=recv, device_id=device,
            device_id_type=MESH,
        )

    def columns(i):
        return pl.ds(pl.multiple_of(i * cols, cols), cols)

    def members(i):
        return pl.ds(i * per_dev, per_dev)

    def local(src, dst, n):
        return pltpu.make_async_copy(src, dst, load_sem.at[n])

    inner = pl.ds(TILE, rows)
    mine = columns(inst)
    own = members(inst)
    loads = [
        local(a_hbm, A, 0),
        local(s_hbm, SP, 1),
        local(a_hbm.at[:, :, :, mine], AT.at[0, own, :, inner, :], 2),
        local(fp_hbm.at[:, :, mine], FP.at[own], 3),
        local(fs_hbm.at[:, :, mine], FS.at[own, inner, :], 4),
        local(ds_hbm.at[:, :, mine], DS.at[own], 5),
        local(vol_hbm.at[:, mine], VOL, 6),
        local(ds_hbm, DH, 7),
    ]
    for copy in loads:
        copy.start()

    barrier = pltpu.get_barrier_semaphore()
    for d in peers:
        pl.semaphore_signal(
            barrier, inc=1, device_id={"inst": (inst + d) % n_inst}, device_id_type=MESH
        )

    has_hi = me < n_space - 2
    has_lo = me > 1
    hi = (me + 2) % n_space
    lo = (me + n_space - 2) % n_space
    pair = me + 1 - 2 * (me % 2)

    def greet(semaphore, device):
        pl.semaphore_signal(
            semaphore, inc=1, device_id={"space": device}, device_id_type=MESH
        )

    greet(barrier, pair)

    @pl.when(has_hi)
    def _():
        greet(barrier, hi)

    @pl.when(has_lo)
    def _():
        greet(barrier, lo)

    def to(d):
        return (inst + d) % n_inst

    def source(d):
        return (inst + n_inst - d) % n_inst

    def a_copy(d, c, sender, receiver):
        span = pl.multiple_of(c * CHUNK, CHUNK)
        return remote(
            a_hbm.at[:, :, pl.ds(span, CHUNK), columns(receiver)],
            AT.at[0, members(sender), :, pl.ds(span + TILE, CHUNK), :],
            a_s.at[d - 1, c], a_r.at[d - 1, c], inst=receiver,
        )

    def fp_copy(d, sender, receiver):
        return remote(
            fp_hbm.at[:, :, columns(receiver)], FP.at[members(sender)],
            c_s.at[d - 1, 0], c_r.at[d - 1, 0], inst=receiver,
        )

    def fs_copy(d, sender, receiver):
        return remote(
            fs_hbm.at[:, :, columns(receiver)], FS.at[members(sender), inner, :],
            c_s.at[d - 1, 1], c_r.at[d - 1, 1], inst=receiver,
        )

    def ds_copy(d, sender, receiver):
        return remote(
            ds_hbm.at[:, :, columns(receiver)], DS.at[members(sender)],
            c_s.at[d - 1, 2], c_r.at[d - 1, 2], inst=receiver,
        )

    def dv_copy(d, sender, receiver):
        return remote(
            DV.at[sender], DV.at[sender], d_s.at[d - 1], d_r.at[d - 1], inst=receiver
        )

    def order(n):
        return (n + nb - 1) % nb

    def s_copy(d, n, sender, receiver):
        row = pl.multiple_of(order(n) * TILE, TILE)
        return remote(
            SP.at[:, :, pl.ds(row, TILE), columns(receiver)],
            ST.at[members(sender), :, pl.ds(row, TILE), :],
            s_s.at[d - 1, n], s_r.at[d - 1, n], inst=receiver,
        )

    def r_copy(d, b, sender, receiver):
        row = pl.multiple_of(b * TILE, TILE)
        return remote(
            RT.at[members(receiver), :, pl.ds(row, TILE), :],
            out_r.at[:, :, pl.ds(row, TILE), columns(sender)],
            r_s.at[d - 1, b], r_r.at[d - 1, b], inst=receiver,
        )

    def s_own(n):
        row = pl.multiple_of(order(n) * TILE, TILE)
        return pltpu.make_async_copy(
            SP.at[:, :, pl.ds(row, TILE), mine], ST.at[own, :, pl.ds(row, TILE), :], own_s.at[n]
        )

    def r_own(b):
        row = pl.multiple_of(b * TILE, TILE)
        return pltpu.make_async_copy(
            RT.at[own, :, pl.ds(row, TILE), :], out_r.at[:, :, pl.ds(row, TILE), mine],
            own_r.at[b],
        )

    def start(copy, *args):
        for d in peers:
            copy(d, *args, inst, to(d)).start()

    def arrived(copy, *args):
        for d in peers:
            copy(d, *args, source(d), inst).wait_recv()

    def sent(copy, *args):
        for d in peers:
            copy(d, *args, inst, to(d)).wait_send()

    has_above = me < n_space - 1
    has_below = me > 0
    above = (me + 1) % n_space
    below = (me + n_space - 1) % n_space
    has_left = inst > 0
    has_right = inst < n_inst - 1
    left_dev = (inst + n_inst - 1) % n_inst
    right_dev = (inst + 1) % n_inst

    def halo_up(sweep):
        return remote(
            AT.at[sweep, :, :, pl.ds(rows + TILE - 1, 1), :],
            AT.at[sweep, :, :, pl.ds(TILE - 1, 1), :],
            hs.at[2 * sweep], hr.at[2 * sweep], space=above,
        )

    def halo_down(sweep):
        return remote(
            AT.at[sweep, :, :, pl.ds(TILE, 1), :],
            AT.at[sweep, :, :, pl.ds(rows + TILE, 1), :],
            hs.at[2 * sweep + 1], hr.at[2 * sweep + 1], space=below,
        )

    def halo_face():
        last = 2 * SWEEPS
        return remote(
            FS.at[:, pl.ds(rows + TILE - 1, 1), :], FS.at[:, pl.ds(TILE - 1, 1), :],
            hs.at[last], hr.at[last], space=above,
        )

    def col_right(sweep, span, n):
        return remote(
            PW.at[sweep, span], CL.at[sweep, span], cols_s.at[0, n], cols_r.at[0, n],
            inst=right_dev,
        )

    def col_left(sweep, span, n):
        return remote(
            PF.at[sweep, span], CR.at[sweep, span], cols_s.at[1, n], cols_r.at[1, n],
            inst=left_dev,
        )

    def zeros(*shape):
        return jnp.zeros(shape, jnp.float32)

    @pl.when(me == 0)
    def _():
        FS[:, 0:TILE, :] = zeros(instances, TILE, cols)
        for sweep in range(SWEEPS):
            AT[sweep, :, :, 0:TILE, :] = zeros(instances, variables, TILE, cols)

    @pl.when(me == n_space - 1)
    def _():
        for sweep in range(SWEEPS):
            AT[sweep, :, :, rows + TILE : rows + 2 * TILE, :] = zeros(
                instances, variables, TILE, cols
            )

    @pl.when(inst == 0)
    def _():
        CL[...] = zeros(SWEEPS, rows, cols)

    @pl.when(inst == n_inst - 1)
    def _():
        CR[...] = zeros(SWEEPS, rows, cols)

    sub8 = lax.broadcasted_iota(jnp.int32, (TILE, cols), 0)
    lane8 = lax.broadcasted_iota(jnp.int32, (TILE, cols), 1)

    packed = zeros(TILE, cols)
    for k in range(per_dev):
        for u in range(variables):
            for v in range(variables):
                n = (k * variables + u) * variables + v
                packed = jnp.where(lane8 == n, dinv[u, k, v], packed)
    DV[inst] = packed

    pl.semaphore_wait(barrier, n_inst + has_hi.astype(jnp.int32) + has_lo.astype(jnp.int32))

    for c in range(min(EARLY, na)):
        start(a_copy, c)
    start(dv_copy)

    @pl.when(jnp.logical_not(has_hi))
    def _():
        greet(token.at[0], lo)

    @pl.when(jnp.logical_not(has_lo))
    def _():
        greet(token.at[1], hi)

    sub_w = lax.broadcasted_iota(jnp.int32, (width, slots), 0)
    sub_r = lax.broadcasted_iota(jnp.int32, (rows, slots), 0)

    def column_table(index, chunk):
        for q in range(TILE):
            line = index(chunk * TILE + q)
            column = jnp.bitwise_and(line, width - 1)
            hot = jnp.where(sub_w == column, 1.0, 0.0).astype(jnp.bfloat16)
            COL[:, q * slots : (q + 1) * slots] = hot

    def cell_line(q):
        return cells[0, pl.ds(q, 1), :]

    def target_line(p):
        return targets[p, 0:1, :]

    chunks = n_space // TILE

    loads[0].wait()

    @pl.loop(0, chunks)
    def _(chunk):
        column_table(cell_line, chunk)

        @pl.loop(0, per_dev)
        def _(k):
            field = A[k].reshape(variables * rows, width)
            stacked = jnp.concatenate(split_parts(field), axis=0)
            terms = jnp.dot(stacked, COL[...], preferred_element_type=jnp.float32)
            height = variables * rows
            found = terms[:height]
            for part in range(1, PARTS):
                found = found + terms[part * height : (part + 1) * height]
            for q in range(TILE):
                hit = sub_r == lax.shift_right_logical(cell_line(chunk * TILE + q), shift_bits)
                for v in range(variables):
                    piece = found[v * rows : (v + 1) * rows, q * slots : (q + 1) * slots]
                    PICK[k, v, chunk, q : q + 1, :] = jnp.sum(
                        jnp.where(hit, piece, 0.0), axis=0, keepdims=True
                    )

        lane = lax.broadcasted_iota(jnp.int32, (TILE, slots), 1)
        sub = lax.broadcasted_iota(jnp.int32, (TILE, slots), 0)
        limit = jnp.zeros((TILE, slots), jnp.int32)
        for q in range(TILE):
            limit = jnp.where(sub == q, counts[0, chunk * TILE + q], limit)
        first = pl.multiple_of(chunk * TILE, TILE)
        weight = jnp.where(lane < limit, weights[0, pl.ds(first, TILE), :], 0.0)

        for k in range(per_dev):
            picked = [PICK[k, v, chunk] for v in range(variables)]
            for u in range(variables):
                mixed = pblock[0, u] * picked[0]
                for v in range(1, variables):
                    mixed = mixed + pblock[v, u] * picked[v]
                ALLP[0, k, u, chunk] = mixed * weight

    p_x = remote(ALLP.at[0], ALLP.at[2], ps.at[0], pr.at[0], inst=across)
    p_sib = remote(ALLP.at[0], ALLP.at[3 - 2 * odd], ps.at[1], pr.at[1 + odd], inst=sibling)
    p_rel = remote(ALLP.at[2], ALLP.at[1 + 2 * odd], ps.at[2], pr.at[2 - odd], inst=sibling)
    p_sib_in = remote(ALLP.at[0], ALLP.at[1 + 2 * odd], ps.at[1], pr.at[2 - odd], inst=sibling)
    p_rel_in = remote(ALLP.at[2], ALLP.at[3 - 2 * odd], ps.at[2], pr.at[1 + odd], inst=sibling)
    p_x.start()
    p_sib.start()
    start(fp_copy)
    for c in range(min(EARLY, na), na):
        start(a_copy, c)
    start(fs_copy)
    start(ds_copy)

    @pl.when(has_hi)
    def _():
        pl.semaphore_wait(token.at[0], 1)

        @pl.when(has_lo)
        def _():
            greet(token.at[0], lo)

    @pl.when(has_lo)
    def _():
        pl.semaphore_wait(token.at[1], 1)

        @pl.when(has_hi)
        def _():
            greet(token.at[1], hi)

    p_x.wait_recv()
    p_rel.start()
    p_sib_in.wait_recv()
    p_rel_in.wait_recv()
    for k in range(per_dev):
        wanted = lax.rem(k - shift[0] + 2 * instances, instances)
        group = lax.div(wanted, per_dev)
        member = lax.rem(wanted, per_dev)

        @pl.loop(0, chunks)
        def _(chunk):
            for u in range(variables):
                value = ALLP[group, member, u, chunk]
                for q in range(TILE):
                    ROUTED[chunk * TILE + q, k, u : u + 1, :] = value[q : q + 1, :]

    def a2a(j):
        return remote(
            ROUTED.at[(me + j) % n_space], ARR.at[me], q_s.at[j], q_r.at[j],
            space=(me + j) % n_space,
        )

    @pl.loop(1, n_space)
    def _(j):
        a2a(j).start()

    ARR[me] = ROUTED[me]
    loads[1].wait()
    column_table(target_line, 0)

    @pl.loop(1, n_space)
    def _(j):
        remote(
            ROUTED.at[0], ARR.at[(me + n_space - j) % n_space], q_s.at[j], q_r.at[j],
            space=(me + j) % n_space,
        ).wait_recv()

    @pl.loop(0, chunks)
    def _(chunk):
        if chunks > 1:
            column_table(target_line, chunk)

        for k in range(per_dev):
            for p in range(TILE):
                hit = sub_r == lax.shift_right_logical(target_line(chunk * TILE + p), shift_bits)
                parts = split_parts(ARR[chunk * TILE + p, k])
                for n, part in enumerate(parts):
                    for u in range(variables):
                        begin = (n * variables + u) * rows
                        LHS[begin : begin + rows, p * slots : (p + 1) * slots] = jnp.where(
                            hit, part[u : u + 1, :].astype(jnp.float32), 0.0
                        ).astype(jnp.bfloat16)
            terms = lax.dot_general(
                LHS[...], COL[...], (((1,), (1,)), ((), ())), preferred_element_type=jnp.float32
            )
            height = variables * rows
            summed = terms[:height]
            for part in range(1, PARTS):
                summed = summed + terms[part * height : (part + 1) * height]
            SP[k] = SP[k] - summed.reshape(variables, rows, width)

    for copy in loads[2:]:
        copy.wait()
    arrived(fp_copy)

    @pl.loop(0, na)
    def _(c):
        arrived(a_copy, c)

    @pl.when(has_above)
    def _():
        halo_up(0).start()

    @pl.when(has_below)
    def _():
        halo_down(0).start()

    def pack(sweep, row):
        here = pl.ds(row, TILE)
        mid = pl.ds(row + TILE, TILE)
        last = zeros(TILE, cols)
        first = zeros(TILE, cols)
        for g in range(instances):
            fp = FP[g, here, :]
            for v in range(variables):
                n = g * variables + v
                a = AT[sweep, g, v, mid, :]
                first = jnp.where(lane8 == n, pltpu.roll(a, n, 1) if n else a, first)
                last = jnp.where(lane8 == n, pltpu.roll(fp * a, n + 1, 1), last)
        PW[sweep, here, :] = last
        PF[sweep, here, :] = first

    @pl.loop(0, nb)
    def _(b):
        pack(0, pl.multiple_of(b * TILE, TILE))

    whole = pl.ds(0, rows)

    @pl.when(has_right)
    def _():
        col_right(0, whole, nb).start()

    @pl.when(has_left)
    def _():
        col_left(0, whole, nb).start()

    for n in range(AHEAD):
        start(s_copy, n)

    @pl.loop(0, nb)
    def _(n):
        s_own(n).start()

    arrived(dv_copy)
    for g in range(instances):
        vector = DV[g // per_dev]
        for n in range(variables * variables):
            lane = (g % per_dev) * variables * variables + n
            DT[g * variables * variables + n] = jnp.broadcast_to(
                vector[:, lane : lane + 1], (TILE, cols)
            )

    arrived(fs_copy)

    @pl.when(has_above)
    def _():
        halo_face().start()

    arrived(ds_copy)

    @pl.when(has_below)
    def _():
        halo_up(0).wait_recv()
        halo_face().wait_recv()

    @pl.when(has_above)
    def _():
        halo_down(0).wait_recv()

    @pl.when(has_left)
    def _():
        col_right(0, whole, nb).wait_recv()

    @pl.when(has_right)
    def _():
        col_left(0, whole, nb).wait_recv()

    f1, f2, f3 = (spectral_entry(d, instances) for d in (1, 2, 3))

    def update(sweep, row):
        here = pl.ds(row, TILE)
        mid = pl.ds(row + TILE, TILE)
        low = pl.ds(row, TILE)
        high = pl.ds(row + 2 * TILE, TILE)
        scaled = freq[0] * VOL[here, :]
        v1 = (0.5 * (f1 - f3)) * scaled
        v2 = f2 * scaled
        v3 = (0.5 * (f1 + f3)) * scaled
        for u in range(variables):
            a = [AT[sweep, g, u, mid, :] for g in range(instances)]
            b = [a[g] - a[g + 4] for g in range(4)]
            c = [a[g] + a[g + 4] for g in range(4)]
            even = v1 * (c[1] - c[3])
            odds = v1 * (c[2] - c[0])
            q = [even, odds, -even, -odds]
            p = [
                v2 * b[2] + v3 * (b[1] + b[3]),
                v2 * b[3] + v3 * (b[2] - b[0]),
                v3 * (b[3] - b[1]) - v2 * b[0],
                -(v2 * b[1] + v3 * (b[0] + b[2])),
            ]
            for g in range(4):
                RT[g, u, here, :] = ST[g, u, here, :] - (q[g] + p[g])
                RT[g + 4, u, here, :] = ST[g + 4, u, here, :] - (q[g] - p[g])
        top = sub8 == TILE - 1
        bottom = sub8 == 0
        for base in range(0, instances, GROUP):
            span = range(base, base + GROUP)
            acc = {(g, u): RT[g, u, here, :] for g in span for u in range(variables)}
            fm = {g: FS[g, mid, :] for g in span}
            fl = {g: jnp.where(top, FS[g, low, :], fm[g]) for g in span}
            fp = {g: FP[g, here, :] for g in span}
            cl = CL[sweep, here, :]
            cr = CR[sweep, here, :]
            for v in range(variables):
                terms = {}
                for g in span:
                    n = g * variables + v
                    a = AT[sweep, g, v, mid, :]
                    x = pltpu.roll(fl[g] * jnp.where(top, AT[sweep, g, v, low, :], a), 1, 0)
                    y = fm[g] * pltpu.roll(
                        jnp.where(bottom, AT[sweep, g, v, high, :], a), TILE - 1, 0
                    )
                    edge = pltpu.roll(cl, cols - n, 1) if n else cl
                    left = jnp.where(lane8 == 0, edge, pltpu.roll(fp[g] * a, 1, 1))
                    edge = pltpu.roll(cr, cols - 1 - n, 1)
                    right = fp[g] * jnp.where(
                        lane8 == cols - 1, edge, pltpu.roll(a, cols - 1, 1)
                    )
                    terms[g] = (x, y, left, right)
                for u in range(variables):
                    k0, k1, k2, k3 = (blocks[v, n, u] for n in range(4))
                    for g in span:
                        x, y, left, right = terms[g]
                        acc[g, u] = acc[g, u] - (
                            (k0 * x + k1 * y) + (k2 * left + k3 * right)
                        )
            if sweep == SWEEPS - 1:
                for g in span:
                    for u in range(variables):
                        RT[g, u, here, :] = acc[g, u]
            else:
                for g in span:
                    scale = DS[g, here, :]
                    for u in range(variables):
                        n = (g * variables + u) * variables
                        new = DT[n] * acc[g, 0]
                        for v in range(1, variables):
                            new = new + DT[n + v] * acc[g, v]
                        AT[sweep + 1, g, u, mid, :] = scale * new

    @pl.loop(0, nb + LAG)
    def _(n):
        @pl.when(n < nb)
        def _():
            row = pl.multiple_of(order(n) * TILE, TILE)
            s_own(n).wait()
            arrived(s_copy, n)

            @pl.when(n + AHEAD < nb)
            def _():
                start(s_copy, n + AHEAD)

            update(0, row)
            pack(1, row)
            span = pl.ds(row, TILE)

            @pl.when(has_right)
            def _():
                col_right(1, span, order(n)).start()

            @pl.when(has_left)
            def _():
                col_left(1, span, order(n)).start()

        @pl.when(n == 1)
        def _():
            @pl.when(has_above)
            def _():
                halo_up(1).start()

            @pl.when(has_below)
            def _():
                halo_down(1).start()

        @pl.when(n == LAG)
        def _():
            @pl.when(has_below)
            def _():
                halo_up(1).wait_recv()

            @pl.when(has_above)
            def _():
                halo_down(1).wait_recv()

        @pl.when(n >= LAG)
        def _():
            b = n - LAG
            row = pl.multiple_of(b * TILE, TILE)
            span = pl.ds(row, TILE)

            @pl.when(has_left)
            def _():
                col_right(1, span, b).wait_recv()

            @pl.when(has_right)
            def _():
                col_left(1, span, b).wait_recv()

            update(1, row)
            start(r_copy, b)
            r_own(b).start()

    @pl.loop(0, nb)
    def _(b):
        here = pl.ds(pl.multiple_of(b * TILE, TILE), TILE)
        r_own(b).wait()
        arrived(r_copy, b)
        for k in range(per_dev):
            scale = DH[k, here, :]
            rest = [out_r[k, v, here, :] for v in range(variables)]
            for u in range(variables):
                new = dinv[u, k, 0] * rest[0]
                for v in range(1, variables):
                    new = new + dinv[u, k, v] * rest[v]
                out_a[k, u, here, :] = scale * new

    for copy in (fp_copy, fs_copy, ds_copy, dv_copy):
        sent(copy)

    @pl.loop(0, na)
    def _(c):
        sent(a_copy, c)

    p_x.wait_send()
    p_sib.wait_send()
    p_rel.wait_send()

    @pl.loop(1, n_space)
    def _(j):
        a2a(j).wait_send()

    @pl.when(has_above)
    def _():
        for sweep in range(SWEEPS):
            halo_up(sweep).wait_send()
        halo_face().wait_send()

    @pl.when(has_below)
    def _():
        for sweep in range(SWEEPS):
            halo_down(sweep).wait_send()

    @pl.when(has_right)
    def _():
        col_right(0, whole, nb).wait_send()

    @pl.when(has_left)
    def _():
        col_left(0, whole, nb).wait_send()

    @pl.loop(0, nb)
    def _(b):
        span = pl.ds(pl.multiple_of(b * TILE, TILE), TILE)

        @pl.when(has_right)
        def _():
            col_right(1, span, b).wait_send()

        @pl.when(has_left)
        def _():
            col_left(1, span, b).wait_send()

        sent(s_copy, b)
        sent(r_copy, b)


def finish(a, r, out_a, out_r, sems):
    copies = [
        pltpu.make_async_copy(a, out_a, sems.at[0]),
        pltpu.make_async_copy(r, out_r, sems.at[1]),
    ]
    for copy in copies:
        copy.start()
    for copy in copies:
        copy.wait()


def body(n_space, n_inst, a, s, fs, fp, ds, vol, blocks, dinv, *rest):
    per_dev, variables, rows, width = a.shape
    slots = rest[3].shape[2]
    nb = rows // TILE
    na = rows // CHUNK
    chunks = n_space // TILE
    instances = n_inst * per_dev
    cols = width // n_inst
    f32 = jnp.float32
    hbm = pl.BlockSpec(memory_space=pl.ANY)
    smem = pl.BlockSpec(memory_space=pltpu.SMEM)
    vmem = pl.BlockSpec(memory_space=pltpu.VMEM)
    dma = pltpu.SemaphoreType.DMA
    field = (per_dev, variables, rows, width)
    out = jax.ShapeDtypeStruct(field, f32)
    moved = (instances, variables, rows, cols)
    blocks = jnp.transpose(blocks, (1, 0, 2))
    dinv = jnp.transpose(dinv, (1, 0, 2))
    placed = pltpu.VMEM(field, f32)
    new, r = pl.pallas_call(
        functools.partial(kernel, n_space, n_inst),
        out_shape=(placed, placed),
        in_specs=[hbm] * 6 + [smem] * 5 + [vmem] * 3 + [smem],
        out_specs=(vmem, vmem),
        scratch_shapes=[
            pltpu.VMEM(field, f32),
            pltpu.VMEM(field, f32),
            pltpu.VMEM((SWEEPS, instances, variables, rows + 2 * TILE, cols), f32),
            pltpu.VMEM(moved, f32),
            pltpu.VMEM(moved, f32),
            pltpu.VMEM((instances, rows + TILE, cols), f32),
            pltpu.VMEM((instances, rows, cols), f32),
            pltpu.VMEM((instances, rows, cols), f32),
            pltpu.VMEM((rows, cols), f32),
            pltpu.VMEM((per_dev, rows, width), f32),
            pltpu.VMEM((SWEEPS, rows, cols), f32),
            pltpu.VMEM((SWEEPS, rows, cols), f32),
            pltpu.VMEM((SWEEPS, rows, cols), f32),
            pltpu.VMEM((SWEEPS, rows, cols), f32),
            pltpu.VMEM((n_inst, TILE, cols), f32),
            pltpu.VMEM((instances * variables * variables, TILE, cols), f32),
            pltpu.VMEM((width, TILE * slots), jnp.bfloat16),
            pltpu.VMEM((per_dev, variables, chunks, TILE, slots), f32),
            pltpu.VMEM((4, per_dev, variables, chunks, TILE, slots), f32),
            pltpu.VMEM((n_space, per_dev, variables, slots), f32),
            pltpu.VMEM((n_space, per_dev, variables, slots), f32),
            pltpu.VMEM((PARTS * variables * rows, TILE * slots), jnp.bfloat16),
            dma((8,)),
            dma((nb,)),
            dma((nb,)),
            dma((3, na)),
            dma((3, na)),
            dma((3, 3)),
            dma((3, 3)),
            dma((3, nb)),
            dma((3, nb)),
            dma((3, nb)),
            dma((3, nb)),
            dma((3,)),
            dma((3,)),
            dma((2, nb + 1)),
            dma((2, nb + 1)),
            dma((2 * SWEEPS + 1,)),
            dma((2 * SWEEPS + 1,)),
            dma((3,)),
            dma((3,)),
            dma((n_space,)),
            dma((n_space,)),
            pltpu.SemaphoreType.REGULAR((2,)),
        ],
        compiler_params=pltpu.CompilerParams(
            collective_id=0, has_side_effects=True, vmem_limit_bytes=56 * 1024 * 1024
        ),
    )(a, s, fs, fp, ds, vol, blocks, dinv, *rest)
    return pl.pallas_call(
        finish,
        out_shape=(out, out),
        in_specs=[vmem, vmem],
        out_specs=(hbm, hbm),
        scratch_shapes=[dma((2,))],
    )(*(pltpu.with_memory_space_constraint(x, pltpu.VMEM) for x in (new, r)))


def solution(mesh):
    in_specs = (
        P("inst", None, "space", None),
        P("inst", None, "space", None),
        P("inst", "space", None),
        P("inst", "space", None),
        P("inst", "space", None),
        P("space", None),
        P(),
        P("inst", None, None),
        P(),
        P(),
        P(),
        P("space", None, None),
        P(None, "space", None),
        P("space", None, None),
        P("space", None),
    )
    out_specs = (P("inst", None, "space", None), P("inst", None, "space", None))
    return jax.shard_map(
        functools.partial(body, mesh.shape["space"], mesh.shape["inst"]),
        mesh=mesh,
        in_specs=in_specs,
        out_specs=out_specs,
        check_vma=False,
    )
```

```python
import functools
import math

import jax
import jax.numpy as jnp
from jax import lax
from jax.experimental import pallas as pl
from jax.experimental.pallas import tpu as pltpu
from jax.sharding import PartitionSpec as P

SWEEPS = 2
TILE = 8
LANES = 128
PARTS = 2
CHIP = 4
GROUP = 2
MESH = pl.DeviceIdType.MESH


def spectral_entry(offset, count):
    offset = offset % count
    if offset == 0 or 2 * offset == count:
        return 0.0
    return 0.5 * (-1.0) ** offset / math.tan(math.pi * offset / count)


def split_parts(value):
    parts = []
    for _ in range(PARTS):
        part = value.astype(jnp.bfloat16)
        parts.append(part)
        value = value - part.astype(jnp.float32)
    return parts


def kernel(
    n_space,
    n_inst,
    a_hbm,
    s_hbm,
    fs_hbm,
    fp_hbm,
    ds_hbm,
    vol_hbm,
    blocks_hbm,
    dinv_hbm,
    pblock_hbm,
    freq_hbm,
    shift_hbm,
    cells_hbm,
    targets_hbm,
    weights_hbm,
    counts_hbm,
    out_a,
    out_r,
    blocks,
    dinv,
    pblock,
    freq,
    shift,
    cells,
    targets,
    weights,
    counts,
    A,
    AT,
    ST,
    Y,
    RT,
    PT,
    NEAR,
    FAR,
    FS,
    FP,
    DS,
    VOL,
    DH,
    CL,
    CR,
    PW,
    PF,
    DV,
    DT,
    COL,
    PICK,
    ALLP,
    ROUTED,
    ARR,
    LHS,
    load_sem,
    own_r,
    in_s,
    in_r,
    c_s,
    c_r,
    r_s,
    r_r,
    cols_s,
    cols_r,
    hs,
    hr,
    ps,
    pr,
    q_s,
    q_r,
    token,
):
    per_dev, variables, rows, width = a_hbm.shape
    instances = n_inst * per_dev
    cols = width // 2
    slots = cells.shape[2]
    nb = rows // TILE
    part_rows = rows // 2
    inst = lax.axis_index("inst")
    me = lax.axis_index("space")
    odd = inst % 2
    sibling = inst + 1 - 2 * odd
    across = (inst + 2) % n_inst
    diagonal = (sibling + 2) % n_inst
    shift_bits = width.bit_length() - 1
    peers = (across, diagonal, sibling)
    mine = 2 * odd
    other = 2 - 2 * odd
    seats = (4 + mine, 4 + other, other)

    def remote(src, dst, send, recv, **device):
        return pltpu.make_async_remote_copy(
            src_ref=src, dst_ref=dst, send_sem=send, recv_sem=recv, device_id=device,
            device_id_type=MESH,
        )

    def half(c):
        return pl.ds(pl.multiple_of(c * cols, cols), cols)

    def pair(seat):
        return pl.ds(seat, per_dev)

    def local(src, dst, n):
        return pltpu.make_async_copy(src, dst, load_sem.at[n])

    inner = pl.ds(TILE, rows)
    here_cols = half(odd)
    loads = [
        local(a_hbm, A, 0),
        local(s_hbm.at[:, :, :, here_cols], ST.at[pair(mine)], 1),
        local(a_hbm.at[:, :, :, here_cols], AT.at[pair(mine), :, inner, :], 2),
        local(fp_hbm.at[:, :, here_cols], FP.at[pair(mine)], 3),
        local(fs_hbm.at[:, :, here_cols], FS.at[pair(mine), inner, :], 4),
        local(ds_hbm.at[:, :, here_cols], DS.at[pair(mine)], 5),
        local(vol_hbm.at[:, here_cols], VOL, 6),
        local(ds_hbm, DH, 7),
    ]
    tables = [
        local(dinv_hbm, dinv, 8),
        local(cells_hbm, cells, 9),
        local(counts_hbm, counts, 10),
        local(weights_hbm, weights, 11),
        local(pblock_hbm, pblock, 12),
        local(shift_hbm, shift, 13),
        local(targets_hbm, targets, 14),
        local(blocks_hbm, blocks, 15),
        local(freq_hbm, freq, 16),
    ]

    barrier = pltpu.get_barrier_semaphore()
    for peer in peers:
        pl.semaphore_signal(barrier, inc=1, device_id={"inst": peer}, device_id_type=MESH)

    has_hi = me < n_space - 2
    has_lo = me > 1
    hi = (me + 2) % n_space
    lo = (me + n_space - 2) % n_space
    partner = me + 1 - 2 * (me % 2)

    def greet(semaphore, device):
        pl.semaphore_signal(
            semaphore, inc=1, device_id={"space": device}, device_id_type=MESH
        )

    greet(barrier, partner)

    @pl.when(has_hi)
    def _():
        greet(barrier, hi)

    @pl.when(has_lo)
    def _():
        greet(barrier, lo)

    for copy in loads[:1] + tables + loads[1:]:
        copy.start()

    def incoming(n, target, seat):
        if n == 0:
            src, dst = a_hbm, AT.at[pair(seat), :, inner, :]
        else:
            src, dst = s_hbm, ST.at[pair(seat)]
        return remote(
            src.at[:, :, :, half(target)], dst, in_s.at[n], in_r.at[n], inst=sibling
        )

    def seat_there(kind):
        return mine + (4 if kind < 2 else 0)

    def target_half(kind):
        return odd if kind == 0 else 1 - odd

    def ds_copy(kind, column, seat):
        return remote(
            ds_hbm.at[:, :, half(column)], DS.at[pair(seat)],
            c_s.at[kind, 0], c_r.at[kind, 0], inst=peers[kind],
        )

    def fp_copy(kind, column, seat):
        return remote(
            fp_hbm.at[:, :, half(column)], FP.at[pair(seat)],
            c_s.at[kind, 1], c_r.at[kind, 1], inst=peers[kind],
        )

    def fs_part(part):
        def make(kind, column, seat):
            begin = part * part_rows
            return remote(
                fs_hbm.at[:, pl.ds(begin, part_rows), half(column)],
                FS.at[pair(seat), pl.ds(begin + TILE, part_rows), :],
                c_s.at[kind, 2 + part], c_r.at[kind, 2 + part], inst=peers[kind],
            )

        return make

    def dv_copy(kind, column, seat):
        return remote(
            DV.at[0], DV.at[kind + 1], c_s.at[kind, 4], c_r.at[kind, 4], inst=peers[kind]
        )

    fs_low, fs_high = fs_part(0), fs_part(1)
    linked, beside = (0, 1), (2,)

    def start(copy, kinds=(0, 1, 2)):
        for kind in kinds:
            copy(kind, target_half(kind), seat_there(kind)).start()

    def arrived(copy, kinds=(0, 1, 2)):
        for kind in kinds:
            copy(kind, odd, seats[kind]).wait_recv()

    def sent(copy, kinds=(0, 1, 2)):
        for kind in kinds:
            copy(kind, target_half(kind), seat_there(kind)).wait_send()

    def r_copy(kind, b, column):
        row = pl.multiple_of(b * TILE, TILE)
        land = FAR if kind < 2 else NEAR
        return remote(
            RT.at[pair(seats[kind]), :, pl.ds(row, TILE), :],
            land.at[:, :, pl.ds(row, TILE), half(column)],
            r_s.at[kind, b], r_r.at[kind, b], inst=peers[kind],
        )

    def r_own(b):
        row = pl.multiple_of(b * TILE, TILE)
        return pltpu.make_async_copy(
            RT.at[pair(mine), :, pl.ds(row, TILE), :],
            NEAR.at[:, :, pl.ds(row, TILE), here_cols], own_r.at[b],
        )

    has_above = me < n_space - 1
    has_below = me > 0
    above = (me + 1) % n_space
    below = (me + n_space - 1) % n_space
    field_of = (AT, Y.at[pl.ds(CHIP, CHIP)], Y.at[pl.ds(0, CHIP)])

    def halo_up(stage):
        ref = field_of[stage]
        return remote(
            ref.at[:, :, pl.ds(rows + TILE - 1, 1), :], ref.at[:, :, pl.ds(TILE - 1, 1), :],
            hs.at[2 * stage], hr.at[2 * stage], space=above,
        )

    def halo_down(stage):
        ref = field_of[stage]
        return remote(
            ref.at[:, :, pl.ds(TILE, 1), :], ref.at[:, :, pl.ds(rows + TILE, 1), :],
            hs.at[2 * stage + 1], hr.at[2 * stage + 1], space=below,
        )

    def halo_face(side):
        group = pl.ds(side * CHIP, CHIP)
        return remote(
            FS.at[group, pl.ds(rows + TILE - 1, 1), :], FS.at[group, pl.ds(TILE - 1, 1), :],
            hs.at[6 + side], hr.at[6 + side], space=above,
        )

    def col_right(stage):
        return remote(
            PW.at[stage], CL.at[stage], cols_s.at[stage], cols_r.at[stage], inst=sibling
        )

    def col_left(stage):
        return remote(
            PF.at[stage], CR.at[stage], cols_s.at[stage], cols_r.at[stage], inst=sibling
        )

    def halos_start(stage):
        @pl.when(has_above)
        def _():
            halo_up(stage).start()

        @pl.when(has_below)
        def _():
            halo_down(stage).start()

    def halos_wait(stage):
        @pl.when(has_below)
        def _():
            halo_up(stage).wait_recv()

        @pl.when(has_above)
        def _():
            halo_down(stage).wait_recv()

        @pl.when(odd == 1)
        def _():
            col_right(stage).wait_recv()

        @pl.when(odd == 0)
        def _():
            col_left(stage).wait_recv()

    def halos_sent(stage):
        @pl.when(has_above)
        def _():
            halo_up(stage).wait_send()

        @pl.when(has_below)
        def _():
            halo_down(stage).wait_send()

        @pl.when(odd == 0)
        def _():
            col_right(stage).wait_send()

        @pl.when(odd == 1)
        def _():
            col_left(stage).wait_send()

    def zeros(*shape):
        return jnp.zeros(shape, jnp.float32)

    @pl.when(me == 0)
    def _():
        FS[:, 0:TILE, :] = zeros(instances, TILE, cols)
        AT[:, :, 0:TILE, :] = zeros(CHIP, variables, TILE, cols)
        Y[:, :, 0:TILE, :] = zeros(instances, variables, TILE, cols)

    @pl.when(me == n_space - 1)
    def _():
        AT[:, :, rows + TILE : rows + 2 * TILE, :] = zeros(CHIP, variables, TILE, cols)
        Y[:, :, rows + TILE : rows + 2 * TILE, :] = zeros(instances, variables, TILE, cols)

    @pl.when(odd == 0)
    def _():
        CL[...] = zeros(3, rows, LANES)

    @pl.when(odd == 1)
    def _():
        CR[...] = zeros(3, rows, LANES)

    sub8 = lax.broadcasted_iota(jnp.int32, (TILE, cols), 0)
    lane8 = lax.broadcasted_iota(jnp.int32, (TILE, cols), 1)
    lane1 = lax.broadcasted_iota(jnp.int32, (TILE, LANES), 1)

    pl.semaphore_wait(barrier, n_inst + has_hi.astype(jnp.int32) + has_lo.astype(jnp.int32))

    start(ds_copy, linked)
    start(fp_copy, linked)
    incoming(0, 1 - odd, mine).start()
    start(fp_copy, beside)
    start(fs_high, beside)
    start(fs_low, beside)
    start(ds_copy, beside)
    incoming(1, 1 - odd, mine).start()

    tables[0].wait()
    packed = zeros(TILE, LANES)
    for k in range(per_dev):
        for u in range(variables):
            for v in range(variables):
                n = (k * variables + u) * variables + v
                packed = jnp.where(lane1 == n, dinv[u, k, v], packed)
    DV[0] = packed
    start(dv_copy)

    @pl.when(jnp.logical_not(has_hi))
    def _():
        greet(token.at[0], lo)

    @pl.when(jnp.logical_not(has_lo))
    def _():
        greet(token.at[1], hi)

    sub_w = lax.broadcasted_iota(jnp.int32, (width, slots), 0)
    sub_h = lax.broadcasted_iota(jnp.int32, (cols, slots), 0)
    sub_r = lax.broadcasted_iota(jnp.int32, (rows, slots), 0)

    def column_table(index, chunk):
        for q in range(TILE):
            line = index(chunk * TILE + q)
            column = jnp.bitwise_and(line, width - 1)
            hot = jnp.where(sub_w == column, 1.0, 0.0).astype(jnp.bfloat16)
            COL[:, q * slots : (q + 1) * slots] = hot

    def half_table(index, chunk):
        for q in range(TILE):
            line = index(chunk * TILE + q)
            column = jnp.bitwise_and(line, width - 1) - odd * cols
            hot = jnp.where(sub_h == column, 1.0, 0.0).astype(jnp.bfloat16)
            COL[0:cols, q * slots : (q + 1) * slots] = hot

    def cell_line(q):
        return cells[0, pl.ds(q, 1), :]

    def target_line(p):
        return targets[p, 0:1, :]

    chunks = n_space // TILE

    loads[0].wait()
    for copy in tables[1:]:
        copy.wait()

    @pl.loop(0, chunks)
    def _(chunk):
        column_table(cell_line, chunk)

        @pl.loop(0, per_dev)
        def _(k):
            field = A[k].reshape(variables * rows, width)
            stacked = jnp.concatenate(split_parts(field), axis=0)
            terms = jnp.dot(stacked, COL[...], preferred_element_type=jnp.float32)
            height = variables * rows
            found = terms[:height]
            for part in range(1, PARTS):
                found = found + terms[part * height : (part + 1) * height]
            for q in range(TILE):
                hit = sub_r == lax.shift_right_logical(cell_line(chunk * TILE + q), shift_bits)
                for v in range(variables):
                    piece = found[v * rows : (v + 1) * rows, q * slots : (q + 1) * slots]
                    PICK[k, v, chunk, q : q + 1, :] = jnp.sum(
                        jnp.where(hit, piece, 0.0), axis=0, keepdims=True
                    )

        lane = lax.broadcasted_iota(jnp.int32, (TILE, slots), 1)
        sub = lax.broadcasted_iota(jnp.int32, (TILE, slots), 0)
        limit = jnp.zeros((TILE, slots), jnp.int32)
        for q in range(TILE):
            limit = jnp.where(sub == q, counts[0, chunk * TILE + q], limit)
        first = pl.multiple_of(chunk * TILE, TILE)
        weight = jnp.where(lane < limit, weights[0, pl.ds(first, TILE), :], 0.0)

        for k in range(per_dev):
            picked = [PICK[k, v, chunk] for v in range(variables)]
            for u in range(variables):
                mixed = pblock[0, u] * picked[0]
                for v in range(1, variables):
                    mixed = mixed + pblock[v, u] * picked[v]
                ALLP[0, k, u, chunk] = mixed * weight

    p_x = remote(ALLP.at[0], ALLP.at[2], ps.at[0], pr.at[0], inst=across)
    p_sib = remote(ALLP.at[0], ALLP.at[3 - 2 * odd], ps.at[1], pr.at[1 + odd], inst=sibling)
    p_rel = remote(ALLP.at[2], ALLP.at[1 + 2 * odd], ps.at[2], pr.at[2 - odd], inst=sibling)
    p_sib_in = remote(ALLP.at[0], ALLP.at[1 + 2 * odd], ps.at[1], pr.at[2 - odd], inst=sibling)
    p_rel_in = remote(ALLP.at[2], ALLP.at[3 - 2 * odd], ps.at[2], pr.at[1 + odd], inst=sibling)
    p_x.start()
    p_sib.start()
    start(fs_high, linked)
    start(fs_low, linked)

    @pl.when(has_hi)
    def _():
        pl.semaphore_wait(token.at[0], 1)

        @pl.when(has_lo)
        def _():
            greet(token.at[0], lo)

    @pl.when(has_lo)
    def _():
        pl.semaphore_wait(token.at[1], 1)

        @pl.when(has_hi)
        def _():
            greet(token.at[1], hi)

    for copy in loads[1:]:
        copy.wait()
    for n in range(2):
        incoming(n, odd, other).wait_recv()
    for copy in (fp_copy, fs_high, fs_low):
        arrived(copy, beside)
    halos_start(0)

    @pl.when(has_above)
    def _():
        halo_face(0).start()

    def wide(tile):
        return jnp.concatenate([tile] * (cols // LANES), axis=1)

    def pack(stage, ref, base):
        @pl.loop(0, nb)
        def _(b):
            row = pl.multiple_of(b * TILE, TILE)
            here = pl.ds(row, TILE)
            mid = pl.ds(row + TILE, TILE)
            last = zeros(TILE, LANES)
            first = zeros(TILE, LANES)
            for r in range(CHIP):
                fp = FP[base + r, here, cols - LANES : cols]
                for v in range(variables):
                    n = r * variables + v
                    a = ref[base + r, v, mid, 0:LANES]
                    w = fp * ref[base + r, v, mid, cols - LANES : cols]
                    first = jnp.where(lane1 == n, pltpu.roll(a, n, 1) if n else a, first)
                    last = jnp.where(lane1 == n, pltpu.roll(w, n + 1, 1), last)
            PW[stage, here, :] = last
            PF[stage, here, :] = first

        @pl.when(odd == 0)
        def _():
            col_right(stage).start()

        @pl.when(odd == 1)
        def _():
            col_left(stage).start()

    pack(0, AT, 0)

    arrived(dv_copy)
    for position in range(instances):
        if position < CHIP:
            kind = jnp.where(odd == position // per_dev, 0, 3)
        else:
            kind = jnp.where(odd == (position - CHIP) // per_dev, 1, 2)
        vector = DV[kind]
        for n in range(variables * variables):
            lane = (position % per_dev) * variables * variables + n
            DT[position * variables * variables + n] = jnp.broadcast_to(
                vector[:, lane : lane + 1], (TILE, LANES)
            )

    arrived(ds_copy)

    f1, f2, f3 = (spectral_entry(d, instances) for d in (1, 2, 3))

    def spectral(a, row):
        here = pl.ds(row, TILE)
        scaled = freq[0] * VOL[here, :]
        v1 = (0.5 * (f1 - f3)) * scaled
        v2 = f2 * scaled
        v3 = (0.5 * (f1 + f3)) * scaled
        results = []
        for u in range(variables):
            near = [a(r, u) for r in range(4)]
            far = [a(r, u) for r in range(4, 8)]
            b = [m if f is None else m - f for m, f in zip(near, far)]
            c = [m if f is None else m + f for m, f in zip(near, far)]
            even = v1 * (c[1] - c[3])
            odds = v1 * (c[2] - c[0])
            q = [even, odds, -even, -odds]
            p = [
                v2 * b[2] + v3 * (b[1] + b[3]),
                v2 * b[3] + v3 * (b[2] - b[0]),
                v3 * (b[3] - b[1]) - v2 * b[0],
                -(v2 * b[1] + v3 * (b[0] + b[2])),
            ]
            results.append((q, p))
        return results

    def coupling(acc, span, ref, row, stage):
        here = pl.ds(row, TILE)
        mid = pl.ds(row + TILE, TILE)
        low = pl.ds(row, TILE)
        high = pl.ds(row + 2 * TILE, TILE)
        top = sub8 == TILE - 1
        bottom = sub8 == 0
        fm = {r: FS[r, mid, :] for r in span}
        fl = {r: jnp.where(top, FS[r, low, :], fm[r]) for r in span}
        fp = {r: FP[r, here, :] for r in span}
        cl = CL[stage, here, :]
        cr = CR[stage, here, :]
        for v in range(variables):
            terms = {}
            for r in span:
                n = (r % CHIP) * variables + v
                a = ref[r, v, mid, :]
                x = pltpu.roll(fl[r] * jnp.where(top, ref[r, v, low, :], a), 1, 0)
                y = fm[r] * pltpu.roll(
                    jnp.where(bottom, ref[r, v, high, :], a), TILE - 1, 0
                )
                edge = wide(pltpu.roll(cl, LANES - n, 1) if n else cl)
                left = jnp.where(lane8 == 0, edge, pltpu.roll(fp[r] * a, 1, 1))
                edge = wide(pltpu.roll(cr, LANES - 1 - n, 1))
                right = fp[r] * jnp.where(
                    lane8 == cols - 1, edge, pltpu.roll(a, cols - 1, 1)
                )
                terms[r] = (x, y, left, right)
            for u in range(variables):
                k0, k1, k2, k3 = (blocks[v, n, u] for n in range(4))
                for r in span:
                    x, y, left, right = terms[r]
                    acc[r, u] = acc[r, u] - ((k0 * x + k1 * y) + (k2 * left + k3 * right))
        return acc

    def inverse(acc, r, u, here):
        n = (r * variables + u) * variables
        new = wide(DT[n]) * acc[0]
        for v in range(1, variables):
            new = new + wide(DT[n + v]) * acc[v]
        return DS[r, here, :] * new

    halos_wait(0)

    @pl.when(has_below)
    def _():
        halo_face(0).wait_recv()

    @pl.loop(0, nb)
    def _(b):
        row = pl.multiple_of(b * TILE, TILE)
        here = pl.ds(row, TILE)
        mid = pl.ds(row + TILE, TILE)
        found = spectral(lambda r, u: AT[r, u, mid, :] if r < CHIP else None, row)
        for u, (q, p) in enumerate(found):
            for r in range(CHIP):
                RT[r, u, here, :] = ST[r, u, here, :] - (q[r] + p[r])
                RT[CHIP + r, u, here, :] = p[r] - q[r]
        for base in range(0, instances, GROUP):
            span = range(base, base + GROUP)
            acc = {(r, u): RT[r, u, here, :] for r in span for u in range(variables)}
            if base < CHIP:
                acc = coupling(acc, span, AT, row, 0)
            for r in span:
                line = [acc[r, v] for v in range(variables)]
                for u in range(variables):
                    Y[r, u, mid, :] = inverse(line, r, u, here)

    halos_start(1)
    arrived(fp_copy, linked)
    pack(1, Y, CHIP)

    p_x.wait_recv()
    p_rel.start()
    p_sib_in.wait_recv()
    p_rel_in.wait_recv()

    @pl.loop(0, instances)
    def _(k):
        wanted = lax.rem(k - shift[0] + 2 * instances, instances)
        group = lax.div(wanted, per_dev)
        member = lax.rem(wanted, per_dev)

        @pl.loop(0, chunks)
        def _(chunk):
            for u in range(variables):
                value = ALLP[group, member, u, chunk]
                for q in range(TILE):
                    ROUTED[chunk * TILE + q, k, u : u + 1, :] = value[q : q + 1, :]

    def a2a(j):
        return remote(
            ROUTED.at[(me + j) % n_space], ARR.at[me], q_s.at[j], q_r.at[j],
            space=(me + j) % n_space,
        )

    @pl.loop(1, n_space)
    def _(j):
        a2a(j).start()

    ARR[me] = ROUTED[me]
    halos_wait(1)
    arrived(fs_high, linked)

    @pl.when(has_above)
    def _():
        halo_face(1).start()

    def order(n):
        return (n + nb // 2 + 1) % nb

    @pl.loop(0, nb)
    def _(t):
        @pl.when(t == nb // 2 - 1)
        def _():
            arrived(fs_low, linked)

            @pl.when(has_below)
            def _():
                halo_face(1).wait_recv()

        b = order(t)
        row = pl.multiple_of(b * TILE, TILE)
        here = pl.ds(row, TILE)
        mid = pl.ds(row + TILE, TILE)
        found = spectral(lambda r, u: Y[r, u, mid, :], row)
        for u, (q, p) in enumerate(found):
            for r in range(CHIP):
                RT[CHIP + r, u, here, :] = p[r] - q[r]
        for base in range(CHIP, instances, GROUP):
            span = range(base, base + GROUP)
            acc = {(r, u): RT[r, u, here, :] for r in span for u in range(variables)}
            acc = coupling(acc, span, Y, row, 1)
            for r in span:
                for u in range(variables):
                    RT[r, u, here, :] = acc[r, u]
        r_copy(0, b, odd).start()
        r_copy(1, b, odd).start()

    half_table(target_line, 0)

    @pl.loop(1, n_space)
    def _(j):
        remote(
            ROUTED.at[0], ARR.at[(me + n_space - j) % n_space], q_s.at[j], q_r.at[j],
            space=(me + j) % n_space,
        ).wait_recv()

    if chunks > 1:
        PT[...] = zeros(instances, variables, rows, cols)

    @pl.loop(0, chunks)
    def _(chunk):
        if chunks > 1:
            half_table(target_line, chunk)

        @pl.loop(0, instances)
        def _(r):
            k = (r + instances - mine) % instances
            for p in range(TILE):
                hit = sub_r == lax.shift_right_logical(target_line(chunk * TILE + p), shift_bits)
                parts = split_parts(ARR[chunk * TILE + p, k])
                for n, part in enumerate(parts):
                    for u in range(variables):
                        begin = (n * variables + u) * rows
                        LHS[begin : begin + rows, p * slots : (p + 1) * slots] = jnp.where(
                            hit, part[u : u + 1, :].astype(jnp.float32), 0.0
                        ).astype(jnp.bfloat16)
            terms = lax.dot_general(
                LHS[...], COL[0:cols, :], (((1,), (1,)), ((), ())),
                preferred_element_type=jnp.float32,
            )
            height = variables * rows
            summed = terms[:height]
            for part in range(1, PARTS):
                summed = summed + terms[part * height : (part + 1) * height]
            summed = summed.reshape(variables, rows, cols)
            if chunks > 1:
                summed = summed + PT[r]
            PT[r] = summed

    halos_sent(1)

    @pl.loop(0, nb)
    def _(b):
        row = pl.multiple_of(b * TILE, TILE)
        here = pl.ds(row, TILE)
        mid = pl.ds(row + TILE, TILE)
        for r in range(instances):
            line = [PT[r, v, here, :] for v in range(variables)]
            for u in range(variables):
                Y[r, u, mid, :] = Y[r, u, mid, :] - inverse(line, r, u, here)
                if r < CHIP:
                    ST[r, u, here, :] = ST[r, u, here, :] - line[u]

    halos_start(2)
    pack(2, Y, 0)
    halos_wait(2)

    @pl.loop(0, nb)
    def _(b):
        row = pl.multiple_of(b * TILE, TILE)
        here = pl.ds(row, TILE)
        mid = pl.ds(row + TILE, TILE)
        found = spectral(lambda r, u: Y[r, u, mid, :], row)
        for u, (q, p) in enumerate(found):
            for r in range(CHIP):
                RT[r, u, here, :] = ST[r, u, here, :] - (q[r] + p[r])
        for base in range(0, CHIP, GROUP):
            span = range(base, base + GROUP)
            acc = {(r, u): RT[r, u, here, :] for r in span for u in range(variables)}
            acc = coupling(acc, span, Y, row, 2)
            for r in span:
                for u in range(variables):
                    RT[r, u, here, :] = acc[r, u]
        r_copy(2, b, odd).start()
        r_own(b).start()

    @pl.loop(0, nb)
    def _(t):
        b = order(t)
        here = pl.ds(pl.multiple_of(b * TILE, TILE), TILE)
        r_own(b).wait()
        r_copy(2, b, 1 - odd).wait_recv()
        r_copy(0, b, odd).wait_recv()
        r_copy(1, b, 1 - odd).wait_recv()
        for k in range(per_dev):
            scale = DH[k, here, :]
            rest = [NEAR[k, v, here, :] + FAR[k, v, here, :] for v in range(variables)]
            for u in range(variables):
                out_r[k, u, here, :] = rest[u]
                new = dinv[u, k, 0] * rest[0]
                for v in range(1, variables):
                    new = new + dinv[u, k, v] * rest[v]
                out_a[k, u, here, :] = scale * new

    for copy in (ds_copy, dv_copy, fp_copy, fs_low, fs_high):
        sent(copy)
    for n in range(2):
        incoming(n, 1 - odd, mine).wait_send()

    p_x.wait_send()
    p_sib.wait_send()
    p_rel.wait_send()

    @pl.loop(1, n_space)
    def _(j):
        a2a(j).wait_send()

    @pl.when(has_above)
    def _():
        halo_face(0).wait_send()
        halo_face(1).wait_send()

    halos_sent(0)
    halos_sent(2)

    @pl.loop(0, nb)
    def _(b):
        for kind in range(3):
            r_copy(kind, b, odd).wait_send()


def finish(a, r, out_a, out_r, sems):
    copies = [
        pltpu.make_async_copy(a, out_a, sems.at[0]),
        pltpu.make_async_copy(r, out_r, sems.at[1]),
    ]
    for copy in copies:
        copy.start()
    for copy in copies:
        copy.wait()


def body(n_space, n_inst, a, s, fs, fp, ds, vol, blocks, dinv, *rest):
    per_dev, variables, rows, width = a.shape
    slots = rest[3].shape[2]
    nb = rows // TILE
    chunks = n_space // TILE
    instances = n_inst * per_dev
    cols = width // 2
    f32 = jnp.float32
    hbm = pl.BlockSpec(memory_space=pl.ANY)
    vmem = pl.BlockSpec(memory_space=pltpu.VMEM)
    dma = pltpu.SemaphoreType.DMA
    field = (per_dev, variables, rows, width)
    out = jax.ShapeDtypeStruct(field, f32)
    blocks = jnp.transpose(blocks, (1, 0, 2))
    dinv = jnp.transpose(dinv, (1, 0, 2))
    placed = pltpu.VMEM(field, f32)
    new, r = pl.pallas_call(
        functools.partial(kernel, n_space, n_inst),
        out_shape=(placed, placed),
        in_specs=[hbm] * 15,
        out_specs=(vmem, vmem),
        scratch_shapes=[
            pltpu.SMEM(blocks.shape, f32),
            pltpu.SMEM(dinv.shape, f32),
            pltpu.SMEM(rest[0].shape, f32),
            pltpu.SMEM(rest[1].shape, f32),
            pltpu.SMEM(rest[2].shape, jnp.int32),
            pltpu.VMEM(rest[3].shape, jnp.int32),
            pltpu.VMEM(rest[4].shape, jnp.int32),
            pltpu.VMEM(rest[5].shape, f32),
            pltpu.SMEM(rest[6].shape, jnp.int32),
            pltpu.VMEM(field, f32),
            pltpu.VMEM((CHIP, variables, rows + 2 * TILE, cols), f32),
            pltpu.VMEM((CHIP, variables, rows, cols), f32),
            pltpu.VMEM((instances, variables, rows + 2 * TILE, cols), f32),
            pltpu.VMEM((instances, variables, rows, cols), f32),
            pltpu.VMEM((instances, variables, rows, cols), f32),
            pltpu.VMEM(field, f32),
            pltpu.VMEM(field, f32),
            pltpu.VMEM((instances, rows + TILE, cols), f32),
            pltpu.VMEM((instances, rows, cols), f32),
            pltpu.VMEM((instances, rows, cols), f32),
            pltpu.VMEM((rows, cols), f32),
            pltpu.VMEM((per_dev, rows, width), f32),
            pltpu.VMEM((3, rows, LANES), f32),
            pltpu.VMEM((3, rows, LANES), f32),
            pltpu.VMEM((3, rows, LANES), f32),
            pltpu.VMEM((3, rows, LANES), f32),
            pltpu.VMEM((n_inst, TILE, LANES), f32),
            pltpu.VMEM((instances * variables * variables, TILE, LANES), f32),
            pltpu.VMEM((width, TILE * slots), jnp.bfloat16),
            pltpu.VMEM((per_dev, variables, chunks, TILE, slots), f32),
            pltpu.VMEM((4, per_dev, variables, chunks, TILE, slots), f32),
            pltpu.VMEM((n_space, instances, variables, slots), f32),
            pltpu.VMEM((n_space, instances, variables, slots), f32),
            pltpu.VMEM((PARTS * variables * rows, TILE * slots), jnp.bfloat16),
            dma((17,)),
            dma((nb,)),
            dma((2,)),
            dma((2,)),
            dma((3, 5)),
            dma((3, 5)),
            dma((3, nb)),
            dma((3, nb)),
            dma((3,)),
            dma((3,)),
            dma((8,)),
            dma((8,)),
            dma((3,)),
            dma((3,)),
            dma((n_space,)),
            dma((n_space,)),
            pltpu.SemaphoreType.REGULAR((2,)),
        ],
        compiler_params=pltpu.CompilerParams(
            collective_id=0, has_side_effects=True, vmem_limit_bytes=56 * 1024 * 1024
        ),
    )(a, s, fs, fp, ds, vol, blocks, dinv, *rest)
    return pl.pallas_call(
        finish,
        out_shape=(out, out),
        in_specs=[vmem, vmem],
        out_specs=(hbm, hbm),
        scratch_shapes=[dma((2,))],
    )(*(pltpu.with_memory_space_constraint(x, pltpu.VMEM) for x in (new, r)))


def solution(mesh):
    in_specs = (
        P("inst", None, "space", None),
        P("inst", None, "space", None),
        P("inst", "space", None),
        P("inst", "space", None),
        P("inst", "space", None),
        P("space", None),
        P(),
        P("inst", None, None),
        P(),
        P(),
        P(),
        P("space", None, None),
        P(None, "space", None),
        P("space", None, None),
        P("space", None),
    )
    out_specs = (P("inst", None, "space", None), P("inst", None, "space", None))
    return jax.shard_map(
        functools.partial(body, mesh.shape["space"], mesh.shape["inst"]),
        mesh=mesh,
        in_specs=in_specs,
        out_specs=out_specs,
        check_vma=False,
    )
```

```python
import functools
import math

import jax
import jax.numpy as jnp
from jax import lax
from jax.experimental import pallas as pl
from jax.experimental.pallas import tpu as pltpu
from jax.sharding import PartitionSpec as P

SWEEPS = 2
TILE = 8
LANES = 128
PARTS = 2
CHIP = 4
GROUP = 2
MESH = pl.DeviceIdType.MESH


def spectral_entry(offset, count):
    offset = offset % count
    if offset == 0 or 2 * offset == count:
        return 0.0
    return 0.5 * (-1.0) ** offset / math.tan(math.pi * offset / count)


def split_parts(value):
    parts = []
    for _ in range(PARTS):
        part = value.astype(jnp.bfloat16)
        parts.append(part)
        value = value - part.astype(jnp.float32)
    return parts


def kernel(
    n_space,
    n_inst,
    a_hbm,
    s_hbm,
    fs_hbm,
    fp_hbm,
    ds_hbm,
    vol_hbm,
    blocks_hbm,
    dinv_hbm,
    pblock_hbm,
    freq_hbm,
    shift_hbm,
    cells_hbm,
    targets_hbm,
    weights_hbm,
    counts_hbm,
    out_a,
    out_r,
    blocks,
    dinv,
    pblock,
    freq,
    shift,
    cells,
    targets,
    weights,
    counts,
    A,
    AT,
    ST,
    Y,
    RT,
    PT,
    NEAR,
    FAR,
    FS,
    FP,
    DS,
    VOL,
    DH,
    CL,
    CR,
    PW,
    PF,
    DV,
    DT,
    COL,
    PICK,
    ALLP,
    ROUTED,
    ARR,
    LHS,
    load_sem,
    own_r,
    in_s,
    in_r,
    c_s,
    c_r,
    r_s,
    r_r,
    cols_s,
    cols_r,
    hs,
    hr,
    ps,
    pr,
    q_s,
    q_r,
    token,
):
    per_dev, variables, rows, width = a_hbm.shape
    instances = n_inst * per_dev
    cols = width // 2
    slots = cells.shape[2]
    nb = rows // TILE
    part_rows = rows // 2
    inst = lax.axis_index("inst")
    me = lax.axis_index("space")
    odd = inst % 2
    sibling = inst + 1 - 2 * odd
    across = (inst + 2) % n_inst
    diagonal = (sibling + 2) % n_inst
    shift_bits = width.bit_length() - 1
    peers = (across, diagonal, sibling)
    mine = 2 * odd
    other = 2 - 2 * odd
    seats = (4 + mine, 4 + other, other)

    def remote(src, dst, send, recv, **device):
        return pltpu.make_async_remote_copy(
            src_ref=src, dst_ref=dst, send_sem=send, recv_sem=recv, device_id=device,
            device_id_type=MESH,
        )

    def half(c):
        return pl.ds(pl.multiple_of(c * cols, cols), cols)

    def pair(seat):
        return pl.ds(seat, per_dev)

    def local(src, dst, n):
        return pltpu.make_async_copy(src, dst, load_sem.at[n])

    inner = pl.ds(TILE, rows)
    here_cols = half(odd)
    loads = [
        local(a_hbm, A, 0),
        local(s_hbm.at[:, :, :, here_cols], ST.at[pair(mine)], 1),
        local(a_hbm.at[:, :, :, here_cols], AT.at[pair(mine), :, inner, :], 2),
        local(fp_hbm.at[:, :, here_cols], FP.at[pair(mine)], 3),
        local(fs_hbm.at[:, :, here_cols], FS.at[pair(mine), inner, :], 4),
        local(ds_hbm.at[:, :, here_cols], DS.at[pair(mine)], 5),
        local(vol_hbm.at[:, here_cols], VOL, 6),
        local(ds_hbm, DH, 7),
    ]
    tables = [
        local(dinv_hbm, dinv, 8),
        local(cells_hbm, cells, 9),
        local(counts_hbm, counts, 10),
        local(weights_hbm, weights, 11),
        local(pblock_hbm, pblock, 12),
        local(shift_hbm, shift, 13),
        local(targets_hbm, targets, 14),
        local(blocks_hbm, blocks, 15),
        local(freq_hbm, freq, 16),
    ]

    barrier = pltpu.get_barrier_semaphore()
    for peer in peers:
        pl.semaphore_signal(barrier, inc=1, device_id={"inst": peer}, device_id_type=MESH)

    has_hi = me < n_space - 2
    has_lo = me > 1
    hi = (me + 2) % n_space
    lo = (me + n_space - 2) % n_space
    partner = me + 1 - 2 * (me % 2)

    def greet(semaphore, device):
        pl.semaphore_signal(
            semaphore, inc=1, device_id={"space": device}, device_id_type=MESH
        )

    greet(barrier, partner)

    @pl.when(has_hi)
    def _():
        greet(barrier, hi)

    @pl.when(has_lo)
    def _():
        greet(barrier, lo)

    for copy in loads[:1] + tables + loads[1:]:
        copy.start()

    def incoming(n, target, seat):
        if n == 0:
            src, dst = a_hbm, AT.at[pair(seat), :, inner, :]
        else:
            src, dst = s_hbm, ST.at[pair(seat)]
        return remote(
            src.at[:, :, :, half(target)], dst, in_s.at[n], in_r.at[n], inst=sibling
        )

    def seat_there(kind):
        return mine + (4 if kind < 2 else 0)

    def target_half(kind):
        return odd if kind == 0 else 1 - odd

    def share(which, part):
        begin = part * part_rows
        span = pl.ds(begin, part_rows)
        src, dst, land = (
            (ds_hbm, DS, span),
            (fp_hbm, FP, span),
            (fs_hbm, FS, pl.ds(begin + TILE, part_rows)),
        )[which]
        n = 2 * which + part

        def make(kind, column, seat):
            return remote(
                src.at[:, span, half(column)], dst.at[pair(seat), land, :],
                c_s.at[kind, n], c_r.at[kind, n], inst=peers[kind],
            )

        return make

    def dv_copy(kind, column, seat):
        return remote(
            DV.at[0], DV.at[kind + 1], c_s.at[kind, 6], c_r.at[kind, 6], inst=peers[kind]
        )

    lower, upper = ([share(which, part) for which in range(3)] for part in range(2))
    linked, beside = (0, 1), (2,)

    def start(copy, kinds=(0, 1, 2)):
        for kind in kinds:
            copy(kind, target_half(kind), seat_there(kind)).start()

    def arrived(copy, kinds=(0, 1, 2)):
        for kind in kinds:
            copy(kind, odd, seats[kind]).wait_recv()

    def sent(copy, kinds=(0, 1, 2)):
        for kind in kinds:
            copy(kind, target_half(kind), seat_there(kind)).wait_send()

    def r_copy(kind, b, column):
        row = pl.multiple_of(b * TILE, TILE)
        land = FAR if kind < 2 else NEAR
        return remote(
            RT.at[pair(seats[kind]), :, pl.ds(row, TILE), :],
            land.at[:, :, pl.ds(row, TILE), half(column)],
            r_s.at[kind, b], r_r.at[kind, b], inst=peers[kind],
        )

    def r_own(b):
        row = pl.multiple_of(b * TILE, TILE)
        return pltpu.make_async_copy(
            RT.at[pair(mine), :, pl.ds(row, TILE), :],
            NEAR.at[:, :, pl.ds(row, TILE), here_cols], own_r.at[b],
        )

    has_above = me < n_space - 1
    has_below = me > 0
    above = (me + 1) % n_space
    below = (me + n_space - 1) % n_space
    field_of = (AT, Y.at[pl.ds(CHIP, CHIP)], Y.at[pl.ds(0, CHIP)])

    def halo_up(stage):
        ref = field_of[stage]
        return remote(
            ref.at[:, :, pl.ds(rows + TILE - 1, 1), :], ref.at[:, :, pl.ds(TILE - 1, 1), :],
            hs.at[2 * stage], hr.at[2 * stage], space=above,
        )

    def halo_down(stage):
        ref = field_of[stage]
        return remote(
            ref.at[:, :, pl.ds(TILE, 1), :], ref.at[:, :, pl.ds(rows + TILE, 1), :],
            hs.at[2 * stage + 1], hr.at[2 * stage + 1], space=below,
        )

    def halo_face(side):
        group = pl.ds(side * CHIP, CHIP)
        return remote(
            FS.at[group, pl.ds(rows + TILE - 1, 1), :], FS.at[group, pl.ds(TILE - 1, 1), :],
            hs.at[6 + side], hr.at[6 + side], space=above,
        )

    def col_copies(stage, span, n):
        return (
            remote(
                PW.at[stage, span], CL.at[stage, span], cols_s.at[n], cols_r.at[n], inst=sibling
            ),
            remote(
                PF.at[stage, span], CR.at[stage, span], cols_s.at[n], cols_r.at[n], inst=sibling
            ),
        )

    def col_do(way, stage, span, n):
        to_right, to_left = col_copies(stage, span, n)
        is_left = odd == 0
        if way == "receive":
            is_left = odd == 1

        @pl.when(is_left)
        def _():
            act(way, to_right)

        @pl.when(jnp.logical_not(is_left))
        def _():
            act(way, to_left)

    def act(way, copy):
        if way == "start":
            copy.start()
        elif way == "receive":
            copy.wait_recv()
        else:
            copy.wait_send()

    def rows_do(way, stage):
        up, down = has_above, has_below
        if way == "receive":
            up, down = has_below, has_above

        @pl.when(up)
        def _():
            act(way, halo_up(stage))

        @pl.when(down)
        def _():
            act(way, halo_down(stage))

    def zeros(*shape):
        return jnp.zeros(shape, jnp.float32)

    @pl.when(me == 0)
    def _():
        FS[:, 0:TILE, :] = zeros(instances, TILE, cols)
        AT[:, :, 0:TILE, :] = zeros(CHIP, variables, TILE, cols)
        Y[:, :, 0:TILE, :] = zeros(instances, variables, TILE, cols)

    @pl.when(me == n_space - 1)
    def _():
        AT[:, :, rows + TILE : rows + 2 * TILE, :] = zeros(CHIP, variables, TILE, cols)
        Y[:, :, rows + TILE : rows + 2 * TILE, :] = zeros(instances, variables, TILE, cols)

    @pl.when(odd == 0)
    def _():
        CL[...] = zeros(3, rows, LANES)

    @pl.when(odd == 1)
    def _():
        CR[...] = zeros(3, rows, LANES)

    sub8 = lax.broadcasted_iota(jnp.int32, (TILE, cols), 0)
    lane8 = lax.broadcasted_iota(jnp.int32, (TILE, cols), 1)
    lane1 = lax.broadcasted_iota(jnp.int32, (TILE, LANES), 1)

    pl.semaphore_wait(barrier, n_inst + has_hi.astype(jnp.int32) + has_lo.astype(jnp.int32))

    for copy in upper:
        start(copy, linked)
    incoming(0, 1 - odd, mine).start()
    for copy in upper + lower:
        start(copy, beside)
    incoming(1, 1 - odd, mine).start()

    tables[0].wait()
    packed = zeros(TILE, LANES)
    for k in range(per_dev):
        for u in range(variables):
            for v in range(variables):
                n = (k * variables + u) * variables + v
                packed = jnp.where(lane1 == n, dinv[u, k, v], packed)
    DV[0] = packed
    start(dv_copy)

    @pl.when(jnp.logical_not(has_hi))
    def _():
        greet(token.at[0], lo)

    @pl.when(jnp.logical_not(has_lo))
    def _():
        greet(token.at[1], hi)

    sub_w = lax.broadcasted_iota(jnp.int32, (width, slots), 0)
    sub_h = lax.broadcasted_iota(jnp.int32, (cols, slots), 0)
    sub_r = lax.broadcasted_iota(jnp.int32, (rows, slots), 0)

    def column_table(index, chunk):
        for q in range(TILE):
            line = index(chunk * TILE + q)
            column = jnp.bitwise_and(line, width - 1)
            hot = jnp.where(sub_w == column, 1.0, 0.0).astype(jnp.bfloat16)
            COL[:, q * slots : (q + 1) * slots] = hot

    def half_table(index, chunk):
        for q in range(TILE):
            line = index(chunk * TILE + q)
            column = jnp.bitwise_and(line, width - 1) - odd * cols
            hot = jnp.where(sub_h == column, 1.0, 0.0).astype(jnp.bfloat16)
            COL[0:cols, q * slots : (q + 1) * slots] = hot

    def cell_line(q):
        return cells[0, pl.ds(q, 1), :]

    def target_line(p):
        return targets[p, 0:1, :]

    chunks = n_space // TILE

    loads[0].wait()
    for copy in tables[1:]:
        copy.wait()

    @pl.loop(0, chunks)
    def _(chunk):
        column_table(cell_line, chunk)

        @pl.loop(0, per_dev)
        def _(k):
            field = A[k].reshape(variables * rows, width)
            stacked = jnp.concatenate(split_parts(field), axis=0)
            terms = jnp.dot(stacked, COL[...], preferred_element_type=jnp.float32)
            height = variables * rows
            found = terms[:height]
            for part in range(1, PARTS):
                found = found + terms[part * height : (part + 1) * height]
            for q in range(TILE):
                hit = sub_r == lax.shift_right_logical(cell_line(chunk * TILE + q), shift_bits)
                for v in range(variables):
                    piece = found[v * rows : (v + 1) * rows, q * slots : (q + 1) * slots]
                    PICK[k, v, chunk, q : q + 1, :] = jnp.sum(
                        jnp.where(hit, piece, 0.0), axis=0, keepdims=True
                    )

        lane = lax.broadcasted_iota(jnp.int32, (TILE, slots), 1)
        sub = lax.broadcasted_iota(jnp.int32, (TILE, slots), 0)
        limit = jnp.zeros((TILE, slots), jnp.int32)
        for q in range(TILE):
            limit = jnp.where(sub == q, counts[0, chunk * TILE + q], limit)
        first = pl.multiple_of(chunk * TILE, TILE)
        weight = jnp.where(lane < limit, weights[0, pl.ds(first, TILE), :], 0.0)

        for k in range(per_dev):
            picked = [PICK[k, v, chunk] for v in range(variables)]
            for u in range(variables):
                mixed = pblock[0, u] * picked[0]
                for v in range(1, variables):
                    mixed = mixed + pblock[v, u] * picked[v]
                ALLP[0, k, u, chunk] = mixed * weight

    p_x = remote(ALLP.at[0], ALLP.at[2], ps.at[0], pr.at[0], inst=across)
    p_sib = remote(ALLP.at[0], ALLP.at[3 - 2 * odd], ps.at[1], pr.at[1 + odd], inst=sibling)
    p_rel = remote(ALLP.at[2], ALLP.at[1 + 2 * odd], ps.at[2], pr.at[2 - odd], inst=sibling)
    p_sib_in = remote(ALLP.at[0], ALLP.at[1 + 2 * odd], ps.at[1], pr.at[2 - odd], inst=sibling)
    p_rel_in = remote(ALLP.at[2], ALLP.at[3 - 2 * odd], ps.at[2], pr.at[1 + odd], inst=sibling)
    p_x.start()
    p_sib.start()
    for copy in lower:
        start(copy, linked)

    @pl.when(has_hi)
    def _():
        pl.semaphore_wait(token.at[0], 1)

        @pl.when(has_lo)
        def _():
            greet(token.at[0], lo)

    @pl.when(has_lo)
    def _():
        pl.semaphore_wait(token.at[1], 1)

        @pl.when(has_hi)
        def _():
            greet(token.at[1], hi)

    for copy in loads[1:]:
        copy.wait()
    for n in range(2):
        incoming(n, odd, other).wait_recv()
    for copy in upper + lower:
        arrived(copy, beside)
    rows_do("start", 0)

    @pl.when(has_above)
    def _():
        halo_face(0).start()

    def wide(tile):
        return jnp.concatenate([tile] * (cols // LANES), axis=1)

    whole = pl.ds(0, rows)

    def pack(stage, ref, base, row):
        here = pl.ds(row, TILE)
        mid = pl.ds(row + TILE, TILE)
        last = zeros(TILE, LANES)
        first = zeros(TILE, LANES)
        for r in range(CHIP):
            fp = FP[base + r, here, cols - LANES : cols]
            for v in range(variables):
                n = r * variables + v
                a = ref[base + r, v, mid, 0:LANES]
                w = fp * ref[base + r, v, mid, cols - LANES : cols]
                first = jnp.where(lane1 == n, pltpu.roll(a, n, 1) if n else a, first)
                last = jnp.where(lane1 == n, pltpu.roll(w, n + 1, 1), last)
        PW[stage, here, :] = last
        PF[stage, here, :] = first

    @pl.loop(0, nb)
    def _(b):
        pack(0, AT, 0, pl.multiple_of(b * TILE, TILE))

    col_do("start", 0, whole, nb)

    arrived(dv_copy)
    for position in range(instances):
        if position < CHIP:
            kind = jnp.where(odd == position // per_dev, 0, 3)
        else:
            kind = jnp.where(odd == (position - CHIP) // per_dev, 1, 2)
        vector = DV[kind]
        for n in range(variables * variables):
            lane = (position % per_dev) * variables * variables + n
            DT[position * variables * variables + n] = jnp.broadcast_to(
                vector[:, lane : lane + 1], (TILE, LANES)
            )

    for copy in upper:
        arrived(copy, linked)

    @pl.when(has_above)
    def _():
        halo_face(1).start()

    f1, f2, f3 = (spectral_entry(d, instances) for d in (1, 2, 3))

    def spectral(a, row):
        here = pl.ds(row, TILE)
        scaled = freq[0] * VOL[here, :]
        v1 = (0.5 * (f1 - f3)) * scaled
        v2 = f2 * scaled
        v3 = (0.5 * (f1 + f3)) * scaled
        results = []
        for u in range(variables):
            near = [a(r, u) for r in range(4)]
            far = [a(r, u) for r in range(4, 8)]
            b = [m if f is None else m - f for m, f in zip(near, far)]
            c = [m if f is None else m + f for m, f in zip(near, far)]
            even = v1 * (c[1] - c[3])
            odds = v1 * (c[2] - c[0])
            q = [even, odds, -even, -odds]
            p = [
                v2 * b[2] + v3 * (b[1] + b[3]),
                v2 * b[3] + v3 * (b[2] - b[0]),
                v3 * (b[3] - b[1]) - v2 * b[0],
                -(v2 * b[1] + v3 * (b[0] + b[2])),
            ]
            results.append((q, p))
        return results

    def coupling(acc, span, ref, row, stage):
        here = pl.ds(row, TILE)
        mid = pl.ds(row + TILE, TILE)
        low = pl.ds(row, TILE)
        high = pl.ds(row + 2 * TILE, TILE)
        top = sub8 == TILE - 1
        bottom = sub8 == 0
        fm = {r: FS[r, mid, :] for r in span}
        fl = {r: jnp.where(top, FS[r, low, :], fm[r]) for r in span}
        fp = {r: FP[r, here, :] for r in span}
        cl = CL[stage, here, :]
        cr = CR[stage, here, :]
        for v in range(variables):
            terms = {}
            for r in span:
                n = (r % CHIP) * variables + v
                a = ref[r, v, mid, :]
                x = pltpu.roll(fl[r] * jnp.where(top, ref[r, v, low, :], a), 1, 0)
                y = fm[r] * pltpu.roll(
                    jnp.where(bottom, ref[r, v, high, :], a), TILE - 1, 0
                )
                edge = wide(pltpu.roll(cl, LANES - n, 1) if n else cl)
                left = jnp.where(lane8 == 0, edge, pltpu.roll(fp[r] * a, 1, 1))
                edge = wide(pltpu.roll(cr, LANES - 1 - n, 1))
                right = fp[r] * jnp.where(
                    lane8 == cols - 1, edge, pltpu.roll(a, cols - 1, 1)
                )
                terms[r] = (x, y, left, right)
            for u in range(variables):
                k0, k1, k2, k3 = (blocks[v, n, u] for n in range(4))
                for r in span:
                    x, y, left, right = terms[r]
                    acc[r, u] = acc[r, u] - ((k0 * x + k1 * y) + (k2 * left + k3 * right))
        return acc

    def inverse(acc, r, u, here):
        n = (r * variables + u) * variables
        new = wide(DT[n]) * acc[0]
        for v in range(1, variables):
            new = new + wide(DT[n + v]) * acc[v]
        return DS[r, here, :] * new

    rows_do("receive", 0)
    col_do("receive", 0, whole, nb)

    @pl.when(has_below)
    def _():
        halo_face(0).wait_recv()

    middle = nb // 2

    def sweep(b):
        row = pl.multiple_of(b * TILE, TILE)
        here = pl.ds(row, TILE)
        mid = pl.ds(row + TILE, TILE)
        found = spectral(lambda r, u: AT[r, u, mid, :] if r < CHIP else None, row)
        for u, (q, p) in enumerate(found):
            for r in range(CHIP):
                RT[r, u, here, :] = ST[r, u, here, :] - (q[r] + p[r])
                RT[CHIP + r, u, here, :] = p[r] - q[r]
        for base in range(0, instances, GROUP):
            span = range(base, base + GROUP)
            acc = {(r, u): RT[r, u, here, :] for r in span for u in range(variables)}
            if base < CHIP:
                acc = coupling(acc, span, AT, row, 0)
            for r in span:
                line = [acc[r, v] for v in range(variables)]
                for u in range(variables):
                    Y[r, u, mid, :] = inverse(line, r, u, here)
        pack(1, Y, CHIP, row)
        col_do("start", 1, here, b)

    def export(b):
        row = pl.multiple_of(b * TILE, TILE)
        here = pl.ds(row, TILE)
        mid = pl.ds(row + TILE, TILE)
        col_do("receive", 1, here, b)
        found = spectral(lambda r, u: Y[r, u, mid, :], row)
        for u, (q, p) in enumerate(found):
            for r in range(CHIP):
                RT[CHIP + r, u, here, :] = p[r] - q[r]
        for base in range(CHIP, instances, GROUP):
            span = range(base, base + GROUP)
            acc = {(r, u): RT[r, u, here, :] for r in span for u in range(variables)}
            acc = coupling(acc, span, Y, row, 1)
            for r in span:
                for u in range(variables):
                    RT[r, u, here, :] = acc[r, u]
        r_copy(0, b, odd).start()
        r_copy(1, b, odd).start()

    def order(t):
        early = (t < middle - 2).astype(jnp.int32)
        late = (t >= nb - 2).astype(jnp.int32)
        between = (1 - early) * (1 - late)
        return (
            early * (t + middle + 1)
            + between * (t - middle + 3)
            + late * (nb - 1 - t) * (nb - 1)
        )

    @pl.loop(0, nb + 4)
    def _(n):
        @pl.when(n < nb)
        def _():
            @pl.when(n == middle)
            def _():
                for copy in lower:
                    arrived(copy, linked)

            sweep((n + middle) % nb)

        @pl.when(n == middle)
        def _():
            rows_do("start", 1)

        @pl.when(n == nb + 2)
        def _():
            rows_do("receive", 1)

            @pl.when(has_below)
            def _():
                halo_face(1).wait_recv()

        @pl.when((n >= 2) & (n < middle))
        def _():
            export(order(n - 2))

        @pl.when(n >= middle + 2)
        def _():
            export(order(n - 4))

    p_x.wait_recv()
    p_rel.start()
    p_sib_in.wait_recv()
    p_rel_in.wait_recv()

    @pl.loop(0, instances)
    def _(k):
        wanted = lax.rem(k - shift[0] + 2 * instances, instances)
        group = lax.div(wanted, per_dev)
        member = lax.rem(wanted, per_dev)

        @pl.loop(0, chunks)
        def _(chunk):
            for u in range(variables):
                value = ALLP[group, member, u, chunk]
                for q in range(TILE):
                    ROUTED[chunk * TILE + q, k, u : u + 1, :] = value[q : q + 1, :]

    def a2a(j):
        return remote(
            ROUTED.at[(me + j) % n_space], ARR.at[me], q_s.at[j], q_r.at[j],
            space=(me + j) % n_space,
        )

    @pl.loop(1, n_space)
    def _(j):
        a2a(j).start()

    ARR[me] = ROUTED[me]

    half_table(target_line, 0)

    @pl.loop(1, n_space)
    def _(j):
        remote(
            ROUTED.at[0], ARR.at[(me + n_space - j) % n_space], q_s.at[j], q_r.at[j],
            space=(me + j) % n_space,
        ).wait_recv()

    if chunks > 1:
        PT[...] = zeros(instances, variables, rows, cols)

    @pl.loop(0, chunks)
    def _(chunk):
        if chunks > 1:
            half_table(target_line, chunk)

        @pl.loop(0, instances)
        def _(r):
            k = (r + instances - mine) % instances
            for p in range(TILE):
                hit = sub_r == lax.shift_right_logical(target_line(chunk * TILE + p), shift_bits)
                parts = split_parts(ARR[chunk * TILE + p, k])
                for n, part in enumerate(parts):
                    for u in range(variables):
                        begin = (n * variables + u) * rows
                        LHS[begin : begin + rows, p * slots : (p + 1) * slots] = jnp.where(
                            hit, part[u : u + 1, :].astype(jnp.float32), 0.0
                        ).astype(jnp.bfloat16)
            terms = lax.dot_general(
                LHS[...], COL[0:cols, :], (((1,), (1,)), ((), ())),
                preferred_element_type=jnp.float32,
            )
            height = variables * rows
            summed = terms[:height]
            for part in range(1, PARTS):
                summed = summed + terms[part * height : (part + 1) * height]
            summed = summed.reshape(variables, rows, cols)
            if chunks > 1:
                summed = summed + PT[r]
            PT[r] = summed

    rows_do("sent", 1)

    @pl.loop(0, nb)
    def _(b):
        row = pl.multiple_of(b * TILE, TILE)
        here = pl.ds(row, TILE)
        mid = pl.ds(row + TILE, TILE)
        for r in range(instances):
            line = [PT[r, v, here, :] for v in range(variables)]
            for u in range(variables):
                Y[r, u, mid, :] = Y[r, u, mid, :] - inverse(line, r, u, here)
                if r < CHIP:
                    ST[r, u, here, :] = ST[r, u, here, :] - line[u]

    rows_do("start", 2)

    @pl.loop(0, nb)
    def _(b):
        pack(2, Y, 0, pl.multiple_of(b * TILE, TILE))

    col_do("start", 2, whole, nb + 1)
    rows_do("receive", 2)
    col_do("receive", 2, whole, nb + 1)

    @pl.loop(0, nb)
    def _(b):
        row = pl.multiple_of(b * TILE, TILE)
        here = pl.ds(row, TILE)
        mid = pl.ds(row + TILE, TILE)
        found = spectral(lambda r, u: Y[r, u, mid, :], row)
        for u, (q, p) in enumerate(found):
            for r in range(CHIP):
                RT[r, u, here, :] = ST[r, u, here, :] - (q[r] + p[r])
        for base in range(0, CHIP, GROUP):
            span = range(base, base + GROUP)
            acc = {(r, u): RT[r, u, here, :] for r in span for u in range(variables)}
            acc = coupling(acc, span, Y, row, 2)
            for r in span:
                for u in range(variables):
                    RT[r, u, here, :] = acc[r, u]
        r_copy(2, b, odd).start()
        r_own(b).start()

    @pl.loop(0, nb)
    def _(t):
        b = order(t)
        here = pl.ds(pl.multiple_of(b * TILE, TILE), TILE)
        r_own(b).wait()
        r_copy(2, b, 1 - odd).wait_recv()
        r_copy(0, b, odd).wait_recv()
        r_copy(1, b, 1 - odd).wait_recv()
        for k in range(per_dev):
            scale = DH[k, here, :]
            rest = [NEAR[k, v, here, :] + FAR[k, v, here, :] for v in range(variables)]
            for u in range(variables):
                out_r[k, u, here, :] = rest[u]
                new = dinv[u, k, 0] * rest[0]
                for v in range(1, variables):
                    new = new + dinv[u, k, v] * rest[v]
                out_a[k, u, here, :] = scale * new

    for copy in (dv_copy, *upper, *lower):
        sent(copy)
    for n in range(2):
        incoming(n, 1 - odd, mine).wait_send()

    p_x.wait_send()
    p_sib.wait_send()
    p_rel.wait_send()

    @pl.loop(1, n_space)
    def _(j):
        a2a(j).wait_send()

    @pl.when(has_above)
    def _():
        halo_face(0).wait_send()
        halo_face(1).wait_send()

    rows_do("sent", 0)
    rows_do("sent", 2)
    col_do("sent", 0, whole, nb)
    col_do("sent", 2, whole, nb + 1)

    @pl.loop(0, nb)
    def _(b):
        for kind in range(3):
            r_copy(kind, b, odd).wait_send()
        col_do("sent", 1, pl.ds(pl.multiple_of(b * TILE, TILE), TILE), b)


def finish(a, r, out_a, out_r, sems):
    copies = [
        pltpu.make_async_copy(a, out_a, sems.at[0]),
        pltpu.make_async_copy(r, out_r, sems.at[1]),
    ]
    for copy in copies:
        copy.start()
    for copy in copies:
        copy.wait()


def body(n_space, n_inst, a, s, fs, fp, ds, vol, blocks, dinv, *rest):
    per_dev, variables, rows, width = a.shape
    slots = rest[3].shape[2]
    nb = rows // TILE
    chunks = n_space // TILE
    instances = n_inst * per_dev
    cols = width // 2
    f32 = jnp.float32
    hbm = pl.BlockSpec(memory_space=pl.ANY)
    vmem = pl.BlockSpec(memory_space=pltpu.VMEM)
    dma = pltpu.SemaphoreType.DMA
    field = (per_dev, variables, rows, width)
    out = jax.ShapeDtypeStruct(field, f32)
    blocks = jnp.transpose(blocks, (1, 0, 2))
    dinv = jnp.transpose(dinv, (1, 0, 2))
    placed = pltpu.VMEM(field, f32)
    new, r = pl.pallas_call(
        functools.partial(kernel, n_space, n_inst),
        out_shape=(placed, placed),
        in_specs=[hbm] * 15,
        out_specs=(vmem, vmem),
        scratch_shapes=[
            pltpu.SMEM(blocks.shape, f32),
            pltpu.SMEM(dinv.shape, f32),
            pltpu.SMEM(rest[0].shape, f32),
            pltpu.SMEM(rest[1].shape, f32),
            pltpu.SMEM(rest[2].shape, jnp.int32),
            pltpu.VMEM(rest[3].shape, jnp.int32),
            pltpu.VMEM(rest[4].shape, jnp.int32),
            pltpu.VMEM(rest[5].shape, f32),
            pltpu.SMEM(rest[6].shape, jnp.int32),
            pltpu.VMEM(field, f32),
            pltpu.VMEM((CHIP, variables, rows + 2 * TILE, cols), f32),
            pltpu.VMEM((CHIP, variables, rows, cols), f32),
            pltpu.VMEM((instances, variables, rows + 2 * TILE, cols), f32),
            pltpu.VMEM((instances, variables, rows, cols), f32),
            pltpu.VMEM((instances, variables, rows, cols), f32),
            pltpu.VMEM(field, f32),
            pltpu.VMEM(field, f32),
            pltpu.VMEM((instances, rows + TILE, cols), f32),
            pltpu.VMEM((instances, rows, cols), f32),
            pltpu.VMEM((instances, rows, cols), f32),
            pltpu.VMEM((rows, cols), f32),
            pltpu.VMEM((per_dev, rows, width), f32),
            pltpu.VMEM((3, rows, LANES), f32),
            pltpu.VMEM((3, rows, LANES), f32),
            pltpu.VMEM((3, rows, LANES), f32),
            pltpu.VMEM((3, rows, LANES), f32),
            pltpu.VMEM((n_inst, TILE, LANES), f32),
            pltpu.VMEM((instances * variables * variables, TILE, LANES), f32),
            pltpu.VMEM((width, TILE * slots), jnp.bfloat16),
            pltpu.VMEM((per_dev, variables, chunks, TILE, slots), f32),
            pltpu.VMEM((4, per_dev, variables, chunks, TILE, slots), f32),
            pltpu.VMEM((n_space, instances, variables, slots), f32),
            pltpu.VMEM((n_space, instances, variables, slots), f32),
            pltpu.VMEM((PARTS * variables * rows, TILE * slots), jnp.bfloat16),
            dma((17,)),
            dma((nb,)),
            dma((2,)),
            dma((2,)),
            dma((3, 7)),
            dma((3, 7)),
            dma((3, nb)),
            dma((3, nb)),
            dma((nb + 2,)),
            dma((nb + 2,)),
            dma((8,)),
            dma((8,)),
            dma((3,)),
            dma((3,)),
            dma((n_space,)),
            dma((n_space,)),
            pltpu.SemaphoreType.REGULAR((2,)),
        ],
        compiler_params=pltpu.CompilerParams(
            collective_id=0, has_side_effects=True, vmem_limit_bytes=56 * 1024 * 1024
        ),
    )(a, s, fs, fp, ds, vol, blocks, dinv, *rest)
    return pl.pallas_call(
        finish,
        out_shape=(out, out),
        in_specs=[vmem, vmem],
        out_specs=(hbm, hbm),
        scratch_shapes=[dma((2,))],
    )(*(pltpu.with_memory_space_constraint(x, pltpu.VMEM) for x in (new, r)))


def solution(mesh):
    in_specs = (
        P("inst", None, "space", None),
        P("inst", None, "space", None),
        P("inst", "space", None),
        P("inst", "space", None),
        P("inst", "space", None),
        P("space", None),
        P(),
        P("inst", None, None),
        P(),
        P(),
        P(),
        P("space", None, None),
        P(None, "space", None),
        P("space", None, None),
        P("space", None),
    )
    out_specs = (P("inst", None, "space", None), P("inst", None, "space", None))
    return jax.shard_map(
        functools.partial(body, mesh.shape["space"], mesh.shape["inst"]),
        mesh=mesh,
        in_specs=in_specs,
        out_specs=out_specs,
        check_vma=False,
    )
```

```python
import functools
import math

import jax
import jax.numpy as jnp
from jax import lax
from jax.experimental import pallas as pl
from jax.experimental.pallas import tpu as pltpu
from jax.sharding import PartitionSpec as P

SWEEPS = 2
TILE = 8
LANES = 128
PARTS = 2
CHIP = 4
GROUP = 2
MESH = pl.DeviceIdType.MESH


def spectral_entry(offset, count):
    offset = offset % count
    if offset == 0 or 2 * offset == count:
        return 0.0
    return 0.5 * (-1.0) ** offset / math.tan(math.pi * offset / count)


def split_parts(value):
    parts = []
    for _ in range(PARTS):
        part = value.astype(jnp.bfloat16)
        parts.append(part)
        value = value - part.astype(jnp.float32)
    return parts


def kernel(
    n_space,
    n_inst,
    a_hbm,
    s_hbm,
    fs_hbm,
    fp_hbm,
    ds_hbm,
    vol_hbm,
    blocks_hbm,
    dinv_hbm,
    pblock_hbm,
    freq_hbm,
    shift_hbm,
    cells_hbm,
    targets_hbm,
    weights_hbm,
    counts_hbm,
    out_a,
    out_r,
    blocks,
    dinv,
    pblock,
    freq,
    shift,
    cells,
    targets,
    weights,
    counts,
    A,
    AT,
    ST,
    Y,
    RT,
    PT,
    NEAR,
    FAR,
    FS,
    FP,
    DS,
    VOL,
    DH,
    CL,
    CR,
    PW,
    PF,
    DV,
    DT,
    COL,
    PICK,
    ALLP,
    ROUTED,
    ARR,
    LHS,
    load_sem,
    own_r,
    in_s,
    in_r,
    c_s,
    c_r,
    r_s,
    r_r,
    cols_s,
    cols_r,
    hs,
    hr,
    ps,
    pr,
    q_s,
    q_r,
    token,
):
    per_dev, variables, rows, width = a_hbm.shape
    instances = n_inst * per_dev
    cols = width // 2
    slots = cells.shape[2]
    nb = rows // TILE
    part_rows = rows // 2
    inst = lax.axis_index("inst")
    me = lax.axis_index("space")
    odd = inst % 2
    sibling = inst + 1 - 2 * odd
    across = (inst + 2) % n_inst
    diagonal = (sibling + 2) % n_inst
    shift_bits = width.bit_length() - 1
    peers = (across, diagonal, sibling)
    mine = 2 * odd
    other = 2 - 2 * odd
    seats = (4 + mine, 4 + other, other)

    def remote(src, dst, send, recv, **device):
        return pltpu.make_async_remote_copy(
            src_ref=src, dst_ref=dst, send_sem=send, recv_sem=recv, device_id=device,
            device_id_type=MESH,
        )

    def half(c):
        return pl.ds(pl.multiple_of(c * cols, cols), cols)

    def pair(seat):
        return pl.ds(seat, per_dev)

    def local(src, dst, n):
        return pltpu.make_async_copy(src, dst, load_sem.at[n])

    inner = pl.ds(TILE, rows)
    here_cols = half(odd)
    loads = [
        local(a_hbm, A, 0),
        local(s_hbm.at[:, :, :, here_cols], ST.at[pair(mine)], 1),
        local(a_hbm.at[:, :, :, here_cols], AT.at[pair(mine), :, inner, :], 2),
        local(fp_hbm.at[:, :, here_cols], FP.at[pair(mine)], 3),
        local(fs_hbm.at[:, :, here_cols], FS.at[pair(mine), inner, :], 4),
        local(ds_hbm.at[:, :, here_cols], DS.at[pair(mine)], 5),
        local(vol_hbm.at[:, here_cols], VOL, 6),
        local(ds_hbm, DH, 7),
    ]
    tables = [
        local(dinv_hbm, dinv, 8),
        local(cells_hbm, cells, 9),
        local(counts_hbm, counts, 10),
        local(weights_hbm, weights, 11),
        local(pblock_hbm, pblock, 12),
        local(shift_hbm, shift, 13),
        local(targets_hbm, targets, 14),
        local(blocks_hbm, blocks, 15),
        local(freq_hbm, freq, 16),
    ]

    barrier = pltpu.get_barrier_semaphore()
    for peer in peers:
        pl.semaphore_signal(barrier, inc=1, device_id={"inst": peer}, device_id_type=MESH)

    has_hi = me < n_space - 2
    has_lo = me > 1
    hi = (me + 2) % n_space
    lo = (me + n_space - 2) % n_space
    partner = me + 1 - 2 * (me % 2)

    def greet(semaphore, device):
        pl.semaphore_signal(
            semaphore, inc=1, device_id={"space": device}, device_id_type=MESH
        )

    even = me % 2 == 0

    @pl.when(even)
    def _():
        greet(barrier, partner)

    @pl.when(has_hi)
    def _():
        greet(barrier, hi)

    for copy in loads[:1] + tables + loads[1:]:
        copy.start()

    def incoming(n, target, seat):
        if n == 0:
            src, dst = a_hbm, AT.at[pair(seat), :, inner, :]
        else:
            src, dst = s_hbm, ST.at[pair(seat)]
        return remote(
            src.at[:, :, :, half(target)], dst, in_s.at[n], in_r.at[n], inst=sibling
        )

    def seat_there(kind):
        return mine + (4 if kind < 2 else 0)

    def target_half(kind):
        return odd if kind == 0 else 1 - odd

    def share(which, part):
        begin = part * part_rows
        span = pl.ds(begin, part_rows)
        src, dst, land = (
            (ds_hbm, DS, span),
            (fp_hbm, FP, span),
            (fs_hbm, FS, pl.ds(begin + TILE, part_rows)),
        )[which]
        n = 2 * which + part

        def make(kind, column, seat):
            return remote(
                src.at[:, span, half(column)], dst.at[pair(seat), land, :],
                c_s.at[kind, n], c_r.at[kind, n], inst=peers[kind],
            )

        return make

    def dv_copy(kind, column, seat):
        return remote(
            DV.at[0, pl.ds(0, 1)], DV.at[kind + 1, pl.ds(0, 1)], c_s.at[kind, 6], c_r.at[kind, 6], inst=peers[kind]
        )

    lower, upper = ([share(which, part) for which in range(3)] for part in range(2))
    linked, beside = (0, 1), (2,)

    def start(copy, kinds=(0, 1, 2)):
        for kind in kinds:
            copy(kind, target_half(kind), seat_there(kind)).start()

    def arrived(copy, kinds=(0, 1, 2)):
        for kind in kinds:
            copy(kind, odd, seats[kind]).wait_recv()

    def sent(copy, kinds=(0, 1, 2)):
        for kind in kinds:
            copy(kind, target_half(kind), seat_there(kind)).wait_send()

    def r_copy(kind, b, column):
        row = pl.multiple_of(b * TILE, TILE)
        land = FAR if kind < 2 else NEAR
        return remote(
            RT.at[pair(seats[kind]), :, pl.ds(row, TILE), :],
            land.at[:, :, pl.ds(row, TILE), half(column)],
            r_s.at[kind, b], r_r.at[kind, b], inst=peers[kind],
        )

    def r_own(b):
        row = pl.multiple_of(b * TILE, TILE)
        return pltpu.make_async_copy(
            RT.at[pair(mine), :, pl.ds(row, TILE), :],
            NEAR.at[:, :, pl.ds(row, TILE), here_cols], own_r.at[b],
        )

    has_above = me < n_space - 1
    has_below = me > 0
    above = (me + 1) % n_space
    below = (me + n_space - 1) % n_space
    field_of = (AT, Y.at[pl.ds(CHIP, CHIP)], Y.at[pl.ds(0, CHIP)])

    def halo_up(stage):
        ref = field_of[stage]
        return remote(
            ref.at[:, :, pl.ds(rows + TILE - 1, 1), :], ref.at[:, :, pl.ds(TILE - 1, 1), :],
            hs.at[2 * stage], hr.at[2 * stage], space=above,
        )

    def halo_down(stage):
        ref = field_of[stage]
        return remote(
            ref.at[:, :, pl.ds(TILE, 1), :], ref.at[:, :, pl.ds(rows + TILE, 1), :],
            hs.at[2 * stage + 1], hr.at[2 * stage + 1], space=below,
        )

    def halo_face(side):
        group = pl.ds(side * CHIP, CHIP)
        return remote(
            FS.at[group, pl.ds(rows + TILE - 1, 1), :], FS.at[group, pl.ds(TILE - 1, 1), :],
            hs.at[6 + side], hr.at[6 + side], space=above,
        )

    def col_copies(stage, span, n):
        return (
            remote(
                PW.at[stage, span], CL.at[stage, span], cols_s.at[n], cols_r.at[n], inst=sibling
            ),
            remote(
                PF.at[stage, span], CR.at[stage, span], cols_s.at[n], cols_r.at[n], inst=sibling
            ),
        )

    def col_do(way, stage, span, n):
        to_right, to_left = col_copies(stage, span, n)
        is_left = odd == 0
        if way == "receive":
            is_left = odd == 1

        @pl.when(is_left)
        def _():
            act(way, to_right)

        @pl.when(jnp.logical_not(is_left))
        def _():
            act(way, to_left)

    def act(way, copy):
        if way == "start":
            copy.start()
        elif way == "receive":
            copy.wait_recv()
        else:
            copy.wait_send()

    def rows_do(way, stage):
        up, down = has_above, has_below
        if way == "receive":
            up, down = has_below, has_above

        @pl.when(up)
        def _():
            act(way, halo_up(stage))

        @pl.when(down)
        def _():
            act(way, halo_down(stage))

    def zeros(*shape):
        return jnp.zeros(shape, jnp.float32)

    @pl.when(me == 0)
    def _():
        FS[:, 0:TILE, :] = zeros(instances, TILE, cols)
        AT[:, :, 0:TILE, :] = zeros(CHIP, variables, TILE, cols)
        Y[:, :, 0:TILE, :] = zeros(instances, variables, TILE, cols)

    @pl.when(me == n_space - 1)
    def _():
        AT[:, :, rows + TILE : rows + 2 * TILE, :] = zeros(CHIP, variables, TILE, cols)
        Y[:, :, rows + TILE : rows + 2 * TILE, :] = zeros(instances, variables, TILE, cols)

    @pl.when(odd == 0)
    def _():
        CL[...] = zeros(3, rows, LANES)

    @pl.when(odd == 1)
    def _():
        CR[...] = zeros(3, rows, LANES)

    sub8 = lax.broadcasted_iota(jnp.int32, (TILE, cols), 0)
    lane8 = lax.broadcasted_iota(jnp.int32, (TILE, cols), 1)
    lane1 = lax.broadcasted_iota(jnp.int32, (TILE, LANES), 1)

    pl.semaphore_wait(barrier, n_inst - 1 + has_lo.astype(jnp.int32) + me % 2)

    for copy in upper:
        start(copy, linked)
    incoming(0, 1 - odd, mine).start()
    for copy in upper + lower:
        start(copy, beside)
    incoming(1, 1 - odd, mine).start()

    tables[0].wait()
    packed = zeros(TILE, LANES)
    for k in range(per_dev):
        for u in range(variables):
            for v in range(variables):
                n = (k * variables + u) * variables + v
                packed = jnp.where(lane1 == n, dinv[u, k, v], packed)
    DV[0] = packed
    start(dv_copy)

    @pl.when(jnp.logical_not(even))
    def _():
        greet(token.at[2], partner)

    @pl.when(has_lo)
    def _():
        greet(token.at[3], lo)

    sub_w = lax.broadcasted_iota(jnp.int32, (width, slots), 0)
    sub_h = lax.broadcasted_iota(jnp.int32, (cols, slots), 0)
    sub_r = lax.broadcasted_iota(jnp.int32, (rows, slots), 0)

    def column_table(index, chunk):
        for q in range(TILE):
            line = index(chunk * TILE + q)
            column = jnp.bitwise_and(line, width - 1)
            hot = jnp.where(sub_w == column, 1.0, 0.0).astype(jnp.bfloat16)
            COL[:, q * slots : (q + 1) * slots] = hot

    def half_table(index, chunk):
        for q in range(TILE):
            line = index(chunk * TILE + q)
            column = jnp.bitwise_and(line, width - 1) - odd * cols
            hot = jnp.where(sub_h == column, 1.0, 0.0).astype(jnp.bfloat16)
            COL[0:cols, q * slots : (q + 1) * slots] = hot

    def cell_line(q):
        return cells[0, pl.ds(q, 1), :]

    def target_line(p):
        return targets[p, 0:1, :]

    chunks = n_space // TILE

    loads[0].wait()
    for copy in tables[1:]:
        copy.wait()

    @pl.loop(0, chunks)
    def _(chunk):
        column_table(cell_line, chunk)

        @pl.loop(0, per_dev)
        def _(k):
            field = A[k].reshape(variables * rows, width)
            stacked = jnp.concatenate(split_parts(field), axis=0)
            terms = jnp.dot(stacked, COL[...], preferred_element_type=jnp.float32)
            height = variables * rows
            found = terms[:height]
            for part in range(1, PARTS):
                found = found + terms[part * height : (part + 1) * height]
            for q in range(TILE):
                hit = sub_r == lax.shift_right_logical(cell_line(chunk * TILE + q), shift_bits)
                for v in range(variables):
                    piece = found[v * rows : (v + 1) * rows, q * slots : (q + 1) * slots]
                    PICK[k, v, chunk, q : q + 1, :] = jnp.sum(
                        jnp.where(hit, piece, 0.0), axis=0, keepdims=True
                    )

        lane = lax.broadcasted_iota(jnp.int32, (TILE, slots), 1)
        sub = lax.broadcasted_iota(jnp.int32, (TILE, slots), 0)
        limit = jnp.zeros((TILE, slots), jnp.int32)
        for q in range(TILE):
            limit = jnp.where(sub == q, counts[0, chunk * TILE + q], limit)
        first = pl.multiple_of(chunk * TILE, TILE)
        weight = jnp.where(lane < limit, weights[0, pl.ds(first, TILE), :], 0.0)

        for k in range(per_dev):
            picked = [PICK[k, v, chunk] for v in range(variables)]
            for u in range(variables):
                mixed = pblock[0, u] * picked[0]
                for v in range(1, variables):
                    mixed = mixed + pblock[v, u] * picked[v]
                ALLP[0, k, u, chunk] = mixed * weight

    p_x = remote(ALLP.at[0], ALLP.at[2], ps.at[0], pr.at[0], inst=across)
    p_sib = remote(ALLP.at[0], ALLP.at[3 - 2 * odd], ps.at[1], pr.at[1 + odd], inst=sibling)
    p_rel = remote(ALLP.at[2], ALLP.at[1 + 2 * odd], ps.at[2], pr.at[2 - odd], inst=sibling)
    p_sib_in = remote(ALLP.at[0], ALLP.at[1 + 2 * odd], ps.at[1], pr.at[2 - odd], inst=sibling)
    p_rel_in = remote(ALLP.at[2], ALLP.at[3 - 2 * odd], ps.at[2], pr.at[1 + odd], inst=sibling)
    p_x.start()
    p_sib.start()
    for copy in lower:
        start(copy, linked)

    @pl.when(even)
    def _():
        pl.semaphore_wait(token.at[2], 1)

    @pl.when(has_hi)
    def _():
        pl.semaphore_wait(token.at[3], 1)
        pl.semaphore_wait(token.at[0], 1)

    @pl.when(has_lo)
    def _():
        greet(token.at[0], lo)
        pl.semaphore_wait(token.at[1], 1)

    @pl.when(has_hi)
    def _():
        greet(token.at[1], hi)

    for copy in loads[1:]:
        copy.wait()
    for n in range(2):
        incoming(n, odd, other).wait_recv()
    for copy in upper + lower:
        arrived(copy, beside)
    rows_do("start", 0)

    @pl.when(has_above)
    def _():
        halo_face(0).start()

    def wide(tile):
        return jnp.concatenate([tile] * (cols // LANES), axis=1)

    whole = pl.ds(0, rows)

    def pack(stage, ref, base, row):
        here = pl.ds(row, TILE)
        mid = pl.ds(row + TILE, TILE)
        last = zeros(TILE, LANES)
        first = zeros(TILE, LANES)
        for r in range(CHIP):
            fp = FP[base + r, here, cols - LANES : cols]
            for v in range(variables):
                n = r * variables + v
                a = ref[base + r, v, mid, 0:LANES]
                w = fp * ref[base + r, v, mid, cols - LANES : cols]
                first = jnp.where(lane1 == n, pltpu.roll(a, n, 1) if n else a, first)
                last = jnp.where(lane1 == n, pltpu.roll(w, n + 1, 1), last)
        PW[stage, here, :] = last
        PF[stage, here, :] = first

    @pl.loop(0, nb)
    def _(b):
        pack(0, AT, 0, pl.multiple_of(b * TILE, TILE))

    col_do("start", 0, whole, nb)

    arrived(dv_copy)
    for position in range(instances):
        if position < CHIP:
            kind = jnp.where(odd == position // per_dev, 0, 3)
        else:
            kind = jnp.where(odd == (position - CHIP) // per_dev, 1, 2)
        vector = DV[kind, 0:1, :]
        for n in range(variables * variables):
            lane = (position % per_dev) * variables * variables + n
            DT[position * variables * variables + n] = jnp.broadcast_to(
                vector[:, lane : lane + 1], (TILE, LANES)
            )

    for copy in upper:
        arrived(copy, linked)

    @pl.when(has_above)
    def _():
        halo_face(1).start()

    f1, f2, f3 = (spectral_entry(d, instances) for d in (1, 2, 3))

    def spectral(a, row):
        here = pl.ds(row, TILE)
        scaled = freq[0] * VOL[here, :]
        v1 = (0.5 * (f1 - f3)) * scaled
        v2 = f2 * scaled
        v3 = (0.5 * (f1 + f3)) * scaled
        results = []
        for u in range(variables):
            near = [a(r, u) for r in range(4)]
            far = [a(r, u) for r in range(4, 8)]
            b = [m if f is None else m - f for m, f in zip(near, far)]
            c = [m if f is None else m + f for m, f in zip(near, far)]
            even = v1 * (c[1] - c[3])
            odds = v1 * (c[2] - c[0])
            q = [even, odds, -even, -odds]
            p = [
                v2 * b[2] + v3 * (b[1] + b[3]),
                v2 * b[3] + v3 * (b[2] - b[0]),
                v3 * (b[3] - b[1]) - v2 * b[0],
                -(v2 * b[1] + v3 * (b[0] + b[2])),
            ]
            results.append((q, p))
        return results

    def coupling(acc, span, ref, row, stage):
        here = pl.ds(row, TILE)
        mid = pl.ds(row + TILE, TILE)
        low = pl.ds(row, TILE)
        high = pl.ds(row + 2 * TILE, TILE)
        top = sub8 == TILE - 1
        bottom = sub8 == 0
        fm = {r: FS[r, mid, :] for r in span}
        fl = {r: jnp.where(top, FS[r, low, :], fm[r]) for r in span}
        fp = {r: FP[r, here, :] for r in span}
        cl = CL[stage, here, :]
        cr = CR[stage, here, :]
        for v in range(variables):
            terms = {}
            for r in span:
                n = (r % CHIP) * variables + v
                a = ref[r, v, mid, :]
                x = pltpu.roll(fl[r] * jnp.where(top, ref[r, v, low, :], a), 1, 0)
                y = fm[r] * pltpu.roll(
                    jnp.where(bottom, ref[r, v, high, :], a), TILE - 1, 0
                )
                edge = wide(pltpu.roll(cl, LANES - n, 1) if n else cl)
                left = jnp.where(lane8 == 0, edge, pltpu.roll(fp[r] * a, 1, 1))
                edge = wide(pltpu.roll(cr, LANES - 1 - n, 1))
                right = fp[r] * jnp.where(
                    lane8 == cols - 1, edge, pltpu.roll(a, cols - 1, 1)
                )
                terms[r] = (x, y, left, right)
            for u in range(variables):
                k0, k1, k2, k3 = (blocks[v, n, u] for n in range(4))
                for r in span:
                    x, y, left, right = terms[r]
                    acc[r, u] = acc[r, u] - ((k0 * x + k1 * y) + (k2 * left + k3 * right))
        return acc

    def inverse(acc, r, u, here):
        n = (r * variables + u) * variables
        new = wide(DT[n]) * acc[0]
        for v in range(1, variables):
            new = new + wide(DT[n + v]) * acc[v]
        return DS[r, here, :] * new

    rows_do("receive", 0)
    col_do("receive", 0, whole, nb)

    @pl.when(has_below)
    def _():
        halo_face(0).wait_recv()

    middle = nb // 2

    def sweep(b):
        row = pl.multiple_of(b * TILE, TILE)
        here = pl.ds(row, TILE)
        mid = pl.ds(row + TILE, TILE)
        found = spectral(lambda r, u: AT[r, u, mid, :] if r < CHIP else None, row)
        for u, (q, p) in enumerate(found):
            for r in range(CHIP):
                RT[r, u, here, :] = ST[r, u, here, :] - (q[r] + p[r])
                RT[CHIP + r, u, here, :] = p[r] - q[r]
        for base in range(0, instances, GROUP):
            span = range(base, base + GROUP)
            acc = {(r, u): RT[r, u, here, :] for r in span for u in range(variables)}
            if base < CHIP:
                acc = coupling(acc, span, AT, row, 0)
            for r in span:
                line = [acc[r, v] for v in range(variables)]
                for u in range(variables):
                    Y[r, u, mid, :] = inverse(line, r, u, here)
        pack(1, Y, CHIP, row)
        col_do("start", 1, here, b)

    def export(b):
        row = pl.multiple_of(b * TILE, TILE)
        here = pl.ds(row, TILE)
        mid = pl.ds(row + TILE, TILE)
        col_do("receive", 1, here, b)
        found = spectral(lambda r, u: Y[r, u, mid, :], row)
        for u, (q, p) in enumerate(found):
            for r in range(CHIP):
                RT[CHIP + r, u, here, :] = p[r] - q[r]
        for base in range(CHIP, instances, GROUP):
            span = range(base, base + GROUP)
            acc = {(r, u): RT[r, u, here, :] for r in span for u in range(variables)}
            acc = coupling(acc, span, Y, row, 1)
            for r in span:
                for u in range(variables):
                    RT[r, u, here, :] = acc[r, u]
        r_copy(0, b, odd).start()
        r_copy(1, b, odd).start()

    def order(t):
        early = (t < middle - 2).astype(jnp.int32)
        late = (t >= nb - 2).astype(jnp.int32)
        between = (1 - early) * (1 - late)
        return (
            early * (t + middle + 1)
            + between * (t - middle + 3)
            + late * (nb - 1 - t) * (nb - 1)
        )

    @pl.loop(0, nb + 4)
    def _(n):
        @pl.when(n < nb)
        def _():
            @pl.when(n == middle)
            def _():
                for copy in lower:
                    arrived(copy, linked)

            sweep((n + middle) % nb)

        @pl.when(n == middle)
        def _():
            rows_do("start", 1)

        @pl.when(n == nb + 2)
        def _():
            rows_do("receive", 1)

            @pl.when(has_below)
            def _():
                halo_face(1).wait_recv()

        @pl.when((n >= 2) & (n < middle))
        def _():
            export(order(n - 2))

        @pl.when(n >= middle + 2)
        def _():
            export(order(n - 4))

    p_x.wait_recv()
    p_rel.start()
    p_sib_in.wait_recv()
    p_rel_in.wait_recv()

    @pl.loop(0, instances)
    def _(k):
        wanted = lax.rem(k - shift[0] + 2 * instances, instances)
        group = lax.div(wanted, per_dev)
        member = lax.rem(wanted, per_dev)

        @pl.loop(0, chunks)
        def _(chunk):
            for u in range(variables):
                value = ALLP[group, member, u, chunk]
                for q in range(TILE):
                    ROUTED[chunk * TILE + q, k, u : u + 1, :] = value[q : q + 1, :]

    def a2a(j):
        return remote(
            ROUTED.at[(me + j) % n_space], ARR.at[me], q_s.at[j], q_r.at[j],
            space=(me + j) % n_space,
        )

    @pl.loop(1, n_space)
    def _(j):
        a2a(j).start()

    ARR[me] = ROUTED[me]

    half_table(target_line, 0)

    @pl.loop(1, n_space)
    def _(j):
        remote(
            ROUTED.at[0], ARR.at[(me + n_space - j) % n_space], q_s.at[j], q_r.at[j],
            space=(me + j) % n_space,
        ).wait_recv()

    if chunks > 1:
        PT[...] = zeros(instances, variables, rows, cols)

    @pl.loop(0, chunks)
    def _(chunk):
        if chunks > 1:
            half_table(target_line, chunk)

        @pl.loop(0, instances)
        def _(r):
            k = (r + instances - mine) % instances
            for p in range(TILE):
                hit = sub_r == lax.shift_right_logical(target_line(chunk * TILE + p), shift_bits)
                parts = split_parts(ARR[chunk * TILE + p, k])
                for n, part in enumerate(parts):
                    for u in range(variables):
                        begin = (n * variables + u) * rows
                        LHS[begin : begin + rows, p * slots : (p + 1) * slots] = jnp.where(
                            hit, part[u : u + 1, :].astype(jnp.float32), 0.0
                        ).astype(jnp.bfloat16)
            terms = lax.dot_general(
                LHS[...], COL[0:cols, :], (((1,), (1,)), ((), ())),
                preferred_element_type=jnp.float32,
            )
            height = variables * rows
            summed = terms[:height]
            for part in range(1, PARTS):
                summed = summed + terms[part * height : (part + 1) * height]
            summed = summed.reshape(variables, rows, cols)
            if chunks > 1:
                summed = summed + PT[r]
            PT[r] = summed

    rows_do("sent", 1)

    @pl.loop(0, nb)
    def _(b):
        row = pl.multiple_of(b * TILE, TILE)
        here = pl.ds(row, TILE)
        mid = pl.ds(row + TILE, TILE)
        for r in range(instances):
            line = [PT[r, v, here, :] for v in range(variables)]
            for u in range(variables):
                Y[r, u, mid, :] = Y[r, u, mid, :] - inverse(line, r, u, here)
                if r < CHIP:
                    ST[r, u, here, :] = ST[r, u, here, :] - line[u]

    rows_do("start", 2)

    @pl.loop(0, nb)
    def _(b):
        pack(2, Y, 0, pl.multiple_of(b * TILE, TILE))

    col_do("start", 2, whole, nb + 1)
    rows_do("receive", 2)
    col_do("receive", 2, whole, nb + 1)

    @pl.loop(0, nb)
    def _(b):
        row = pl.multiple_of(b * TILE, TILE)
        here = pl.ds(row, TILE)
        mid = pl.ds(row + TILE, TILE)
        found = spectral(lambda r, u: Y[r, u, mid, :], row)
        for u, (q, p) in enumerate(found):
            for r in range(CHIP):
                RT[r, u, here, :] = ST[r, u, here, :] - (q[r] + p[r])
        for base in range(0, CHIP, GROUP):
            span = range(base, base + GROUP)
            acc = {(r, u): RT[r, u, here, :] for r in span for u in range(variables)}
            acc = coupling(acc, span, Y, row, 2)
            for r in span:
                for u in range(variables):
                    RT[r, u, here, :] = acc[r, u]
        r_copy(2, b, odd).start()
        r_own(b).start()

    @pl.loop(0, nb)
    def _(t):
        b = order(t)
        here = pl.ds(pl.multiple_of(b * TILE, TILE), TILE)
        r_own(b).wait()
        r_copy(2, b, 1 - odd).wait_recv()
        r_copy(0, b, odd).wait_recv()
        r_copy(1, b, 1 - odd).wait_recv()
        for k in range(per_dev):
            scale = DH[k, here, :]
            rest = [NEAR[k, v, here, :] + FAR[k, v, here, :] for v in range(variables)]
            for u in range(variables):
                out_r[k, u, here, :] = rest[u]
                new = dinv[u, k, 0] * rest[0]
                for v in range(1, variables):
                    new = new + dinv[u, k, v] * rest[v]
                out_a[k, u, here, :] = scale * new

    for copy in (dv_copy, *upper, *lower):
        sent(copy)
    for n in range(2):
        incoming(n, 1 - odd, mine).wait_send()

    p_x.wait_send()
    p_sib.wait_send()
    p_rel.wait_send()

    @pl.loop(1, n_space)
    def _(j):
        a2a(j).wait_send()

    @pl.when(has_above)
    def _():
        halo_face(0).wait_send()
        halo_face(1).wait_send()

    rows_do("sent", 0)
    rows_do("sent", 2)
    col_do("sent", 0, whole, nb)
    col_do("sent", 2, whole, nb + 1)

    @pl.loop(0, nb)
    def _(b):
        for kind in range(3):
            r_copy(kind, b, odd).wait_send()
        col_do("sent", 1, pl.ds(pl.multiple_of(b * TILE, TILE), TILE), b)


def finish(a, r, out_a, out_r, sems):
    copies = [
        pltpu.make_async_copy(a, out_a, sems.at[0]),
        pltpu.make_async_copy(r, out_r, sems.at[1]),
    ]
    for copy in copies:
        copy.start()
    for copy in copies:
        copy.wait()


def body(n_space, n_inst, a, s, fs, fp, ds, vol, blocks, dinv, *rest):
    per_dev, variables, rows, width = a.shape
    slots = rest[3].shape[2]
    nb = rows // TILE
    chunks = n_space // TILE
    instances = n_inst * per_dev
    cols = width // 2
    f32 = jnp.float32
    hbm = pl.BlockSpec(memory_space=pl.ANY)
    vmem = pl.BlockSpec(memory_space=pltpu.VMEM)
    dma = pltpu.SemaphoreType.DMA
    field = (per_dev, variables, rows, width)
    out = jax.ShapeDtypeStruct(field, f32)
    blocks = jnp.transpose(blocks, (1, 0, 2))
    dinv = jnp.transpose(dinv, (1, 0, 2))
    placed = pltpu.VMEM(field, f32)
    new, r = pl.pallas_call(
        functools.partial(kernel, n_space, n_inst),
        out_shape=(placed, placed),
        in_specs=[hbm] * 15,
        out_specs=(vmem, vmem),
        scratch_shapes=[
            pltpu.SMEM(blocks.shape, f32),
            pltpu.SMEM(dinv.shape, f32),
            pltpu.SMEM(rest[0].shape, f32),
            pltpu.SMEM(rest[1].shape, f32),
            pltpu.SMEM(rest[2].shape, jnp.int32),
            pltpu.VMEM(rest[3].shape, jnp.int32),
            pltpu.VMEM(rest[4].shape, jnp.int32),
            pltpu.VMEM(rest[5].shape, f32),
            pltpu.SMEM(rest[6].shape, jnp.int32),
            pltpu.VMEM(field, f32),
            pltpu.VMEM((CHIP, variables, rows + 2 * TILE, cols), f32),
            pltpu.VMEM((CHIP, variables, rows, cols), f32),
            pltpu.VMEM((instances, variables, rows + 2 * TILE, cols), f32),
            pltpu.VMEM((instances, variables, rows, cols), f32),
            pltpu.VMEM((instances, variables, rows, cols), f32),
            pltpu.VMEM(field, f32),
            pltpu.VMEM(field, f32),
            pltpu.VMEM((instances, rows + TILE, cols), f32),
            pltpu.VMEM((instances, rows, cols), f32),
            pltpu.VMEM((instances, rows, cols), f32),
            pltpu.VMEM((rows, cols), f32),
            pltpu.VMEM((per_dev, rows, width), f32),
            pltpu.VMEM((3, rows, LANES), f32),
            pltpu.VMEM((3, rows, LANES), f32),
            pltpu.VMEM((3, rows, LANES), f32),
            pltpu.VMEM((3, rows, LANES), f32),
            pltpu.VMEM((n_inst, TILE, LANES), f32),
            pltpu.VMEM((instances * variables * variables, TILE, LANES), f32),
            pltpu.VMEM((width, TILE * slots), jnp.bfloat16),
            pltpu.VMEM((per_dev, variables, chunks, TILE, slots), f32),
            pltpu.VMEM((4, per_dev, variables, chunks, TILE, slots), f32),
            pltpu.VMEM((n_space, instances, variables, slots), f32),
            pltpu.VMEM((n_space, instances, variables, slots), f32),
            pltpu.VMEM((PARTS * variables * rows, TILE * slots), jnp.bfloat16),
            dma((17,)),
            dma((nb,)),
            dma((2,)),
            dma((2,)),
            dma((3, 7)),
            dma((3, 7)),
            dma((3, nb)),
            dma((3, nb)),
            dma((nb + 2,)),
            dma((nb + 2,)),
            dma((8,)),
            dma((8,)),
            dma((3,)),
            dma((3,)),
            dma((n_space,)),
            dma((n_space,)),
            pltpu.SemaphoreType.REGULAR((4,)),
        ],
        compiler_params=pltpu.CompilerParams(
            collective_id=0, has_side_effects=True, vmem_limit_bytes=56 * 1024 * 1024
        ),
    )(a, s, fs, fp, ds, vol, blocks, dinv, *rest)
    return pl.pallas_call(
        finish,
        out_shape=(out, out),
        in_specs=[vmem, vmem],
        out_specs=(hbm, hbm),
        scratch_shapes=[dma((2,))],
    )(*(pltpu.with_memory_space_constraint(x, pltpu.VMEM) for x in (new, r)))


def solution(mesh):
    in_specs = (
        P("inst", None, "space", None),
        P("inst", None, "space", None),
        P("inst", "space", None),
        P("inst", "space", None),
        P("inst", "space", None),
        P("space", None),
        P(),
        P("inst", None, None),
        P(),
        P(),
        P(),
        P("space", None, None),
        P(None, "space", None),
        P("space", None, None),
        P("space", None),
    )
    out_specs = (P("inst", None, "space", None), P("inst", None, "space", None))
    return jax.shard_map(
        functools.partial(body, mesh.shape["space"], mesh.shape["inst"]),
        mesh=mesh,
        in_specs=in_specs,
        out_specs=out_specs,
        check_vma=False,
    )
```

```python
import functools
import math

import jax
import jax.numpy as jnp
from jax import lax
from jax.experimental import pallas as pl
from jax.experimental.pallas import tpu as pltpu
from jax.sharding import PartitionSpec as P

SWEEPS = 2
TILE = 8
LANES = 128
PARTS = 2
CHIP = 4
GROUP = 2
MESH = pl.DeviceIdType.MESH


def spectral_entry(offset, count):
    offset = offset % count
    if offset == 0 or 2 * offset == count:
        return 0.0
    return 0.5 * (-1.0) ** offset / math.tan(math.pi * offset / count)


def split_parts(value):
    parts = []
    for _ in range(PARTS):
        part = value.astype(jnp.bfloat16)
        parts.append(part)
        value = value - part.astype(jnp.float32)
    return parts


def kernel(
    n_space,
    n_inst,
    a_hbm,
    s_hbm,
    fs_hbm,
    fp_hbm,
    ds_hbm,
    vol_hbm,
    blocks_hbm,
    dinv_hbm,
    pblock_hbm,
    freq_hbm,
    shift_hbm,
    cells_hbm,
    targets_hbm,
    weights_hbm,
    counts_hbm,
    out_a,
    out_r,
    blocks,
    dinv,
    pblock,
    freq,
    shift,
    cells,
    targets,
    weights,
    counts,
    A,
    AT,
    ST,
    Y,
    RT,
    PT,
    NEAR,
    FAR,
    FS,
    FP,
    DS,
    VOL,
    DH,
    CL,
    CR,
    PW,
    PF,
    DV,
    DT,
    COL,
    PICK,
    ALLP,
    ROUTED,
    ARR,
    LHS,
    load_sem,
    own_r,
    in_s,
    in_r,
    c_s,
    c_r,
    r_s,
    r_r,
    cols_s,
    cols_r,
    hs,
    hr,
    ps,
    pr,
    q_s,
    q_r,
    token,
):
    per_dev, variables, rows, width = a_hbm.shape
    instances = n_inst * per_dev
    cols = width // 2
    slots = cells.shape[2]
    nb = rows // TILE
    part_rows = rows // 2
    inst = lax.axis_index("inst")
    me = lax.axis_index("space")
    odd = inst % 2
    sibling = inst + 1 - 2 * odd
    across = (inst + 2) % n_inst
    diagonal = (sibling + 2) % n_inst
    shift_bits = width.bit_length() - 1
    peers = (across, diagonal, sibling)
    mine = 2 * odd
    other = 2 - 2 * odd
    seats = (4 + mine, 4 + other, other)

    def remote(src, dst, send, recv, **device):
        return pltpu.make_async_remote_copy(
            src_ref=src, dst_ref=dst, send_sem=send, recv_sem=recv, device_id=device,
            device_id_type=MESH,
        )

    def half(c):
        return pl.ds(pl.multiple_of(c * cols, cols), cols)

    def pair(seat):
        return pl.ds(seat, per_dev)

    def local(src, dst, n):
        return pltpu.make_async_copy(src, dst, load_sem.at[n])

    inner = pl.ds(TILE, rows)
    here_cols = half(odd)
    loads = [
        local(a_hbm, A, 0),
        local(s_hbm.at[:, :, :, here_cols], ST.at[pair(mine)], 1),
        local(a_hbm.at[:, :, :, here_cols], AT.at[pair(mine), :, inner, :], 2),
        local(fp_hbm.at[:, :, here_cols], FP.at[pair(mine)], 3),
        local(fs_hbm.at[:, :, here_cols], FS.at[pair(mine), inner, :], 4),
        local(ds_hbm.at[:, :, here_cols], DS.at[pair(mine)], 5),
        local(vol_hbm.at[:, here_cols], VOL, 6),
        local(ds_hbm, DH, 7),
    ]
    tables = [
        local(dinv_hbm, dinv, 8),
        local(cells_hbm, cells, 9),
        local(counts_hbm, counts, 10),
        local(weights_hbm, weights, 11),
        local(pblock_hbm, pblock, 12),
        local(shift_hbm, shift, 13),
        local(targets_hbm, targets, 14),
        local(blocks_hbm, blocks, 15),
        local(freq_hbm, freq, 16),
    ]

    barrier = pltpu.get_barrier_semaphore()
    for peer in peers:
        pl.semaphore_signal(barrier, inc=1, device_id={"inst": peer}, device_id_type=MESH)

    has_hi = me < n_space - 2
    has_lo = me > 1
    hi = (me + 2) % n_space
    lo = (me + n_space - 2) % n_space
    partner = me + 1 - 2 * (me % 2)

    def greet(semaphore, device):
        pl.semaphore_signal(
            semaphore, inc=1, device_id={"space": device}, device_id_type=MESH
        )

    even = me % 2 == 0

    @pl.when(even)
    def _():
        greet(barrier, partner)

    @pl.when(has_hi)
    def _():
        greet(barrier, hi)

    def incoming(n, target, seat):
        if n == 0:
            src, dst = a_hbm, AT.at[pair(seat), :, inner, :]
        else:
            src, dst = s_hbm, ST.at[pair(seat)]
        return remote(
            src.at[:, :, :, half(target)], dst, in_s.at[n], in_r.at[n], inst=sibling
        )

    def seat_there(kind):
        return mine + (4 if kind < 2 else 0)

    def target_half(kind):
        return odd if kind == 0 else 1 - odd

    def share(which, part):
        begin = part * part_rows
        span = pl.ds(begin, part_rows)
        src, dst, land = (
            (ds_hbm, DS, span),
            (fp_hbm, FP, span),
            (fs_hbm, FS, pl.ds(begin + TILE, part_rows)),
        )[which]
        n = 2 * which + part

        def make(kind, column, seat):
            return remote(
                src.at[:, span, half(column)], dst.at[pair(seat), land, :],
                c_s.at[kind, n], c_r.at[kind, n], inst=peers[kind],
            )

        return make

    def dv_copy(kind, column, seat):
        return remote(
            DV.at[0, pl.ds(0, 1)], DV.at[kind + 1, pl.ds(0, 1)], c_s.at[kind, 6], c_r.at[kind, 6], inst=peers[kind]
        )

    lower, upper = ([share(which, part) for which in range(3)] for part in range(2))
    linked, beside = (0, 1), (2,)

    def start(copy, kinds=(0, 1, 2)):
        for kind in kinds:
            copy(kind, target_half(kind), seat_there(kind)).start()

    def arrived(copy, kinds=(0, 1, 2)):
        for kind in kinds:
            copy(kind, odd, seats[kind]).wait_recv()

    def sent(copy, kinds=(0, 1, 2)):
        for kind in kinds:
            copy(kind, target_half(kind), seat_there(kind)).wait_send()

    def r_copy(kind, b, column):
        row = pl.multiple_of(b * TILE, TILE)
        land = FAR if kind < 2 else NEAR
        return remote(
            RT.at[pair(seats[kind]), :, pl.ds(row, TILE), :],
            land.at[:, :, pl.ds(row, TILE), half(column)],
            r_s.at[kind, b], r_r.at[kind, b], inst=peers[kind],
        )

    def r_own(b):
        row = pl.multiple_of(b * TILE, TILE)
        return pltpu.make_async_copy(
            RT.at[pair(mine), :, pl.ds(row, TILE), :],
            NEAR.at[:, :, pl.ds(row, TILE), here_cols], own_r.at[b],
        )

    has_above = me < n_space - 1
    has_below = me > 0
    above = (me + 1) % n_space
    below = (me + n_space - 1) % n_space
    field_of = (AT, Y.at[pl.ds(CHIP, CHIP)], Y.at[pl.ds(0, CHIP)])

    def halo_up(stage):
        ref = field_of[stage]
        return remote(
            ref.at[:, :, pl.ds(rows + TILE - 1, 1), :], ref.at[:, :, pl.ds(TILE - 1, 1), :],
            hs.at[2 * stage], hr.at[2 * stage], space=above,
        )

    def halo_down(stage):
        ref = field_of[stage]
        return remote(
            ref.at[:, :, pl.ds(TILE, 1), :], ref.at[:, :, pl.ds(rows + TILE, 1), :],
            hs.at[2 * stage + 1], hr.at[2 * stage + 1], space=below,
        )

    def halo_face(side):
        group = pl.ds(side * CHIP, CHIP)
        return remote(
            FS.at[group, pl.ds(rows + TILE - 1, 1), :], FS.at[group, pl.ds(TILE - 1, 1), :],
            hs.at[6 + side], hr.at[6 + side], space=above,
        )

    def col_copies(stage, span, n):
        return (
            remote(
                PW.at[stage, span], CL.at[stage, span], cols_s.at[n], cols_r.at[n], inst=sibling
            ),
            remote(
                PF.at[stage, span], CR.at[stage, span], cols_s.at[n], cols_r.at[n], inst=sibling
            ),
        )

    def col_do(way, stage, span, n):
        to_right, to_left = col_copies(stage, span, n)
        is_left = odd == 0
        if way == "receive":
            is_left = odd == 1

        @pl.when(is_left)
        def _():
            act(way, to_right)

        @pl.when(jnp.logical_not(is_left))
        def _():
            act(way, to_left)

    def act(way, copy):
        if way == "start":
            copy.start()
        elif way == "receive":
            copy.wait_recv()
        else:
            copy.wait_send()

    def rows_do(way, stage):
        up, down = has_above, has_below
        if way == "receive":
            up, down = has_below, has_above

        @pl.when(up)
        def _():
            act(way, halo_up(stage))

        @pl.when(down)
        def _():
            act(way, halo_down(stage))

    def zeros(*shape):
        return jnp.zeros(shape, jnp.float32)

    sub8 = lax.broadcasted_iota(jnp.int32, (TILE, cols), 0)
    lane8 = lax.broadcasted_iota(jnp.int32, (TILE, cols), 1)
    lane1 = lax.broadcasted_iota(jnp.int32, (TILE, LANES), 1)

    pl.semaphore_wait(barrier, n_inst - 1 + has_lo.astype(jnp.int32) + me % 2)

    for copy in upper:
        start(copy, linked)
    incoming(0, 1 - odd, mine).start()
    for copy in upper + lower:
        start(copy, beside)
    incoming(1, 1 - odd, mine).start()

    for copy in loads[:1] + tables + loads[1:]:
        copy.start()

    @pl.when(me == 0)
    def _():
        FS[:, 0:TILE, :] = zeros(instances, TILE, cols)
        AT[:, :, 0:TILE, :] = zeros(CHIP, variables, TILE, cols)
        Y[:, :, 0:TILE, :] = zeros(instances, variables, TILE, cols)

    @pl.when(me == n_space - 1)
    def _():
        AT[:, :, rows + TILE : rows + 2 * TILE, :] = zeros(CHIP, variables, TILE, cols)
        Y[:, :, rows + TILE : rows + 2 * TILE, :] = zeros(instances, variables, TILE, cols)

    @pl.when(odd == 0)
    def _():
        CL[...] = zeros(3, rows, LANES)

    @pl.when(odd == 1)
    def _():
        CR[...] = zeros(3, rows, LANES)

    tables[0].wait()
    packed = zeros(TILE, LANES)
    for k in range(per_dev):
        for u in range(variables):
            for v in range(variables):
                n = (k * variables + u) * variables + v
                packed = jnp.where(lane1 == n, dinv[u, k, v], packed)
    DV[0] = packed
    start(dv_copy)

    @pl.when(jnp.logical_not(even))
    def _():
        greet(token.at[2], partner)

    @pl.when(has_lo)
    def _():
        greet(token.at[3], lo)

    sub_w = lax.broadcasted_iota(jnp.int32, (width, slots), 0)
    sub_h = lax.broadcasted_iota(jnp.int32, (cols, slots), 0)
    sub_r = lax.broadcasted_iota(jnp.int32, (rows, slots), 0)

    def column_table(index, chunk):
        for q in range(TILE):
            line = index(chunk * TILE + q)
            column = jnp.bitwise_and(line, width - 1)
            hot = jnp.where(sub_w == column, 1.0, 0.0).astype(jnp.bfloat16)
            COL[:, q * slots : (q + 1) * slots] = hot

    def half_table(index, chunk):
        for q in range(TILE):
            line = index(chunk * TILE + q)
            column = jnp.bitwise_and(line, width - 1) - odd * cols
            hot = jnp.where(sub_h == column, 1.0, 0.0).astype(jnp.bfloat16)
            COL[0:cols, q * slots : (q + 1) * slots] = hot

    def cell_line(q):
        return cells[0, pl.ds(q, 1), :]

    def target_line(p):
        return targets[p, 0:1, :]

    chunks = n_space // TILE

    loads[0].wait()
    for copy in tables[1:]:
        copy.wait()

    @pl.loop(0, chunks)
    def _(chunk):
        column_table(cell_line, chunk)

        @pl.loop(0, per_dev)
        def _(k):
            field = A[k].reshape(variables * rows, width)
            stacked = jnp.concatenate(split_parts(field), axis=0)
            terms = jnp.dot(stacked, COL[...], preferred_element_type=jnp.float32)
            height = variables * rows
            found = terms[:height]
            for part in range(1, PARTS):
                found = found + terms[part * height : (part + 1) * height]
            for q in range(TILE):
                hit = sub_r == lax.shift_right_logical(cell_line(chunk * TILE + q), shift_bits)
                for v in range(variables):
                    piece = found[v * rows : (v + 1) * rows, q * slots : (q + 1) * slots]
                    PICK[k, v, chunk, q : q + 1, :] = jnp.sum(
                        jnp.where(hit, piece, 0.0), axis=0, keepdims=True
                    )

        lane = lax.broadcasted_iota(jnp.int32, (TILE, slots), 1)
        sub = lax.broadcasted_iota(jnp.int32, (TILE, slots), 0)
        limit = jnp.zeros((TILE, slots), jnp.int32)
        for q in range(TILE):
            limit = jnp.where(sub == q, counts[0, chunk * TILE + q], limit)
        first = pl.multiple_of(chunk * TILE, TILE)
        weight = jnp.where(lane < limit, weights[0, pl.ds(first, TILE), :], 0.0)

        for k in range(per_dev):
            picked = [PICK[k, v, chunk] for v in range(variables)]
            for u in range(variables):
                mixed = pblock[0, u] * picked[0]
                for v in range(1, variables):
                    mixed = mixed + pblock[v, u] * picked[v]
                ALLP[0, k, u, chunk] = mixed * weight

    p_x = remote(ALLP.at[0], ALLP.at[2], ps.at[0], pr.at[0], inst=across)
    p_sib = remote(ALLP.at[0], ALLP.at[3 - 2 * odd], ps.at[1], pr.at[1 + odd], inst=sibling)
    p_rel = remote(ALLP.at[2], ALLP.at[1 + 2 * odd], ps.at[2], pr.at[2 - odd], inst=sibling)
    p_sib_in = remote(ALLP.at[0], ALLP.at[1 + 2 * odd], ps.at[1], pr.at[2 - odd], inst=sibling)
    p_rel_in = remote(ALLP.at[2], ALLP.at[3 - 2 * odd], ps.at[2], pr.at[1 + odd], inst=sibling)
    p_x.start()
    p_sib.start()
    for copy in lower:
        start(copy, linked)

    @pl.when(even)
    def _():
        pl.semaphore_wait(token.at[2], 1)

    @pl.when(has_hi)
    def _():
        pl.semaphore_wait(token.at[3], 1)
        pl.semaphore_wait(token.at[0], 1)

    @pl.when(has_lo)
    def _():
        greet(token.at[0], lo)
        pl.semaphore_wait(token.at[1], 1)

    @pl.when(has_hi)
    def _():
        greet(token.at[1], hi)

    for copy in loads[1:]:
        copy.wait()
    for n in range(2):
        incoming(n, odd, other).wait_recv()
    for copy in upper + lower:
        arrived(copy, beside)
    rows_do("start", 0)

    @pl.when(has_above)
    def _():
        halo_face(0).start()

    def wide(tile):
        return jnp.concatenate([tile] * (cols // LANES), axis=1)

    whole = pl.ds(0, rows)

    def pack(stage, ref, base, row):
        here = pl.ds(row, TILE)
        mid = pl.ds(row + TILE, TILE)
        last = zeros(TILE, LANES)
        first = zeros(TILE, LANES)
        for r in range(CHIP):
            fp = FP[base + r, here, cols - LANES : cols]
            for v in range(variables):
                n = r * variables + v
                a = ref[base + r, v, mid, 0:LANES]
                w = fp * ref[base + r, v, mid, cols - LANES : cols]
                first = jnp.where(lane1 == n, pltpu.roll(a, n, 1) if n else a, first)
                last = jnp.where(lane1 == n, pltpu.roll(w, n + 1, 1), last)
        PW[stage, here, :] = last
        PF[stage, here, :] = first

    @pl.loop(0, nb)
    def _(b):
        pack(0, AT, 0, pl.multiple_of(b * TILE, TILE))

    col_do("start", 0, whole, nb)

    arrived(dv_copy)
    for position in range(instances):
        if position < CHIP:
            kind = jnp.where(odd == position // per_dev, 0, 3)
        else:
            kind = jnp.where(odd == (position - CHIP) // per_dev, 1, 2)
        vector = DV[kind, 0:1, :]
        for n in range(variables * variables):
            lane = (position % per_dev) * variables * variables + n
            DT[position * variables * variables + n] = jnp.broadcast_to(
                vector[:, lane : lane + 1], (TILE, LANES)
            )

    for copy in upper:
        arrived(copy, linked)

    @pl.when(has_above)
    def _():
        halo_face(1).start()

    f1, f2, f3 = (spectral_entry(d, instances) for d in (1, 2, 3))

    def spectral(a, row):
        here = pl.ds(row, TILE)
        scaled = freq[0] * VOL[here, :]
        v1 = (0.5 * (f1 - f3)) * scaled
        v2 = f2 * scaled
        v3 = (0.5 * (f1 + f3)) * scaled
        results = []
        for u in range(variables):
            near = [a(r, u) for r in range(4)]
            far = [a(r, u) for r in range(4, 8)]
            b = [m if f is None else m - f for m, f in zip(near, far)]
            c = [m if f is None else m + f for m, f in zip(near, far)]
            even = v1 * (c[1] - c[3])
            odds = v1 * (c[2] - c[0])
            q = [even, odds, -even, -odds]
            p = [
                v2 * b[2] + v3 * (b[1] + b[3]),
                v2 * b[3] + v3 * (b[2] - b[0]),
                v3 * (b[3] - b[1]) - v2 * b[0],
                -(v2 * b[1] + v3 * (b[0] + b[2])),
            ]
            results.append((q, p))
        return results

    def coupling(acc, span, ref, row, stage):
        here = pl.ds(row, TILE)
        mid = pl.ds(row + TILE, TILE)
        low = pl.ds(row, TILE)
        high = pl.ds(row + 2 * TILE, TILE)
        top = sub8 == TILE - 1
        bottom = sub8 == 0
        fm = {r: FS[r, mid, :] for r in span}
        fl = {r: jnp.where(top, FS[r, low, :], fm[r]) for r in span}
        fp = {r: FP[r, here, :] for r in span}
        cl = CL[stage, here, :]
        cr = CR[stage, here, :]
        for v in range(variables):
            terms = {}
            for r in span:
                n = (r % CHIP) * variables + v
                a = ref[r, v, mid, :]
                x = pltpu.roll(fl[r] * jnp.where(top, ref[r, v, low, :], a), 1, 0)
                y = fm[r] * pltpu.roll(
                    jnp.where(bottom, ref[r, v, high, :], a), TILE - 1, 0
                )
                edge = wide(pltpu.roll(cl, LANES - n, 1) if n else cl)
                left = jnp.where(lane8 == 0, edge, pltpu.roll(fp[r] * a, 1, 1))
                edge = wide(pltpu.roll(cr, LANES - 1 - n, 1))
                right = fp[r] * jnp.where(
                    lane8 == cols - 1, edge, pltpu.roll(a, cols - 1, 1)
                )
                terms[r] = (x, y, left, right)
            for u in range(variables):
                k0, k1, k2, k3 = (blocks[v, n, u] for n in range(4))
                for r in span:
                    x, y, left, right = terms[r]
                    acc[r, u] = acc[r, u] - ((k0 * x + k1 * y) + (k2 * left + k3 * right))
        return acc

    def inverse(acc, r, u, here):
        n = (r * variables + u) * variables
        new = wide(DT[n]) * acc[0]
        for v in range(1, variables):
            new = new + wide(DT[n + v]) * acc[v]
        return DS[r, here, :] * new

    rows_do("receive", 0)
    col_do("receive", 0, whole, nb)

    @pl.when(has_below)
    def _():
        halo_face(0).wait_recv()

    middle = nb // 2

    def sweep(b):
        row = pl.multiple_of(b * TILE, TILE)
        here = pl.ds(row, TILE)
        mid = pl.ds(row + TILE, TILE)
        found = spectral(lambda r, u: AT[r, u, mid, :] if r < CHIP else None, row)
        for u, (q, p) in enumerate(found):
            for r in range(CHIP):
                RT[r, u, here, :] = ST[r, u, here, :] - (q[r] + p[r])
                RT[CHIP + r, u, here, :] = p[r] - q[r]
        for base in range(0, instances, GROUP):
            span = range(base, base + GROUP)
            acc = {(r, u): RT[r, u, here, :] for r in span for u in range(variables)}
            if base < CHIP:
                acc = coupling(acc, span, AT, row, 0)
            for r in span:
                line = [acc[r, v] for v in range(variables)]
                for u in range(variables):
                    Y[r, u, mid, :] = inverse(line, r, u, here)
        pack(1, Y, CHIP, row)
        col_do("start", 1, here, b)

    def export(b):
        row = pl.multiple_of(b * TILE, TILE)
        here = pl.ds(row, TILE)
        mid = pl.ds(row + TILE, TILE)
        col_do("receive", 1, here, b)
        found = spectral(lambda r, u: Y[r, u, mid, :], row)
        for u, (q, p) in enumerate(found):
            for r in range(CHIP):
                RT[CHIP + r, u, here, :] = p[r] - q[r]
        for base in range(CHIP, instances, GROUP):
            span = range(base, base + GROUP)
            acc = {(r, u): RT[r, u, here, :] for r in span for u in range(variables)}
            acc = coupling(acc, span, Y, row, 1)
            for r in span:
                for u in range(variables):
                    RT[r, u, here, :] = acc[r, u]
        r_copy(0, b, odd).start()
        r_copy(1, b, odd).start()

    def order(t):
        early = (t < middle - 2).astype(jnp.int32)
        late = (t >= nb - 2).astype(jnp.int32)
        between = (1 - early) * (1 - late)
        return (
            early * (t + middle + 1)
            + between * (t - middle + 3)
            + late * (nb - 1 - t) * (nb - 1)
        )

    @pl.loop(0, nb + 4)
    def _(n):
        @pl.when(n < nb)
        def _():
            @pl.when(n == middle)
            def _():
                for copy in lower:
                    arrived(copy, linked)

            sweep((n + middle) % nb)

        @pl.when(n == middle)
        def _():
            rows_do("start", 1)

        @pl.when(n == nb + 2)
        def _():
            rows_do("receive", 1)

            @pl.when(has_below)
            def _():
                halo_face(1).wait_recv()

        @pl.when((n >= 2) & (n < middle))
        def _():
            export(order(n - 2))

        @pl.when(n >= middle + 2)
        def _():
            export(order(n - 4))

    p_x.wait_recv()
    p_rel.start()
    p_sib_in.wait_recv()
    p_rel_in.wait_recv()

    @pl.loop(0, instances)
    def _(k):
        wanted = lax.rem(k - shift[0] + 2 * instances, instances)
        group = lax.div(wanted, per_dev)
        member = lax.rem(wanted, per_dev)

        @pl.loop(0, chunks)
        def _(chunk):
            for u in range(variables):
                value = ALLP[group, member, u, chunk]
                for q in range(TILE):
                    ROUTED[chunk * TILE + q, k, u : u + 1, :] = value[q : q + 1, :]

    def a2a(j):
        return remote(
            ROUTED.at[(me + j) % n_space], ARR.at[me], q_s.at[j], q_r.at[j],
            space=(me + j) % n_space,
        )

    @pl.loop(1, n_space)
    def _(j):
        a2a(j).start()

    ARR[me] = ROUTED[me]

    half_table(target_line, 0)

    @pl.loop(1, n_space)
    def _(j):
        remote(
            ROUTED.at[0], ARR.at[(me + n_space - j) % n_space], q_s.at[j], q_r.at[j],
            space=(me + j) % n_space,
        ).wait_recv()

    if chunks > 1:
        PT[...] = zeros(instances, variables, rows, cols)

    @pl.loop(0, chunks)
    def _(chunk):
        if chunks > 1:
            half_table(target_line, chunk)

        @pl.loop(0, instances)
        def _(r):
            k = (r + instances - mine) % instances
            for p in range(TILE):
                hit = sub_r == lax.shift_right_logical(target_line(chunk * TILE + p), shift_bits)
                parts = split_parts(ARR[chunk * TILE + p, k])
                for n, part in enumerate(parts):
                    for u in range(variables):
                        begin = (n * variables + u) * rows
                        LHS[begin : begin + rows, p * slots : (p + 1) * slots] = jnp.where(
                            hit, part[u : u + 1, :].astype(jnp.float32), 0.0
                        ).astype(jnp.bfloat16)
            terms = lax.dot_general(
                LHS[...], COL[0:cols, :], (((1,), (1,)), ((), ())),
                preferred_element_type=jnp.float32,
            )
            height = variables * rows
            summed = terms[:height]
            for part in range(1, PARTS):
                summed = summed + terms[part * height : (part + 1) * height]
            summed = summed.reshape(variables, rows, cols)
            if chunks > 1:
                summed = summed + PT[r]
            PT[r] = summed

    rows_do("sent", 1)

    @pl.loop(0, nb)
    def _(b):
        row = pl.multiple_of(b * TILE, TILE)
        here = pl.ds(row, TILE)
        mid = pl.ds(row + TILE, TILE)
        for r in range(instances):
            line = [PT[r, v, here, :] for v in range(variables)]
            for u in range(variables):
                Y[r, u, mid, :] = Y[r, u, mid, :] - inverse(line, r, u, here)
                if r < CHIP:
                    ST[r, u, here, :] = ST[r, u, here, :] - line[u]

    rows_do("start", 2)

    @pl.loop(0, nb)
    def _(b):
        pack(2, Y, 0, pl.multiple_of(b * TILE, TILE))

    col_do("start", 2, whole, nb + 1)
    rows_do("receive", 2)
    col_do("receive", 2, whole, nb + 1)

    @pl.loop(0, nb)
    def _(b):
        row = pl.multiple_of(b * TILE, TILE)
        here = pl.ds(row, TILE)
        mid = pl.ds(row + TILE, TILE)
        found = spectral(lambda r, u: Y[r, u, mid, :], row)
        for u, (q, p) in enumerate(found):
            for r in range(CHIP):
                RT[r, u, here, :] = ST[r, u, here, :] - (q[r] + p[r])
        for base in range(0, CHIP, GROUP):
            span = range(base, base + GROUP)
            acc = {(r, u): RT[r, u, here, :] for r in span for u in range(variables)}
            acc = coupling(acc, span, Y, row, 2)
            for r in span:
                for u in range(variables):
                    RT[r, u, here, :] = acc[r, u]
        r_copy(2, b, odd).start()
        r_own(b).start()

    @pl.loop(0, nb)
    def _(t):
        b = order(t)
        here = pl.ds(pl.multiple_of(b * TILE, TILE), TILE)
        r_own(b).wait()
        r_copy(2, b, 1 - odd).wait_recv()
        r_copy(0, b, odd).wait_recv()
        r_copy(1, b, 1 - odd).wait_recv()
        for k in range(per_dev):
            scale = DH[k, here, :]
            rest = [NEAR[k, v, here, :] + FAR[k, v, here, :] for v in range(variables)]
            for u in range(variables):
                out_r[k, u, here, :] = rest[u]
                new = dinv[u, k, 0] * rest[0]
                for v in range(1, variables):
                    new = new + dinv[u, k, v] * rest[v]
                out_a[k, u, here, :] = scale * new

    for copy in (dv_copy, *upper, *lower):
        sent(copy)
    for n in range(2):
        incoming(n, 1 - odd, mine).wait_send()

    p_x.wait_send()
    p_sib.wait_send()
    p_rel.wait_send()

    @pl.loop(1, n_space)
    def _(j):
        a2a(j).wait_send()

    @pl.when(has_above)
    def _():
        halo_face(0).wait_send()
        halo_face(1).wait_send()

    rows_do("sent", 0)
    rows_do("sent", 2)
    col_do("sent", 0, whole, nb)
    col_do("sent", 2, whole, nb + 1)

    @pl.loop(0, nb)
    def _(b):
        for kind in range(3):
            r_copy(kind, b, odd).wait_send()
        col_do("sent", 1, pl.ds(pl.multiple_of(b * TILE, TILE), TILE), b)


def finish(a, r, out_a, out_r, sems):
    copies = [
        pltpu.make_async_copy(a, out_a, sems.at[0]),
        pltpu.make_async_copy(r, out_r, sems.at[1]),
    ]
    for copy in copies:
        copy.start()
    for copy in copies:
        copy.wait()


def body(n_space, n_inst, a, s, fs, fp, ds, vol, blocks, dinv, *rest):
    per_dev, variables, rows, width = a.shape
    slots = rest[3].shape[2]
    nb = rows // TILE
    chunks = n_space // TILE
    instances = n_inst * per_dev
    cols = width // 2
    f32 = jnp.float32
    hbm = pl.BlockSpec(memory_space=pl.ANY)
    vmem = pl.BlockSpec(memory_space=pltpu.VMEM)
    dma = pltpu.SemaphoreType.DMA
    field = (per_dev, variables, rows, width)
    out = jax.ShapeDtypeStruct(field, f32)
    blocks = jnp.transpose(blocks, (1, 0, 2))
    dinv = jnp.transpose(dinv, (1, 0, 2))
    placed = pltpu.VMEM(field, f32)
    new, r = pl.pallas_call(
        functools.partial(kernel, n_space, n_inst),
        out_shape=(placed, placed),
        in_specs=[hbm] * 15,
        out_specs=(vmem, vmem),
        scratch_shapes=[
            pltpu.SMEM(blocks.shape, f32),
            pltpu.SMEM(dinv.shape, f32),
            pltpu.SMEM(rest[0].shape, f32),
            pltpu.SMEM(rest[1].shape, f32),
            pltpu.SMEM(rest[2].shape, jnp.int32),
            pltpu.VMEM(rest[3].shape, jnp.int32),
            pltpu.VMEM(rest[4].shape, jnp.int32),
            pltpu.VMEM(rest[5].shape, f32),
            pltpu.SMEM(rest[6].shape, jnp.int32),
            pltpu.VMEM(field, f32),
            pltpu.VMEM((CHIP, variables, rows + 2 * TILE, cols), f32),
            pltpu.VMEM((CHIP, variables, rows, cols), f32),
            pltpu.VMEM((instances, variables, rows + 2 * TILE, cols), f32),
            pltpu.VMEM((instances, variables, rows, cols), f32),
            pltpu.VMEM((instances, variables, rows, cols), f32),
            pltpu.VMEM(field, f32),
            pltpu.VMEM(field, f32),
            pltpu.VMEM((instances, rows + TILE, cols), f32),
            pltpu.VMEM((instances, rows, cols), f32),
            pltpu.VMEM((instances, rows, cols), f32),
            pltpu.VMEM((rows, cols), f32),
            pltpu.VMEM((per_dev, rows, width), f32),
            pltpu.VMEM((3, rows, LANES), f32),
            pltpu.VMEM((3, rows, LANES), f32),
            pltpu.VMEM((3, rows, LANES), f32),
            pltpu.VMEM((3, rows, LANES), f32),
            pltpu.VMEM((n_inst, TILE, LANES), f32),
            pltpu.VMEM((instances * variables * variables, TILE, LANES), f32),
            pltpu.VMEM((width, TILE * slots), jnp.bfloat16),
            pltpu.VMEM((per_dev, variables, chunks, TILE, slots), f32),
            pltpu.VMEM((4, per_dev, variables, chunks, TILE, slots), f32),
            pltpu.VMEM((n_space, instances, variables, slots), f32),
            pltpu.VMEM((n_space, instances, variables, slots), f32),
            pltpu.VMEM((PARTS * variables * rows, TILE * slots), jnp.bfloat16),
            dma((17,)),
            dma((nb,)),
            dma((2,)),
            dma((2,)),
            dma((3, 7)),
            dma((3, 7)),
            dma((3, nb)),
            dma((3, nb)),
            dma((nb + 2,)),
            dma((nb + 2,)),
            dma((8,)),
            dma((8,)),
            dma((3,)),
            dma((3,)),
            dma((n_space,)),
            dma((n_space,)),
            pltpu.SemaphoreType.REGULAR((4,)),
        ],
        compiler_params=pltpu.CompilerParams(
            collective_id=0, has_side_effects=True, vmem_limit_bytes=56 * 1024 * 1024
        ),
    )(a, s, fs, fp, ds, vol, blocks, dinv, *rest)
    return pl.pallas_call(
        finish,
        out_shape=(out, out),
        in_specs=[vmem, vmem],
        out_specs=(hbm, hbm),
        scratch_shapes=[dma((2,))],
    )(*(pltpu.with_memory_space_constraint(x, pltpu.VMEM) for x in (new, r)))


def solution(mesh):
    in_specs = (
        P("inst", None, "space", None),
        P("inst", None, "space", None),
        P("inst", "space", None),
        P("inst", "space", None),
        P("inst", "space", None),
        P("space", None),
        P(),
        P("inst", None, None),
        P(),
        P(),
        P(),
        P("space", None, None),
        P(None, "space", None),
        P("space", None, None),
        P("space", None),
    )
    out_specs = (P("inst", None, "space", None), P("inst", None, "space", None))
    return jax.shard_map(
        functools.partial(body, mesh.shape["space"], mesh.shape["inst"]),
        mesh=mesh,
        in_specs=in_specs,
        out_specs=out_specs,
        check_vma=False,
    )
```
